32 devices in a mesh: heads: 8 (over y, x, core), batch: 4 (over z).
Axes of the slice: x: 2, y: 2, z: 4, core: 2. Of those that a mesh axis runs over, the one named last changes fastest.
Arguments:
- tokens: bfloat16 [2, 4, 1024, 2048], P(None, 'batch', 'heads'), may hold values from -6 to 6
- cotangent: bfloat16 [2, 4, 1024, 2048], P(None, 'batch', 'heads'), may hold values from -6 to 6
- doc_lengths: int32 [2, 4, 4], P(None, 'batch'), may hold values from 1 to 768, 1024 in all within a row
- pad_mask: int32 [2, 4, 1024], P(None, 'batch'), may hold values 0 or 1
- w_query: bfloat16 [2048, 1024], P(None, 'heads'), may hold values from -0.1875 to 0.1875
- w_key: bfloat16 [2048, 1024], P(None, 'heads'), may hold values from -0.1875 to 0.1875
- w_value: bfloat16 [2048, 1024], P(None, 'heads'), may hold values from -0.125 to 0.125
- w_out: bfloat16 [1024, 2048], P('heads'), may hold values from -0.75 to 0.75
- w_gate: bfloat16 [2048, 8192], P(None, 'heads'), may hold values from -0.125 to 0.125
- w_up: bfloat16 [2048, 8192], P(None, 'heads'), may hold values from -0.125 to 0.125
- w_down: bfloat16 [8192, 2048], P('heads'), may hold values from -0.0625 to 0.0625
- norm_attn: float32 [2048], replicated, may hold values from 0.1 to 1.9
- norm_mlp: float32 [2048], replicated, may hold values from 0.1 to 1.9
- mix_gate: float32 [8], P('heads'), may hold values from -2 to 2
Outputs:
- layer_out: bfloat16 [2, 4, 1024, 2048], P(None, 'batch', 'heads')
- grad_tokens: float32 [2, 4, 1024, 2048], P(None, 'batch', 'heads')
- grad_w_query: float32 [2048, 1024], P(None, 'heads')
- grad_w_key: float32 [2048, 1024], P(None, 'heads')
- grad_w_value: float32 [2048, 1024], P(None, 'heads')
- grad_w_out: float32 [1024, 2048], P('heads')
- grad_w_gate: float32 [2048, 8192], P(None, 'heads')
- grad_w_up: float32 [2048, 8192], P(None, 'heads')
- grad_w_down: float32 [8192, 2048], P('heads')
- grad_norm_attn: float32 [2048], replicated
- grad_norm_mlp: float32 [2048], replicated
- grad_mix_gate: float32 [8], P('heads')
The draws below stay inside these ranges and needn't reach their ends.
Inputs may be any that keep to these rules, and one draw needn't show every extreme that they name: `doc_lengths`: the 4 lengths of a sequence sum to 1024; the longest is 768.
All inputs are finite; a program needn't handle non-finite values. No bound on the sum of `pad_mask` on one device may be relied on, other than what follows from the above.
Results may differ from the reference program's by a relative error of at most 0.018.
Values may be sent and summed in bfloat16 or wider, within the bound.
No kernel may reach another device: no remote copies, remote signals or barrier semaphores. Data moves between devices by JAX's collectives and lax.ppermute only.
A program may use at most 256 MiB of HBM per device.

```python
import math
import jax
import jax.numpy as jnp
import numpy as np
from jax import lax

D = 2048
DH = 128
FF = 8192
H = 8
SEG = 512
LEN = 1024
MICRO = 2
NDOC = 4
SEQS = 4


def place_ends(drawn, key, smallest, high):
    place = [jax.random.randint(jax.random.fold_in(key, axis), (), 0, length) for axis, length in enumerate(drawn.shape)]
    longest = drawn.shape.index(max(drawn.shape))
    neighbour = place[:longest] + [(place[longest] + 1) % drawn.shape[longest]] + place[longest + 1:]
    return drawn.at[tuple(place)].set(smallest).at[tuple(neighbour)].set(high)


def levels(rng, dims, cuts, least, high):
    loudness = 1.0
    for position, shards_of in cuts:
        steps = jax.random.uniform(jax.random.fold_in(jax.random.fold_in(rng, 6), position), (shards_of,), jnp.float32, least / len(cuts), high / len(cuts))
        loudness = loudness * jnp.repeat(jnp.exp(steps), dims[position] // shards_of).reshape((-1,) + (1,) * (len(dims) - 1 - position))
    return loudness


def length_profile(number_of, total, limit, lean):
    portions = [(1 << 20) // math.isqrt(standing ** lean) + 1 for standing in range(2, number_of + 1)]
    spare, counts = total - limit - (number_of - 1), [1] * (number_of - 1)
    while spare > 0:
        movable = [i for i in range(number_of - 1) if counts[i] < limit]
        mass, budget = sum([portions[i] for i in movable]), spare
        for i in movable:
            extra = min(limit - counts[i], max(1, budget * portions[i] // mass), spare)
            counts[i] = counts[i] + extra
            spare = spare - extra
    return np.array([limit] + counts)


def uneven(stream_key, count, total, most, skew):
    if count == 2:
        one = jax.random.randint(stream_key, (), max(1, total - most), min(most, total - 1) + 1)
        return jnp.stack([one, total - one])
    sizes = jnp.asarray(length_profile(count, total, most, skew), jnp.int32)
    twos = (count - 1) // 2
    giver, taker = sizes[1:1 + 2 * twos:2], sizes[2:2 + 2 * twos:2]
    slack = jnp.minimum(giver - 1, most - taker)
    passed = jax.random.randint(jax.random.fold_in(stream_key, 1), (twos,), 0, 1 << 20) % (slack + 1)
    sizes = sizes.at[1:1 + 2 * twos:2].set(giver - passed).at[2:2 + 2 * twos:2].set(taker + passed)
    return sizes[jax.random.permutation(jax.random.fold_in(stream_key, 2), count)]


def gaussian(stream_key, extent, deviation, reach, cuts=(), kind=jnp.bfloat16):
    level = levels(stream_key, extent, cuts, -0.22, 0.18) if cuts else 1.0
    result = jax.random.normal(stream_key, extent, jnp.float32) * deviation * level
    return jnp.minimum(jnp.maximum(result, -reach), reach).astype(kind)


def setup_inputs(seed: int = 0) -> dict:
    splits = jax.random.split(jax.random.key(seed), 15)
    return {
        "tokens": gaussian(splits[0], (MICRO, SEQS, LEN, D), 1.0, 6.0, ((1, 4), (2, 8))),
        "cotangent": gaussian(splits[1], (MICRO, SEQS, LEN, D), 1.0, 6.0, ((1, 4), (2, 8))),
        "doc_lengths": jax.vmap(lambda own: uneven(own, NDOC, LEN, 3 * LEN // 4, 0))(jax.random.split(splits[2], MICRO * SEQS)).reshape((MICRO, SEQS, NDOC)).astype(jnp.int32),
        "pad_mask": place_ends((jax.random.randint(splits[3], (MICRO, SEQS, LEN), 0, 8) < 7).astype(jnp.int32), jax.random.fold_in(splits[3], 1), 0, 1),
        "w_query": gaussian(splits[4], (D, H * DH), (D // 2) ** -0.5, 0.1875, ((1, 8),)),
        "w_key": gaussian(splits[5], (D, H * DH), (D // 2) ** -0.5, 0.1875, ((1, 8),)),
        "w_value": gaussian(splits[6], (D, H * DH), D ** -0.5, 0.125, ((1, 8),)),
        "w_out": gaussian(splits[7], (H * DH, D), (H * DH // 16) ** -0.5, 0.75, ((0, 8),)),
        "w_gate": gaussian(splits[8], (D, FF), D ** -0.5, 0.125, ((1, 8),)),
        "w_up": gaussian(splits[9], (D, FF), D ** -0.5, 0.125, ((1, 8),)),
        "w_down": gaussian(splits[10], (FF, D), FF ** -0.5, 0.0625, ((0, 8),)),
        "norm_attn": jnp.clip(1.0 + 0.18 * jax.random.normal(splits[11], (D,), jnp.float32), 0.1, 1.9),
        "norm_mlp": jnp.clip(1.0 + 0.18 * jax.random.normal(splits[12], (D,), jnp.float32), 0.1, 1.9),
        "mix_gate": jnp.clip(jax.random.uniform(splits[13], (H,), jnp.float32, -2.0, 2.0) * levels(splits[13], (H,), ((0, 8),), -0.4, 0.0), -2.0, 2.0),
    }


@jax.custom_vjp
def low(v):
    return lax.optimization_barrier(v.astype(jnp.bfloat16)).astype(jnp.float32)

@jax.custom_vjp
def low_back(v):
    return v

def low_keep(v):
    return (low(v), None)

def low_pass(kept, grad):
    return (grad,)

def back_keep(v):
    return (v, None)

def back_low(kept, grad):
    return (low(grad),)
low.defvjp(low_keep, low_pass)
low_back.defvjp(back_keep, back_low)
epsilon = 1e-05
big_negative = -1e+30

def matmul(left_mat, right_mat):
    return jnp.dot(left_mat, right_mat, precision=lax.Precision.HIGHEST, preferred_element_type=jnp.float32)

def rms_gain(values_in, gain_vec):
    return values_in * lax.rsqrt(lax.optimization_barrier(jnp.mean(values_in * values_in, axis=-1, keepdims=True)) + epsilon) * gain_vec

def positive(values_in):
    return jnp.where(values_in > 0, values_in + 1.0, jnp.exp(values_in))

def sequence_masks(lengths, pad_row):
    positions = jnp.arange(LEN, dtype=jnp.int32)
    doc_ends = jnp.cumsum(lengths).astype(jnp.int32)
    doc_ids = lax.optimization_barrier(jnp.sum((positions[:, None] >= doc_ends[None, :]).astype(jnp.int32), axis=1))
    segment_ids = positions // SEG
    same_doc = doc_ids[:, None] == doc_ids[None, :]
    valid_keys = pad_row[None, :] == 1
    diagonal = positions[:, None] == positions[None, :]
    local_mask = same_doc & (segment_ids[:, None] == segment_ids[None, :]) & (positions[None, :] <= positions[:, None]) & (valid_keys | diagonal)
    memory_mask = same_doc & (segment_ids[None, :] < segment_ids[:, None]) & valid_keys
    return (local_mask, memory_mask)

def head_mix(query_all, key_all, value_all, gate_logit, local_mask, memory_mask):
    scores = low_back(matmul(query_all, key_all.T) * DH ** (-0.5))
    soft_probs = low(jax.nn.softmax(jnp.where(local_mask, scores, big_negative), axis=-1))
    dotted = low_back(matmul(soft_probs, value_all))
    pos_query = low(positive(query_all))
    pos_key = low(positive(key_all))
    weights = low_back(jnp.where(memory_mask, matmul(pos_query, pos_key.T), 0.0))
    numerator = low_back(matmul(low(weights), value_all))
    denominator = jnp.maximum(lax.optimization_barrier(jnp.sum(weights, axis=-1, keepdims=True)), 1.0)
    share = jax.nn.sigmoid(gate_logit)
    return share * (numerator / denominator) + (1.0 - share) * dotted

def split_heads(values_in):
    return values_in.reshape(LEN, H, DH).transpose(1, 0, 2)

def block_forward(x_seq, w_query, w_key, w_value, w_out, w_gate, w_up, w_down, norm_attn, norm_mlp, mix_gate, local_mask, memory_mask):
    normed = low(rms_gain(x_seq, norm_attn))
    query_all = low_back(low(matmul(normed, w_query)))
    key_all = low_back(low(matmul(normed, w_key)))
    value_all = low_back(low(matmul(normed, w_value)))

    def one_head(head_args):
        return head_mix(head_args[0], head_args[1], head_args[2], head_args[3], local_mask, memory_mask)
    mixed = lax.map(jax.checkpoint(one_head), (split_heads(query_all), split_heads(key_all), split_heads(value_all), mix_gate))
    mixed = mixed.transpose(1, 0, 2).reshape(LEN, H * DH)
    mid_rows = x_seq + low_back(matmul(low(mixed), w_out))
    normed_mlp = low(rms_gain(mid_rows, norm_mlp))
    gate_pre = low_back(matmul(normed_mlp, w_gate))
    up_pre = low_back(matmul(normed_mlp, w_up))
    hidden = low(jax.nn.silu(gate_pre) * up_pre)
    return mid_rows + low_back(matmul(hidden, w_down))

def reference(tokens, cotangent, doc_lengths, pad_mask, w_query, w_key, w_value, w_out, w_gate, w_up, w_down, norm_attn, norm_mlp, mix_gate):
    weights_in = tuple((array_in.astype(jnp.float32) for array_in in (w_query, w_key, w_value, w_out, w_gate, w_up, w_down, norm_attn, norm_mlp, mix_gate)))
    count_seqs = MICRO * SEQS
    flat_tokens = tokens.reshape(count_seqs, LEN, D).astype(jnp.float32)
    flat_cot = cotangent.reshape(count_seqs, LEN, D).astype(jnp.float32)
    flat_len = doc_lengths.reshape(count_seqs, NDOC).astype(jnp.int32)
    flat_pad = pad_mask.reshape(count_seqs, LEN).astype(jnp.int32)

    def one_seq(running, seq_item):
        x_seq, cot_seq, lengths, pad_row = seq_item
        local_mask, memory_mask = sequence_masks(lengths, pad_row)

        def forward_fn(x_in, *weight_list):
            return block_forward(x_in, *weight_list, local_mask, memory_mask)
        out_seq, pull_back = jax.vjp(forward_fn, x_seq, *weights_in)
        grad_list = pull_back(cot_seq)
        running = tuple((acc_grad + new_grad for acc_grad, new_grad in zip(running, grad_list[1:])))
        return (running, (out_seq.astype(jnp.bfloat16), grad_list[0]))
    zero_grads = tuple((jnp.zeros_like(array_in) for array_in in weights_in))
    sums, (outs_all, grads_all) = lax.scan(one_seq, zero_grads, (flat_tokens, flat_cot, flat_len, flat_pad))
    return (outs_all.reshape(MICRO, SEQS, LEN, D), grads_all.reshape(MICRO, SEQS, LEN, D), sums[0], sums[1], sums[2], sums[3], sums[4], sums[5], sums[6], sums[7], sums[8], sums[9])
```

```python
import jax
import jax.numpy as jnp
from jax import lax
from jax.sharding import PartitionSpec as P

DH = 128
SEG = 512
SEGS = 2
LEN = 1024
MICRO = 2


epsilon = 1e-05
big_negative = -1e30


def dot_rows(left_mat, right_mat):
    return lax.dot_general(
        left_mat, right_mat, (((1,), (1,)), ((), ())), preferred_element_type=jnp.float32
    )


def dot_cols(left_mat, right_mat):
    return lax.dot_general(
        left_mat, right_mat, (((0,), (0,)), ((), ())), preferred_element_type=jnp.float32
    )


def batch_mm(left, right):
    return lax.dot_general(
        left, right, (((2,), (1,)), ((0,), (0,))), preferred_element_type=jnp.float32
    )


def batch_mt(left, right):
    return lax.dot_general(
        left, right, (((2,), (2,)), ((0,), (0,))), preferred_element_type=jnp.float32
    )


def batch_tm(left, right):
    return lax.dot_general(
        left, right, (((1,), (1,)), ((0,), (0,))), preferred_element_type=jnp.float32
    )


def norm_scale(row_block):
    return lax.rsqrt(jnp.mean(row_block * row_block, axis=-1, keepdims=True) + epsilon)


def norm_back(row_block, row_scale, gain_vec, upstream):
    shaped = upstream * gain_vec
    inner = jnp.mean(shaped * row_block, axis=-1, keepdims=True)
    d_rows = row_scale * shaped - row_block * row_scale * row_scale * row_scale * inner
    d_gain = jnp.sum(upstream * row_block * row_scale, axis=0)
    return (d_rows, d_gain)


def positive(values_in):
    return jnp.where(values_in > 0, values_in + 1.0, jnp.exp(values_in))


def local_mask(begin_row, positions, doc_ids, valid_keys):
    seg_pos = positions[begin_row : begin_row + SEG]
    seg_doc = doc_ids[:, begin_row : begin_row + SEG]
    seg_valid = valid_keys[:, begin_row : begin_row + SEG]
    same_doc = seg_doc[:, :, None] == seg_doc[:, None, :]
    causal = (seg_pos[None, :] <= seg_pos[:, None])[None]
    diagonal = (seg_pos[None, :] == seg_pos[:, None])[None]
    return same_doc & causal & (seg_valid[:, None, :] | diagonal)


def memory_mask(begin_row, doc_ids, valid_keys):
    seg_doc = doc_ids[:, begin_row : begin_row + SEG]
    return (seg_doc[:, :, None] == doc_ids[:, None, :begin_row]) & valid_keys[:, None, :begin_row]


def head_forward(query_all, key_all, value_all, share, positions, doc_ids, valid_keys):
    score_scale = DH ** (-0.5)
    pos_query = positive(query_all.astype(jnp.float32)).astype(jnp.bfloat16)
    pos_key = positive(key_all.astype(jnp.float32)).astype(jnp.bfloat16)
    kept = []
    dotted_parts, recalled_parts = ([], [])
    for segment in range(SEGS):
        rows = slice(segment * SEG, (segment + 1) * SEG)
        before = slice(0, segment * SEG)
        allowed = local_mask(segment * SEG, positions, doc_ids, valid_keys)
        scores = jnp.where(
            allowed, batch_mt(query_all[:, rows], key_all[:, rows]) * score_scale, big_negative
        )
        shifted = jnp.exp(scores - jnp.max(scores, axis=2, keepdims=True))
        soft_probs = shifted / jnp.sum(shifted, axis=2, keepdims=True)
        dotted_parts.append(batch_mm(soft_probs.astype(jnp.bfloat16), value_all[:, rows]))
        if segment == 0:
            recalled_parts.append(jnp.zeros((query_all.shape[0], SEG, DH), jnp.float32))
            kept.append((soft_probs,))
        else:
            mem_allowed = memory_mask(segment * SEG, doc_ids, valid_keys)
            weights = jnp.where(mem_allowed, batch_mt(pos_query[:, rows], pos_key[:, before]), 0.0)
            row_total = jnp.sum(weights, axis=2, keepdims=True)
            denominator = jnp.maximum(row_total, 1.0)
            weights_low = weights.astype(jnp.bfloat16)
            numerator = batch_mm(weights_low, value_all[:, before])
            recalled_parts.append(numerator / denominator)
            kept.append((soft_probs, mem_allowed, row_total, weights_low, numerator))
    dotted = jnp.concatenate(dotted_parts, axis=1)
    recalled = jnp.concatenate(recalled_parts, axis=1)
    mixed_head = share * recalled + (1.0 - share) * dotted
    return (mixed_head, dotted, recalled, pos_query, pos_key, kept)


def head_backward(query_all, key_all, value_all, share, d_mixed, forward_kept):
    _, dotted, recalled, pos_query, pos_key, kept = forward_kept
    score_scale = DH ** (-0.5)
    query_float = query_all.astype(jnp.float32)
    key_float = key_all.astype(jnp.float32)
    d_share = jnp.sum(d_mixed * (recalled - dotted)) * share * (1.0 - share)
    d_dotted = ((1.0 - share) * d_mixed).astype(jnp.bfloat16)
    d_recalled = share * d_mixed
    nothing = jnp.zeros((query_all.shape[0], SEG, DH), jnp.float32)
    d_query, d_key, d_value, d_posq, d_posk = [
        [nothing for _ in range(SEGS)] for _ in range(5)
    ]
    for segment in range(SEGS):
        rows = slice(segment * SEG, (segment + 1) * SEG)
        before = slice(0, segment * SEG)
        soft_probs = kept[segment][0]
        d_dot_seg = d_dotted[:, rows]
        d_value[segment] += batch_tm(soft_probs.astype(jnp.bfloat16), d_dot_seg)
        d_probs = batch_mt(d_dot_seg, value_all[:, rows])
        d_scores = (
            soft_probs * (d_probs - jnp.sum(soft_probs * d_probs, axis=2, keepdims=True))
        ).astype(jnp.bfloat16)
        d_query[segment] += batch_mm(d_scores, key_all[:, rows]) * score_scale
        d_key[segment] += batch_tm(d_scores, query_all[:, rows]) * score_scale
        if segment > 0:
            _, mem_allowed, row_total, weights_low, numerator = kept[segment]
            denominator = jnp.maximum(row_total, 1.0)
            d_recall_seg = d_recalled[:, rows]
            d_numer = (d_recall_seg / denominator).astype(jnp.bfloat16)
            d_denom = jnp.where(
                row_total > 1.0,
                -jnp.sum(d_recall_seg * numerator, axis=2, keepdims=True)
                / (denominator * denominator),
                0.0,
            )
            d_weights = jnp.where(
                mem_allowed, batch_mt(d_numer, value_all[:, before]) + d_denom, 0.0
            ).astype(jnp.bfloat16)
            d_posq[segment] += batch_mm(d_weights, pos_key[:, before])
            d_posk_all = batch_tm(d_weights, pos_query[:, rows])
            d_value_all = batch_tm(weights_low, d_numer)
            for earlier in range(segment):
                part = slice(earlier * SEG, (earlier + 1) * SEG)
                d_posk[earlier] += d_posk_all[:, part]
                d_value[earlier] += d_value_all[:, part]
    d_query, d_key, d_value, d_posq, d_posk = [
        jnp.concatenate(parts, axis=1) for parts in (d_query, d_key, d_value, d_posq, d_posk)
    ]
    d_query = d_query + d_posq * jnp.where(query_float > 0, 1.0, jnp.exp(query_float))
    d_key = d_key + d_posk * jnp.where(key_float > 0, 1.0, jnp.exp(key_float))
    return (
        d_query.astype(jnp.bfloat16),
        d_key.astype(jnp.bfloat16),
        d_value.astype(jnp.bfloat16),
        d_share,
    )


class Chain:
    def __init__(self, axis, size, depth):
        self.axis, self.size, self.depth = axis, size, depth
        self.place = lax.axis_index(axis)
        half = size // 2
        self.stages = [("in", [(s - 1, s), (size - s, size - 1 - s)]) for s in range(1, half)]
        self.stages.append(("in", [(half - 1, half), (half, half - 1)]))
        self.stages += [("out", [(s, s - 1), (size - 1 - s, size - s)]) for s in range(half - 1, 0, -1)]
        self.entered = []
        self.last = [None] * len(self.stages)

    def add(self, array):
        if self.size == 1:
            return array
        if self.size % 2:
            return lax.psum(array, self.axis)
        if len(self.entered) >= self.depth:
            array, _ = lax.optimization_barrier((array, self.entered[-self.depth]))
        for number, (kind, pairs) in enumerate(self.stages):
            arrived = lax.ppermute(array, self.axis, pairs)
            if self.last[number] is not None:
                array, arrived, _ = lax.optimization_barrier((array, arrived, self.last[number]))
            if kind == "in":
                array = array + arrived
            else:
                receives = jnp.zeros((), jnp.bool_)
                for _, target in pairs:
                    receives = receives | (self.place == target)
                array = jnp.where(receives, arrived, array)
            self.last[number] = array
            if number == 0:
                self.entered.append(array)
        return array


def per_device(
    tokens,
    cotangent,
    doc_lengths,
    pad_mask,
    w_query,
    w_key,
    w_value,
    w_out,
    w_gate,
    w_up,
    w_down,
    norm_attn,
    norm_mlp,
    mix_gate,
    *,
    n_heads,
    n_batch,
):
    width = tokens.shape[-1]
    rows = tokens.shape[2]
    own_rows = MICRO * rows
    all_rows = n_heads * own_rows
    hidden_cols = w_gate.shape[1]
    here = lax.axis_index("heads")
    low = jnp.bfloat16

    def by_sequence(array):
        cols = array.shape[-1]
        return array.reshape(n_heads, MICRO, rows, cols).transpose(1, 0, 2, 3).reshape(MICRO, LEN, cols)

    def by_device(array):
        cols = array.shape[-1]
        return (
            array.reshape(MICRO, n_heads, rows, cols).transpose(1, 0, 2, 3).reshape(all_rows, cols)
        )

    def gather(array):
        return lax.all_gather(array, "heads", axis=0, tiled=True)

    def scatter(array):
        return lax.psum_scatter(array, "heads", scatter_dimension=0, tiled=True)

    def own(array):
        return lax.dynamic_slice_in_dim(array, here * own_rows, own_rows, 0)

    w_qkv = jnp.concatenate([w_query, w_key, w_value], axis=1)
    w_gate_up = jnp.concatenate([w_gate, w_up], axis=1)
    share = jax.nn.sigmoid(mix_gate)[0]
    positions = jnp.arange(LEN, dtype=jnp.int32)
    doc_ends = jnp.cumsum(doc_lengths[:, 0], axis=1)
    doc_ids = jnp.sum((positions[None, :, None] >= doc_ends[:, None, :]).astype(jnp.int32), axis=2)
    valid_keys = pad_mask[:, 0] == 1

    tok_own = tokens.reshape(own_rows, width)
    cot_own = cotangent.reshape(own_rows, width)
    tok_all = gather(tok_own)
    w_out_all = gather(w_out)
    x_all = tok_all.astype(jnp.float32)
    h1_all = (x_all * norm_scale(x_all) * norm_attn).astype(low)
    qkv = jnp.dot(h1_all, w_qkv, preferred_element_type=jnp.float32).astype(low)
    query, key, value = [by_sequence(qkv[:, i * DH : (i + 1) * DH]) for i in range(3)]
    head_kept = head_forward(query, key, value, share, positions, doc_ids, valid_keys)
    mixed = by_device(head_kept[0].astype(low))
    mixed_all = lax.all_gather(mixed, "heads", axis=1, tiled=True)
    cot_all = gather(cot_own)

    y1_all = x_all + jnp.dot(mixed_all, w_out_all, preferred_element_type=jnp.float32)
    h2_all = (y1_all * norm_scale(y1_all) * norm_mlp).astype(low)
    x_own = tok_own.astype(jnp.float32)
    y1_own = own(y1_all)
    gate_up = jnp.dot(h2_all, w_gate_up, preferred_element_type=jnp.float32)
    gate_pre = gate_up[:, :hidden_cols]
    up_pre = gate_up[:, hidden_cols:]
    sig_gate = jax.nn.sigmoid(gate_pre)
    hidden = (gate_pre * sig_gate * up_pre).astype(low)
    d_hidden = dot_rows(cot_all, w_down)
    d_up = d_hidden * gate_pre * sig_gate
    d_gate = d_hidden * up_pre * sig_gate * (1.0 + gate_pre * (1.0 - sig_gate))
    d_gate_up = jnp.concatenate([d_gate, d_up], axis=1).astype(low)

    chain = Chain("batch", n_batch, 3)
    d_h2 = scatter(dot_rows(d_gate_up, w_gate_up).astype(low)).astype(jnp.float32)
    down_parts, gate_up_parts = ([], [])
    step = hidden_cols // 4
    for begin in range(0, hidden_cols, step):
        down_parts.append(chain.add(dot_cols(hidden[:, begin : begin + step], cot_all).astype(low)))
    step = width // 8
    for begin in range(0, width, step):
        gate_up_parts.append(
            chain.add(dot_cols(h2_all[:, begin : begin + step], d_gate_up).astype(low))
        )
    mlp_own = scatter(jnp.dot(hidden, w_down, preferred_element_type=jnp.float32).astype(low))
    layer_out = (y1_own + mlp_own.astype(jnp.float32)).astype(low)

    scale_mlp = norm_scale(y1_own)
    d_y1, gain_mlp_part = norm_back(y1_own, scale_mlp, norm_mlp, d_h2)
    d_y1 = d_y1 + cot_own.astype(jnp.float32)
    d_attn = d_y1.astype(low)
    d_mixed_own = dot_rows(d_attn, w_out_all).astype(low)
    d_mixed = lax.all_to_all(d_mixed_own, "heads", split_axis=1, concat_axis=0, tiled=True)
    grad_out = scatter(dot_cols(own(mixed_all), d_attn).astype(low))

    d_query, d_key, d_value, d_share = head_backward(
        query, key, value, share, by_sequence(d_mixed).astype(jnp.float32), head_kept
    )
    d_qkv = jnp.concatenate([by_device(d_query), by_device(d_key), by_device(d_value)], axis=1)
    d_h1 = scatter(dot_rows(d_qkv, w_qkv).astype(low)).astype(jnp.float32)
    grad_out = chain.add(grad_out)
    grad_qkv = chain.add(dot_cols(h1_all, d_qkv).astype(low))

    d_x, gain_attn_part = norm_back(x_own, norm_scale(x_own), norm_attn, d_h1)
    grad_tokens = (d_x + d_y1).reshape(tokens.shape)
    slots = jnp.where(jnp.arange(n_heads) == here, d_share, 0.0)
    sums = lax.psum(jnp.concatenate([gain_attn_part, gain_mlp_part, slots]), ("heads", "batch"))
    grad_mix = lax.dynamic_slice_in_dim(sums, 2 * width + here, 1, 0)

    wide = jnp.float32
    grad_qkv = grad_qkv.astype(wide)
    grad_gate_up = jnp.concatenate([p.astype(wide) for p in gate_up_parts], axis=0)
    grad_down = jnp.concatenate([p.astype(wide) for p in down_parts], axis=0)
    return (
        layer_out.reshape(tokens.shape),
        grad_tokens,
        grad_qkv[:, :DH],
        grad_qkv[:, DH : 2 * DH],
        grad_qkv[:, 2 * DH :],
        grad_out.astype(wide),
        grad_gate_up[:, :hidden_cols],
        grad_gate_up[:, hidden_cols:],
        grad_down,
        sums[:width],
        sums[width : 2 * width],
        grad_mix,
    )


def solution(mesh):
    in_specs = (
        P(None, "batch", "heads", None),
        P(None, "batch", "heads", None),
        P(None, "batch", None),
        P(None, "batch", None),
        P(None, "heads"),
        P(None, "heads"),
        P(None, "heads"),
        P("heads", None),
        P(None, "heads"),
        P(None, "heads"),
        P("heads", None),
        P(),
        P(),
        P("heads"),
    )
    out_specs = (
        P(None, "batch", "heads", None),
        P(None, "batch", "heads", None),
        P(None, "heads"),
        P(None, "heads"),
        P(None, "heads"),
        P("heads", None),
        P(None, "heads"),
        P(None, "heads"),
        P("heads", None),
        P(),
        P(),
        P("heads"),
    )

    def program(*arrays):
        return per_device(*arrays, n_heads=mesh.shape["heads"], n_batch=mesh.shape["batch"])

    return jax.shard_map(
        program, mesh=mesh, in_specs=in_specs, out_specs=out_specs, check_vma=False
    )
```

```python
import functools

import jax
import jax.numpy as jnp
from jax import lax
from jax.experimental import pallas as pl
from jax.experimental.pallas import tpu as pltpu
from jax.sharding import PartitionSpec as P

DH = 128
SEG = 512
SEGS = 2
LEN = 1024
MICRO = 2
FFN_CHUNKS = 4
WAITS = (225, 57, 57, 1)
ROW_BLOCK = 512
MIB = 1 << 20
VMEM_ALONE = 60
IN_VMEM = pl.BlockSpec(memory_space=pltpu.VMEM)
ANYWHERE = pl.BlockSpec(memory_space=pl.ANY)
SMALL = pl.CostEstimate(flops=1, bytes_accessed=1, transcendentals=0)
def busy(microseconds):
    return pl.CostEstimate(flops=int(microseconds * 10**9), bytes_accessed=1, transcendentals=0)


epsilon = 1e-05
big_negative = -1e30
low = jnp.bfloat16
wide = jnp.float32


def mm(left_mat, right_mat):
    return jnp.dot(left_mat, right_mat, preferred_element_type=wide)


def dot_rows(left_mat, right_mat):
    return lax.dot_general(
        left_mat, right_mat, (((1,), (1,)), ((), ())), preferred_element_type=wide
    )


def dot_cols(left_mat, right_mat):
    return lax.dot_general(
        left_mat, right_mat, (((0,), (0,)), ((), ())), preferred_element_type=wide
    )


def norm_scale(row_block):
    return lax.rsqrt(jnp.mean(row_block * row_block, axis=-1, keepdims=True) + epsilon)


def norm_back(row_block, row_scale, gain_vec, upstream):
    shaped = upstream * gain_vec
    inner = jnp.mean(shaped * row_block, axis=-1, keepdims=True)
    d_rows = row_scale * shaped - row_block * row_scale * row_scale * row_scale * inner
    d_gain = jnp.sum(upstream * row_block * row_scale, axis=0)
    return (d_rows, d_gain)


def positive(values_in):
    return jnp.where(values_in > 0, values_in + 1.0, jnp.exp(values_in))


def positive_slope(values_in):
    return jnp.where(values_in > 0, 1.0, jnp.exp(values_in))


def params(mebibytes):
    return pltpu.CompilerParams(vmem_limit_bytes=mebibytes * MIB)


def kept_block(shape):
    return pl.BlockSpec(shape, lambda *_: (0,) * len(shape), pipeline_mode=pl.Buffered(1))


def qkv_kernel(x_ref, gain_ref, w_ref, h1_ref, qkv_ref):
    rows = x_ref[...].astype(wide)
    h1 = (rows * norm_scale(rows) * gain_ref[...]).astype(low)
    h1_ref[...] = h1
    qkv_ref[...] = mm(h1, w_ref[...]).astype(low)


def qkv_rows(x_all, gain, w_qkv):
    count, width = x_all.shape
    cols = w_qkv.shape[1]
    block = min(ROW_BLOCK, count)
    return pl.pallas_call(
        qkv_kernel,
        name="qkv_rows",
        grid=(count // block,),
        in_specs=[
            pl.BlockSpec((block, width), lambda i: (i, 0)),
            kept_block((1, width)),
            kept_block((width, cols)),
        ],
        out_specs=[
            pl.BlockSpec((block, width), lambda i: (i, 0)),
            pl.BlockSpec((block, cols), lambda i: (i, 0)),
        ],
        out_shape=[
            jax.ShapeDtypeStruct((count, width), low),
            jax.ShapeDtypeStruct((count, cols), low),
        ],
        compiler_params=params(VMEM_ALONE),
        cost_estimate=SMALL,
    )(x_all, gain.reshape(1, width), w_qkv)


def seg_of(array, segment):
    return array[segment * SEG : (segment + 1) * SEG]


def local_probs(query_seg, key_seg, doc_rows, doc_cols):
    row_ids = lax.broadcasted_iota(jnp.int32, (SEG, SEG), 0)
    col_ids = lax.broadcasted_iota(jnp.int32, (SEG, SEG), 1)
    allowed = ((doc_rows == doc_cols) & (col_ids <= row_ids)) | (col_ids == row_ids)
    scores = jnp.where(allowed, dot_rows(query_seg, key_seg) * DH ** (-0.5), big_negative)
    shifted = jnp.exp(scores - jnp.max(scores, axis=1, keepdims=True))
    return shifted * (1.0 / jnp.sum(shifted, axis=1, keepdims=True))


def head_kernel(share_ref, qkv_ref, doc_rows_ref, doc_cols_ref, mixed_ref):
    share = share_ref[0]
    qkv = qkv_ref[...].reshape(LEN, 3 * DH)
    query, key, value = [qkv[:, i * DH : (i + 1) * DH] for i in range(3)]
    parts = []
    for segment in range(SEGS):
        begin = segment * SEG
        query_seg = seg_of(query, segment)
        doc_rows = doc_rows_ref[begin : begin + SEG]
        probs = local_probs(
            query_seg, seg_of(key, segment), doc_rows, doc_cols_ref[:, begin : begin + SEG]
        )
        result = (1.0 - share) * mm(probs.astype(low), seg_of(value, segment))
        if segment > 0:
            allowed = doc_rows == doc_cols_ref[:, :begin]
            pos_query = positive(query_seg.astype(wide)).astype(low)
            pos_key = positive(key[:begin].astype(wide)).astype(low)
            weights = jnp.where(allowed, dot_rows(pos_query, pos_key), 0.0)
            den = jnp.maximum(jnp.sum(weights, axis=1, keepdims=True), 1.0)
            result = result + share * (mm(weights.astype(low), value[:begin]) / den)
        parts.append(result.astype(low))
    mixed_ref[...] = jnp.concatenate(parts, axis=0).reshape(mixed_ref.shape)


def micro_spec(n_heads, rows, cols):
    return pl.BlockSpec((n_heads, None, rows, cols), lambda m: (0, m, 0, 0))


def doc_specs():
    return [
        pl.BlockSpec((None, LEN, 1), lambda m: (m, 0, 0)),
        pl.BlockSpec((None, 1, LEN), lambda m: (m, 0, 0)),
    ]


def head_forward(share, qkv, doc_rows, doc_cols):
    n_heads, micro, rows, cols = qkv.shape
    pairs = micro * LEN * SEG * 2
    return pl.pallas_call(
        head_kernel,
        name="head_forward",
        grid=(micro,),
        in_specs=[pl.BlockSpec(memory_space=pltpu.SMEM), micro_spec(n_heads, rows, cols), *doc_specs()],
        out_specs=micro_spec(n_heads, rows, DH),
        out_shape=jax.ShapeDtypeStruct((n_heads, micro, rows, DH), low),
        compiler_params=params(VMEM_ALONE),
        cost_estimate=SMALL,
    )(share, qkv, doc_rows, doc_cols)


def head_back_kernel(
    share_ref, qkv_ref, d_mixed_ref, doc_rows_ref, doc_cols_ref, _, d_qkv_ref, d_share_ref
):
    share = share_ref[0]
    scale = DH ** (-0.5)
    qkv = qkv_ref[...].reshape(LEN, 3 * DH)
    query, key, value = [qkv[:, i * DH : (i + 1) * DH] for i in range(3)]
    d_mixed = d_mixed_ref[...].reshape(LEN, DH).astype(wide)
    d_query, d_key, d_value = [[None] * SEGS for _ in range(3)]
    d_share = jnp.zeros((1, 1), wide)
    for segment in range(SEGS):
        begin = segment * SEG
        query_seg, key_seg, value_seg = [seg_of(a, segment) for a in (query, key, value)]
        doc_rows = doc_rows_ref[begin : begin + SEG]
        probs = local_probs(query_seg, key_seg, doc_rows, doc_cols_ref[:, begin : begin + SEG])
        probs_low = probs.astype(low)
        d_mixed_seg = seg_of(d_mixed, segment)
        d_dotted = ((1.0 - share) * d_mixed_seg).astype(low)
        gap = -mm(probs_low, value_seg)
        d_probs = dot_rows(d_dotted, value_seg)
        d_scores = (
            probs * (d_probs - jnp.sum(probs * d_probs, axis=1, keepdims=True))
        ).astype(low)
        d_value[segment] = dot_cols(probs_low, d_dotted)
        d_query[segment] = mm(d_scores, key_seg) * scale
        d_key[segment] = dot_cols(d_scores, query_seg) * scale
        if segment > 0:
            allowed = doc_rows == doc_cols_ref[:, :begin]
            query_float = query_seg.astype(wide)
            key_float = key[:begin].astype(wide)
            pos_query = positive(query_float).astype(low)
            pos_key = positive(key_float).astype(low)
            weights = jnp.where(allowed, dot_rows(pos_query, pos_key), 0.0)
            row_total = jnp.sum(weights, axis=1, keepdims=True)
            inverse = 1.0 / jnp.maximum(row_total, 1.0)
            weights_low = weights.astype(low)
            numerator = mm(weights_low, value[:begin])
            gap = gap + numerator * inverse
            d_recalled = share * d_mixed_seg
            d_numer = (d_recalled * inverse).astype(low)
            d_denom = jnp.where(
                row_total > 1.0,
                -jnp.sum(d_recalled * numerator, axis=1, keepdims=True) * inverse * inverse,
                0.0,
            )
            d_weights = jnp.where(
                allowed, dot_rows(d_numer, value[:begin]) + d_denom, 0.0
            ).astype(low)
            d_query[segment] += mm(d_weights, pos_key) * positive_slope(query_float)
            d_pos_key = dot_cols(d_weights, pos_query) * positive_slope(key_float)
            d_value_before = dot_cols(weights_low, d_numer)
            for earlier in range(segment):
                d_key[earlier] += seg_of(d_pos_key, earlier)
                d_value[earlier] += seg_of(d_value_before, earlier)
        d_share = d_share + jnp.sum(
            jnp.sum(d_mixed_seg * gap, axis=1, keepdims=True), axis=0, keepdims=True
        )
    whole = jnp.concatenate(
        [jnp.concatenate(parts, axis=0).astype(low) for parts in (d_query, d_key, d_value)], axis=1
    )
    d_qkv_ref[...] = whole.reshape(d_qkv_ref.shape)
    d_share_ref[...] = jnp.broadcast_to(d_share * (share * (1.0 - share)), d_share_ref.shape)


def head_backward(share, qkv, d_mixed, doc_rows, doc_cols, token):
    n_heads, micro, rows, cols = qkv.shape
    pairs = micro * LEN * SEG * 2
    return pl.pallas_call(
        head_back_kernel,
        name="head_backward",
        grid=(micro,),
        in_specs=[
            pl.BlockSpec(memory_space=pltpu.SMEM),
            micro_spec(n_heads, rows, cols),
            micro_spec(n_heads, rows, DH),
            *doc_specs(),
            ANYWHERE,
        ],
        out_specs=[
            micro_spec(n_heads, rows, cols),
            pl.BlockSpec((None, 8, 128), lambda m: (m, 0, 0)),
        ],
        out_shape=[
            jax.ShapeDtypeStruct((n_heads, micro, rows, cols), low),
            jax.ShapeDtypeStruct((micro, 8, 128), wide),
        ],
        compiler_params=params(VMEM_ALONE),
        cost_estimate=SMALL,
    )(share, qkv, d_mixed, doc_rows, doc_cols, token)


def mid_kernel(heads, place_ref, x_ref, *refs):
    mixed_refs = refs[:heads]
    w_ref, gain_ref, h2_ref, y1_ref, mixed_own_ref, w_near = refs[heads:]
    step = pl.program_id(0)
    def owner(number):
        return pl.multiple_of((place_ref[1] ^ number) * DH, DH)

    @pl.when(step == 0)
    def _():
        for number in range(heads):
            w_near[number * DH : (number + 1) * DH] = w_ref[pl.ds(owner(number), DH)]

    mixed = jnp.concatenate([ref[...] for ref in mixed_refs], axis=1)
    y1 = x_ref[...].astype(wide) + mm(mixed, w_near[...])
    h2_ref[...] = (y1 * norm_scale(y1) * gain_ref[...]).astype(low)

    @pl.when(step == place_ref[0])
    def _():
        y1_ref[...] = y1
        for number in range(heads):
            mixed_own_ref[:, pl.ds(owner(number), DH)] = mixed_refs[number][...]


def mid_rows(place, x_all, mixed_pieces, w_out_all, gain):
    count, width = x_all.shape
    heads = len(mixed_pieces)
    inner = w_out_all.shape[0]
    block = count // heads
    return pl.pallas_call(
        functools.partial(mid_kernel, heads),
        name="mid_rows",
        grid_spec=pltpu.PrefetchScalarGridSpec(
            num_scalar_prefetch=1,
            grid=(heads,),
            in_specs=[
                pl.BlockSpec((block, width), lambda i, _: (i, 0)),
                *[pl.BlockSpec((block, DH), lambda i, _: (i, 0))] * heads,
                kept_block((inner, width)),
                kept_block((1, width)),
            ],
            out_specs=[
                pl.BlockSpec((block, width), lambda i, _: (i, 0)),
                pl.BlockSpec((block, width), lambda i, _: (0, 0)),
                pl.BlockSpec((block, inner), lambda i, _: (0, 0)),
            ],
            scratch_shapes=[pltpu.VMEM((inner, width), low)],
        ),
        out_shape=[
            jax.ShapeDtypeStruct((count, width), low),
            jax.ShapeDtypeStruct((block, width), wide),
            jax.ShapeDtypeStruct((block, inner), low),
        ],
        compiler_params=params(30),
        cost_estimate=SMALL,
    )(place, x_all, *mixed_pieces, w_out_all, gain.reshape(1, width))


def ffn_rows(h2_ref, cot_ref, w_gate, w_up, w_down):
    h2 = h2_ref[...]
    gate = mm(h2, w_gate)
    up = mm(h2, w_up)
    d_hidden = dot_rows(cot_ref[...], w_down)
    sig = jax.nn.sigmoid(gate)
    act = gate * sig
    hidden = (act * up).astype(low)
    d_up = (d_hidden * act).astype(low)
    d_gate = (d_hidden * up * sig * (1.0 + gate * (1.0 - sig))).astype(low)
    return hidden, d_gate, d_up


def ffn_grads(step, hidden, d_both, h2_ref, cot_ref, top_ref, bottom_ref):
    cols = hidden.shape[1]
    side = 2 * cols
    half = cols // 2
    span = pl.ds(pl.multiple_of(step * side, side), side)
    top_ref[:cols, span] = dot_cols(hidden[...], cot_ref[...]).astype(low)
    square = dot_cols(h2_ref[...], d_both[...]).astype(low)
    top_ref[cols:, span] = square[:half]
    bottom_ref[:, span] = square[half:]


def first_kernel(
    blocks, h2_ref, cot_ref, h2_col_ref, cot_col_ref, wg_ref, wu_ref, wd_ref, _, *refs
):
    hid_ref, dg_ref, du_ref, top_ref, bottom_ref, hid_all, both_all = refs
    step = pl.program_id(0)
    block, cols = hid_ref.shape

    @pl.when(step < blocks)
    def _():
        rows = pl.ds(pl.multiple_of(step * block, block), block)
        hidden, d_gate, d_up = ffn_rows(h2_ref, cot_ref, wg_ref[...], wu_ref[...], wd_ref[...])
        hid_ref[...] = hid_all[rows] = hidden
        dg_ref[...] = both_all[rows, :cols] = d_gate
        du_ref[...] = both_all[rows, cols:] = d_up

    @pl.when(step >= blocks)
    def _():
        ffn_grads(step - blocks, hid_all, both_all, h2_col_ref, cot_col_ref, top_ref, bottom_ref)


def ffn_first(number, cols, h2_all, cot_all, w_gate, w_up, w_down, token):
    count, width = h2_all.shape
    block = min(ROW_BLOCK, count // 2)
    blocks = count // block
    side = 2 * cols
    row_spec = pl.BlockSpec((block, width), lambda i: (jnp.minimum(i, blocks - 1), 0))
    side_spec = pl.BlockSpec((count, side), lambda i: (0, jnp.maximum(i - blocks, 0)))
    col_spec = pl.BlockSpec((width, cols), lambda i: (0, number), pipeline_mode=pl.Buffered(1))
    down_spec = pl.BlockSpec((cols, width), lambda i: (number, 0), pipeline_mode=pl.Buffered(1))
    out_spec = pl.BlockSpec((block, cols), lambda i: (jnp.minimum(i, blocks - 1), 0))
    piece = (3 * cols // 2, width)
    return pl.pallas_call(
        functools.partial(first_kernel, blocks),
        name="ffn_first",
        grid=(blocks + width // side,),
        in_specs=[row_spec, row_spec, side_spec, side_spec, col_spec, col_spec, down_spec, ANYWHERE],
        out_specs=[out_spec] * 3 + [kept_out(piece)] * 2,
        out_shape=[jax.ShapeDtypeStruct((count, cols), low)] * 3
        + [jax.ShapeDtypeStruct(piece, low)] * 2,
        scratch_shapes=[pltpu.VMEM((count, cols), low), pltpu.VMEM((count, side), low)],
        compiler_params=params(VMEM_ALONE),
        cost_estimate=SMALL,
    )(h2_all, cot_all, h2_all, cot_all, w_gate, w_up, w_down, token)


def rest_kernel(h2_ref, cot_ref, wg_ref, wu_ref, wd_ref, _, *refs):
    results = ffn_rows(h2_ref, cot_ref, wg_ref[...], wu_ref[...], wd_ref[...])
    for ref, result in zip(refs, results):
        ref[...] = result


def ffn_rest(h2_all, cot_all, w_gate, w_up, w_down, token):
    count, width = h2_all.shape
    block = min(ROW_BLOCK, count // 2)
    cols = w_gate.shape[1] // 2
    row_spec = pl.BlockSpec((block, width), lambda i: (i, 0))
    col_spec = pl.BlockSpec((width, cols), lambda i: (0, 1), pipeline_mode=pl.Buffered(1))
    down_spec = pl.BlockSpec((cols, width), lambda i: (1, 0), pipeline_mode=pl.Buffered(1))
    return pl.pallas_call(
        rest_kernel,
        name="ffn_rest",
        grid=(count // block,),
        in_specs=[row_spec, row_spec, col_spec, col_spec, down_spec, ANYWHERE],
        out_specs=[pl.BlockSpec((block, cols), lambda i: (i, 0))] * 3,
        out_shape=[jax.ShapeDtypeStruct((count, cols), low)] * 3,
        compiler_params=params(VMEM_ALONE),
        cost_estimate=SMALL,
    )(h2_all, cot_all, w_gate, w_up, w_down, token)


def grads_kernel(h2_ref, cot_ref, hid_ref, dg_ref, du_ref, _, top_ref, bottom_ref, both_all):
    step = pl.program_id(0)
    cols = hid_ref.shape[1]

    @pl.when(step == 0)
    def _():
        both_all[:, :cols] = dg_ref[...]
        both_all[:, cols:] = du_ref[...]

    ffn_grads(step, hid_ref, both_all, h2_ref, cot_ref, top_ref, bottom_ref)


def ffn_weights(number, cols, h2_all, cot_all, hidden, d_gate, d_up, token):
    count, width = h2_all.shape
    side = 2 * cols
    side_spec = pl.BlockSpec((count, side), lambda i: (0, i))
    col_spec = pl.BlockSpec((count, cols), lambda i: (0, number), pipeline_mode=pl.Buffered(1))
    piece = (3 * cols // 2, width)
    return pl.pallas_call(
        grads_kernel,
        name="ffn_weights",
        grid=(width // side,),
        in_specs=[side_spec, side_spec, col_spec, col_spec, col_spec, ANYWHERE],
        out_specs=[kept_out(piece)] * 2,
        out_shape=[jax.ShapeDtypeStruct(piece, low)] * 2,
        scratch_shapes=[pltpu.VMEM((count, side), low)],
        compiler_params=params(VMEM_ALONE),
        cost_estimate=SMALL,
    )(h2_all, cot_all, hidden, d_gate, d_up, token)


def is_one_of(place_ref, takers):
    found = place_ref[2] == takers[0]
    for taker in takers[1:]:
        found = found | (place_ref[2] == taker)
    return found


def chosen(takers, place_ref, array_ref, arrived_ref):
    if not takers:
        return array_ref[...].astype(wide)
    return jnp.where(is_one_of(place_ref, takers), arrived_ref[...], array_ref[...]).astype(wide)


def top_kernel(takers, place_ref, array_ref, arrived_ref, *refs):
    down_ref, gate_ref, up_ref, token_ref = refs[-4:]
    step = pl.program_id(0)
    cols = gate_ref.shape[2]

    @pl.when(step < 2)
    def _():
        down_ref[...] = chosen(takers, place_ref, array_ref, arrived_ref)

    @pl.when(step == 2)
    def _():
        spread(chosen(takers, place_ref, array_ref, arrived_ref), gate_ref, up_ref)
        token_ref[...] = jnp.zeros_like(token_ref)


def bottom_kernel(takers, place_ref, array_ref, arrived_ref, *refs):
    gate_ref, up_ref, token_ref = refs[-3:]
    spread(chosen(takers, place_ref, array_ref, arrived_ref), gate_ref, up_ref)
    token_ref[...] = jnp.zeros_like(token_ref)


def spread(value, gate_ref, up_ref):
    cols = gate_ref.shape[2]
    for number in range(gate_ref.shape[0]):
        begin = number * 2 * cols
        gate_ref[number] = value[:, begin : begin + cols]
        up_ref[number] = value[:, begin + cols : begin + 2 * cols]


def finish_ffn(is_top, number, cols, hidden_cols, token, place, takers, array, arrived, grads):
    width = array.shape[1]
    half = cols // 2
    squares = width // (2 * cols)
    in_spec = pl.BlockSpec((half, width), lambda i: (i, 0))
    square_shape = jax.ShapeDtypeStruct((squares, 2 * cols, hidden_cols), wide)
    first = 0 if is_top else 1
    square_spec = pl.BlockSpec(
        (squares, half, cols), lambda i: (0, 0 if is_top else i + first, number)
    )
    out_specs = [square_spec, square_spec, kept_out((8, 128))]
    out_shape = [square_shape, square_shape, jax.ShapeDtypeStruct((8, 128), wide)]
    names = ["gate", "up"]
    if is_top:
        out_specs.insert(
            0, pl.BlockSpec((half, width), lambda i: (2 * number + jnp.minimum(i, 1), 0))
        )
        out_shape.insert(0, jax.ShapeDtypeStruct((hidden_cols, width), wide))
        names.insert(0, "down")
    carried = [(i, grads[name]) for i, name in enumerate(names) if name in grads]
    *buffers, token = pl.pallas_call(
        functools.partial(top_kernel if is_top else bottom_kernel, takers),
        name="finish_ffn",
        grid=(3,),
        in_specs=[pl.BlockSpec(memory_space=pltpu.SMEM), in_spec, in_spec, ANYWHERE]
        + [ANYWHERE] * len(carried),
        out_specs=out_specs,
        out_shape=out_shape,
        input_output_aliases={4 + i: target for i, (target, _) in enumerate(carried)},
        compiler_params=params(VMEM_ALONE),
        cost_estimate=SMALL,
    )(place, array, arrived, token, *[buffer for _, buffer in carried])
    grads.update(zip(names, buffers))
    return token


def cut_kernel(takers, place_ref, array_ref, arrived_ref, _, *outs):
    value = chosen(takers, place_ref, array_ref, arrived_ref)
    cols = outs[0].shape[1]
    for number, out in enumerate(outs[:-1]):
        out[...] = value[:, number * cols : (number + 1) * cols]
    outs[-1][...] = jnp.zeros_like(outs[-1])


def finish_cut(pieces, token, place, takers, array, arrived):
    count, width = array.shape
    block = count // 2
    cols = width // pieces
    in_spec = pl.BlockSpec((block, width), lambda i: (i, 0))
    out_spec = pl.BlockSpec((block, cols), lambda i: (i, 0))
    return pl.pallas_call(
        functools.partial(cut_kernel, takers),
        name="finish_cut",
        grid=(2,),
        in_specs=[pl.BlockSpec(memory_space=pltpu.SMEM), in_spec, in_spec, ANYWHERE],
        out_specs=[out_spec] * pieces + [kept_out((8, 128))],
        out_shape=[jax.ShapeDtypeStruct((count, cols), wide)] * pieces
        + [jax.ShapeDtypeStruct((8, 128), wide)],
        compiler_params=params(VMEM_ALONE),
        cost_estimate=SMALL,
    )(place, array, arrived, token)


def tie_kernel(*refs):
    refs[-1][...] = jnp.zeros_like(refs[-1])


def tie(*arrays, estimate=SMALL):
    return pl.pallas_call(
        tie_kernel,
        name="tie",
        in_specs=[ANYWHERE] * len(arrays),
        out_specs=IN_VMEM,
        out_shape=jax.ShapeDtypeStruct((8, 128), wide),
        compiler_params=params(VMEM_ALONE),
        cost_estimate=estimate,
    )(*arrays)


def hold_kernel(*_):
    pass


def hold(array, token, estimate=SMALL):
    return pl.pallas_call(
        hold_kernel,
        name="hold",
        in_specs=[ANYWHERE] * 2,
        out_specs=ANYWHERE,
        out_shape=jax.ShapeDtypeStruct(array.shape, array.dtype),
        input_output_aliases={0: 0},
        compiler_params=params(VMEM_ALONE),
        cost_estimate=estimate,
    )(array, token)


def last_kernel(d_h1_ref, x_ref, d_y1_ref, gain_ref, _, out_ref, d_gain_ref):
    rows = x_ref[...].astype(wide)
    d_rows, d_gain = norm_back(rows, norm_scale(rows), gain_ref[...], d_h1_ref[...].astype(wide))
    out_ref[...] = d_rows + d_y1_ref[...]
    d_gain_ref[...] = d_gain[None]


def last_rows(token, d_h1, x_own, d_y1, gain):
    count, width = d_y1.shape
    return pl.pallas_call(
        last_kernel,
        name="last_rows",
        in_specs=[IN_VMEM] * 4 + [ANYWHERE],
        out_specs=[IN_VMEM] * 2,
        out_shape=[
            jax.ShapeDtypeStruct((count, width), wide),
            jax.ShapeDtypeStruct((1, width), wide),
        ],
        compiler_params=params(VMEM_ALONE),
        cost_estimate=SMALL,
    )(d_h1, x_own, d_y1, gain.reshape(1, width), token)


def kept_out(shape):
    return pl.BlockSpec(shape, lambda *_: (0,) * len(shape))


def sums_kernel(count, wg_ref, wu_ref, wd_ref, *refs):
    hidden, d_gate, d_up = [
        jnp.concatenate([ref[...] for ref in refs[i * count : (i + 1) * count]], axis=1)
        for i in range(3)
    ]
    out_ref = refs[-1]
    devices, both_rows, width = out_ref.shape
    own_rows = both_rows // 2
    d_h2 = dot_rows(d_gate, wg_ref[...]) + dot_rows(d_up, wu_ref[...])
    out_ref[:, :own_rows] = d_h2.astype(low).reshape(devices, own_rows, width)
    mlp = mm(hidden, wd_ref[...])
    out_ref[:, own_rows:] = mlp.astype(low).reshape(devices, own_rows, width)


def ffn_sums(own_rows, w_gate, w_up, w_down, hidden, d_gate, d_up, token):
    count = hidden[0].shape[0]
    width = w_gate.shape[0]
    devices = max(1, 256 // own_rows)

    def row_spec(part):
        return pl.BlockSpec((devices * own_rows, part.shape[1]), lambda i: (i, 0))

    parts = [*hidden, *d_gate, *d_up]
    return pl.pallas_call(
        functools.partial(sums_kernel, len(hidden)),
        name="ffn_sums",
        grid=(count // (devices * own_rows),),
        in_specs=[kept_block(w_gate.shape), kept_block(w_up.shape), kept_block(w_down.shape)]
        + [row_spec(part) for part in parts]
        + [ANYWHERE],
        out_specs=pl.BlockSpec((devices, 2 * own_rows, width), lambda i: (i, 0, 0)),
        out_shape=jax.ShapeDtypeStruct((count // own_rows, 2 * own_rows, width), low),
        compiler_params=params(VMEM_ALONE),
        cost_estimate=SMALL,
    )(w_gate, w_up, w_down, *parts, token)


def own_kernel(sums_ref, y1_ref, cot_ref, gain_ref, w_ref, mixed_ref, _, *refs):
    d_y1_ref, d_mixed_ref, d_w_ref, d_gain_ref, layer_ref = refs
    count = y1_ref.shape[0]
    y1 = y1_ref[...]
    layer_ref[...] = (y1 + sums_ref[count:].astype(wide)).astype(low)
    d_rows, d_gain = norm_back(y1, norm_scale(y1), gain_ref[...], sums_ref[:count].astype(wide))
    d_y1 = d_rows + cot_ref[...].astype(wide)
    d_attn = d_y1.astype(low)
    d_y1_ref[...] = d_y1
    d_gain_ref[...] = d_gain[None]
    d_mixed_ref[...] = dot_rows(d_attn, w_ref[...]).astype(low)
    d_w_ref[...] = dot_cols(mixed_ref[...], d_attn).astype(low)


def own_rows_back(token, sums, y1_own, cot_own, gain, w_out_all, mixed_own):
    count, width = y1_own.shape
    inner = w_out_all.shape[0]
    once = [sums.shape, y1_own.shape, cot_own.shape, (1, width), w_out_all.shape, mixed_own.shape]
    return pl.pallas_call(
        own_kernel,
        name="own_rows_back",
        grid=(1,),
        in_specs=[kept_block(shape) for shape in once] + [ANYWHERE],
        out_specs=[
            kept_block((count, width)),
            kept_block((count, inner)),
            kept_block((inner, width)),
            kept_block((1, width)),
            kept_block((count, width)),
        ],
        out_shape=[
            jax.ShapeDtypeStruct((count, width), wide),
            jax.ShapeDtypeStruct((count, inner), low),
            jax.ShapeDtypeStruct((inner, width), low),
            jax.ShapeDtypeStruct((1, width), wide),
            jax.ShapeDtypeStruct((count, width), low),
        ],
        compiler_params=params(VMEM_ALONE),
        cost_estimate=SMALL,
    )(sums, y1_own, cot_own, gain.reshape(1, width), w_out_all, mixed_own, token)


def qkv_back_kernel(d_qkv_ref, h1_ref, w_ref, d_h1_ref, d_w_ref, total):
    step = pl.program_id(0)
    d_qkv = d_qkv_ref[...]
    d_h1_ref[...] = dot_rows(d_qkv, w_ref[...]).astype(low)
    part = dot_cols(h1_ref[...], d_qkv)

    @pl.when(step == 0)
    def _():
        total[...] = part

    @pl.when(step > 0)
    def _():
        total[...] += part

    @pl.when(step == pl.num_programs(0) - 1)
    def _():
        d_w_ref[...] = total[...].astype(low)


def qkv_back(d_qkv, h1_all, w_qkv):
    count, width = h1_all.shape
    cols = w_qkv.shape[1]
    block = min(ROW_BLOCK, count)
    return pl.pallas_call(
        qkv_back_kernel,
        name="qkv_back",
        grid=(count // block,),
        in_specs=[
            pl.BlockSpec((block, cols), lambda i: (i, 0)),
            pl.BlockSpec((block, width), lambda i: (i, 0)),
            kept_block((width, cols)),
        ],
        out_specs=[pl.BlockSpec((block, width), lambda i: (i, 0)), kept_out((width, cols))],
        out_shape=[
            jax.ShapeDtypeStruct((count, width), low),
            jax.ShapeDtypeStruct((width, cols), low),
        ],
        scratch_shapes=[pltpu.VMEM((width, cols), wide)],
        compiler_params=params(VMEM_ALONE),
        cost_estimate=SMALL,
    )(d_qkv, h1_all, w_qkv)


def join_kernel(takers, place_ref, array_ref, arrived_ref, _, out_ref):
    array, arrived = array_ref[...], arrived_ref[...]
    if takers:
        out_ref[...] = jnp.where(is_one_of(place_ref, takers), arrived, array)
    else:
        out_ref[...] = array + arrived


def join(token, place, takers, array, arrived):
    count, width = array.shape
    block = count // 2
    spec = pl.BlockSpec((block, width), lambda i: (i, 0))
    return pl.pallas_call(
        functools.partial(join_kernel, takers),
        name="join",
        grid=(2,),
        in_specs=[pl.BlockSpec(memory_space=pltpu.SMEM), spec, spec, ANYWHERE],
        out_specs=spec,
        out_shape=jax.ShapeDtypeStruct((count, width), low),
        compiler_params=params(VMEM_ALONE),
        cost_estimate=SMALL,
    )(place, array, arrived, token)


def butterfly(array, axis, size):
    if size & (size - 1):
        return lax.psum(array, axis)
    step = 1
    while step < size:
        array = array + lax.ppermute(array, axis, [(i, i ^ step) for i in range(size)])
        step *= 2
    return array


class Chain:
    def __init__(self, axis, size, place, token):
        self.axis, self.size, self.place, self.token = axis, size, place, token
        half = size // 2
        self.stages = [("in", [(s - 1, s), (size - s, size - 1 - s)]) for s in range(1, half)]
        self.stages.append(("in", [(half - 1, half), (half, half - 1)]))
        self.stages += [("out", [(s, s - 1), (size - 1 - s, size - s)]) for s in range(half - 1, 0, -1)]
        self.waiting = []
        self.moving = [[] for _ in self.stages]

    def push(self, array, land):
        self.waiting.append((land, array))

    def send(self, stage, land, array):
        arrived = lax.ppermute(array, self.axis, self.stages[stage][1])
        self.moving[stage].append((land, array, arrived))

    def move(self, stage):
        land, array, arrived = self.moving[stage].pop(0)
        kind, pairs = self.stages[stage]
        takers = tuple(target for _, target in pairs) if kind == "out" else ()
        last = stage + 1 == len(self.stages)
        if kind == "in" or not last:
            array = join(self.token, self.place, takers, array, arrived)
            arrived, takers = array, ()
            self.token = array
        if last:
            self.token = land(self.token, self.place, takers, array, arrived)
        else:
            self.send(stage + 1, land, array)

    def tick(self, estimate=SMALL):
        if self.size == 1 or self.size % 2:
            for land, array in self.waiting:
                array = lax.psum(array, self.axis)
                self.token = land(self.token, self.place, (), array, array)
            self.waiting = []
            return
        ready = [bool(moving) for moving in self.moving]
        if self.waiting:
            land, array = self.waiting.pop(0)
            array = self.token = hold(array, self.token, estimate)
            self.send(0, land, array)
        for stage, can_move in enumerate(ready):
            if can_move:
                self.move(stage)

    def drain(self):
        while self.waiting or any(self.moving):
            self.tick()


def assemble_kernel(place_ref, *refs):
    *pieces, out_ref = refs
    rows = pieces[0].shape[0]
    for number, piece in enumerate(pieces):
        begin = pl.multiple_of((place_ref[1] ^ number) * rows, rows)
        out_ref[pl.ds(begin, rows)] = piece[...]


def assemble(place, pieces):
    count = len(pieces)
    rows, cols = pieces[0].shape
    return pl.pallas_call(
        assemble_kernel,
        name="assemble",
        in_specs=[pl.BlockSpec(memory_space=pltpu.SMEM)]
        + [pl.BlockSpec(memory_space=pltpu.VMEM)] * count,
        out_specs=pl.BlockSpec(memory_space=pltpu.VMEM),
        out_shape=jax.ShapeDtypeStruct((count * rows, cols), pieces[0].dtype),
        compiler_params=params(24),
        cost_estimate=SMALL,
    )(place, *pieces)


def gather_pieces(array, axis, size):
    if size != 8:
        gathered = lax.all_gather(array, axis, axis=0)
        return [gathered[i] for i in range(size)]

    def flip(value, bits):
        return lax.ppermute(value, axis, [(i, i ^ bits) for i in range(size)])

    half = array.shape[0] // 2
    side_a, side_b = flip(array, 2), flip(array, 4)
    far_a, far_b = flip(side_a[:half], 4), flip(side_b[half:], 2)
    mine = [array, side_a, side_b, jnp.concatenate([far_a, far_b], axis=0)]
    pieces = []
    for piece in mine:
        pieces += [piece, flip(piece, 1)]
    return pieces


def per_device(
    tokens,
    cotangent,
    doc_lengths,
    pad_mask,
    w_query,
    w_key,
    w_value,
    w_out,
    w_gate,
    w_up,
    w_down,
    norm_attn,
    norm_mlp,
    mix_gate,
    *,
    n_heads,
    n_batch,
):
    width = tokens.shape[-1]
    rows = tokens.shape[2]
    own_rows = MICRO * rows
    here = lax.axis_index("heads")

    def gather(array):
        return lax.all_gather(array, "heads", axis=0, tiled=True)

    def scatter(array):
        return lax.psum_scatter(array, "heads", scatter_dimension=0, tiled=True)

    def grouped(array):
        return array.reshape(n_heads, MICRO, rows, array.shape[-1])

    def flat(array):
        return array.reshape(n_heads * own_rows, array.shape[-1])

    w_qkv = jnp.concatenate([w_query, w_key, w_value], axis=1)
    share = jax.nn.sigmoid(mix_gate)
    positions = jnp.arange(LEN, dtype=jnp.int32)
    doc_ends = jnp.cumsum(doc_lengths[:, 0], axis=1)
    doc_ids = jnp.sum((positions[None, :, None] >= doc_ends[:, None, :]).astype(jnp.int32), axis=2)
    doc_rows = doc_ids[:, :, None]
    doc_cols = jnp.where(pad_mask[:, 0] == 1, doc_ids, -1)[:, None, :]

    tok_own = tokens.reshape(own_rows, width)
    cot_own = cotangent.reshape(own_rows, width)
    place = jnp.stack(
        [here, here if n_heads == 8 else jnp.zeros_like(here), lax.axis_index("batch")]
    )
    tok_all = gather(tok_own)
    w_out_all = assemble(place, gather_pieces(w_out, "heads", n_heads))
    tok_all, w_out_all = lax.optimization_barrier((tok_all, w_out_all))
    cot_all = gather(lax.optimization_barrier((cot_own, tok_all))[0])
    h1_all, qkv = qkv_rows(tok_all, norm_attn, w_qkv)
    qkv = grouped(qkv)
    mixed = flat(head_forward(share, qkv, doc_rows, doc_cols))
    mixed_pieces = gather_pieces(mixed, "heads", n_heads)
    h2_all, y1_own, mixed_own = mid_rows(place, tok_all, mixed_pieces, w_out_all, norm_mlp)

    chain = Chain("batch", n_batch, place, norm_mlp)
    hidden_cols = w_gate.shape[1]
    cols = hidden_cols // FFN_CHUNKS
    grads = {}

    def push_ffn(number, top, bottom):
        for is_top, part in ((True, top), (False, bottom)):
            chain.push(
                part,
                lambda *moved, is_top=is_top: finish_ffn(
                    is_top, number, cols, hidden_cols, *moved, grads
                ),
            )

    def land_qkv(*moved):
        *grads["qkv"], token = finish_cut(3, *moved)
        return token

    def land_out(*moved):
        grads["out"], token = finish_cut(1, *moved)
        return token

    def first(number):
        *parts, top, bottom = ffn_first(
            number, cols, h2_all, cot_all, w_gate, w_up, w_down, chain.token
        )
        chain.token = top
        push_ffn(number, top, bottom)
        return parts

    def weights(number, parts):
        top, bottom = ffn_weights(number - 2, cols, h2_all, cot_all, *parts, chain.token)
        chain.token = top
        push_ffn(number, top, bottom)

    def wait_for(microseconds):
        chain.token = tie(chain.token, estimate=busy(microseconds))

    part_a = first(0)
    chain.tick()
    part_b = first(1)
    chain.tick()
    part_c = ffn_rest(h2_all, cot_all, w_gate, w_up, w_down, chain.token)
    chain.token = part_c[0]
    chain.tick()
    sums = chain.token = ffn_sums(
        own_rows, w_gate, w_up, w_down, *zip(part_a, part_b, part_c), chain.token
    )
    sums = scatter(sums.reshape(-1, width))
    chain.tick()
    weights(2, part_c)
    weights(3, part_c)
    chain.tick()
    chain.tick()
    chain.tick()

    wait_for(WAITS[0])
    d_y1, d_mixed_own, grad_out, gain_mlp_part, layer_out = own_rows_back(
        chain.token, sums, y1_own, cot_own, norm_mlp, w_out_all, mixed_own
    )
    chain.token = d_y1
    d_mixed = lax.all_to_all(d_mixed_own, "heads", split_axis=1, concat_axis=0, tiled=True)
    grad_out = scatter(grad_out)
    chain.tick()
    wait_for(WAITS[3])
    d_qkv, d_share = head_backward(
        share, qkv, grouped(d_mixed), doc_rows, doc_cols, chain.token
    )
    d_h1, grad_qkv = qkv_back(flat(d_qkv), h1_all, w_qkv)
    chain.token = grad_qkv
    d_h1 = scatter(d_h1)
    chain.push(grad_qkv, land_qkv)
    chain.tick()
    wait_for(WAITS[1])
    chain.push(grad_out, land_out)
    chain.tick()
    chain.tick()

    wait_for(WAITS[2])
    grad_tokens, gain_attn_part = last_rows(chain.token, d_h1, tok_own, d_y1, norm_attn)
    grad_tokens = grad_tokens.reshape(tokens.shape)
    chain.token = gain_attn_part
    slots = jnp.where(jnp.arange(n_heads) == here, jnp.sum(d_share[:, 0, 0]), 0.0)
    sums = jnp.concatenate([gain_attn_part[0], gain_mlp_part[0], slots])
    sums = butterfly(butterfly(sums, "heads", n_heads), "batch", n_batch)
    grad_mix = lax.dynamic_slice_in_dim(sums, 2 * width + here, 1, 0)
    chain.drain()

    return (
        layer_out.reshape(tokens.shape),
        grad_tokens,
        *grads["qkv"],
        grads["out"],
        grads["gate"].reshape(w_gate.shape),
        grads["up"].reshape(w_up.shape),
        grads["down"],
        sums[:width],
        sums[width : 2 * width],
        grad_mix,
    )


def solution(mesh):
    in_specs = (
        P(None, "batch", "heads", None),
        P(None, "batch", "heads", None),
        P(None, "batch", None),
        P(None, "batch", None),
        P(None, "heads"),
        P(None, "heads"),
        P(None, "heads"),
        P("heads", None),
        P(None, "heads"),
        P(None, "heads"),
        P("heads", None),
        P(),
        P(),
        P("heads"),
    )
    out_specs = (
        P(None, "batch", "heads", None),
        P(None, "batch", "heads", None),
        P(None, "heads"),
        P(None, "heads"),
        P(None, "heads"),
        P("heads", None),
        P(None, "heads"),
        P(None, "heads"),
        P("heads", None),
        P(),
        P(),
        P("heads"),
    )

    def program(*arrays):
        return per_device(*arrays, n_heads=mesh.shape["heads"], n_batch=mesh.shape["batch"])

    return jax.shard_map(
        program, mesh=mesh, in_specs=in_specs, out_specs=out_specs, check_vma=False
    )
```

```python
import functools

import jax
import jax.numpy as jnp
from jax import lax
from jax.experimental import pallas as pl
from jax.experimental.pallas import tpu as pltpu
from jax.sharding import PartitionSpec as P

DH = 128
SEG = 512
SEGS = 2
LEN = 1024
MICRO = 2
FFN_CHUNKS = 4
WAITS = (102, 108, 5, 172)
ROW_BLOCK = 512
MIB = 1 << 20
VMEM_ALONE = 60
IN_VMEM = pl.BlockSpec(memory_space=pltpu.VMEM)
ANYWHERE = pl.BlockSpec(memory_space=pl.ANY)
SMALL = pl.CostEstimate(flops=1, bytes_accessed=1, transcendentals=0)
def busy(microseconds):
    return pl.CostEstimate(flops=int(microseconds * 10**9), bytes_accessed=1, transcendentals=0)


epsilon = 1e-05
big_negative = -1e30
low = jnp.bfloat16
wide = jnp.float32


def mm(left_mat, right_mat):
    return jnp.dot(left_mat, right_mat, preferred_element_type=wide)


def dot_rows(left_mat, right_mat):
    return lax.dot_general(
        left_mat, right_mat, (((1,), (1,)), ((), ())), preferred_element_type=wide
    )


def dot_cols(left_mat, right_mat):
    return lax.dot_general(
        left_mat, right_mat, (((0,), (0,)), ((), ())), preferred_element_type=wide
    )


def norm_scale(row_block):
    return lax.rsqrt(jnp.mean(row_block * row_block, axis=-1, keepdims=True) + epsilon)


def norm_back(row_block, row_scale, gain_vec, upstream):
    shaped = upstream * gain_vec
    inner = jnp.mean(shaped * row_block, axis=-1, keepdims=True)
    d_rows = row_scale * shaped - row_block * row_scale * row_scale * row_scale * inner
    d_gain = jnp.sum(upstream * row_block * row_scale, axis=0)
    return (d_rows, d_gain)


def positive(values_in):
    return jnp.where(values_in > 0, values_in + 1.0, jnp.exp(values_in))


def positive_slope(values_in):
    return jnp.where(values_in > 0, 1.0, jnp.exp(values_in))


def params(mebibytes):
    return pltpu.CompilerParams(vmem_limit_bytes=mebibytes * MIB)


def kept_block(shape):
    return pl.BlockSpec(shape, lambda *_: (0,) * len(shape), pipeline_mode=pl.Buffered(1))


def qkv_kernel(x_ref, gain_ref, w_ref, h1_ref, qkv_ref):
    rows = x_ref[...].astype(wide)
    h1 = (rows * norm_scale(rows) * gain_ref[...]).astype(low)
    h1_ref[...] = h1
    qkv_ref[...] = mm(h1, w_ref[...]).astype(low)


def qkv_rows(x_all, gain, w_qkv):
    count, width = x_all.shape
    cols = w_qkv.shape[1]
    block = min(ROW_BLOCK, count)
    return pl.pallas_call(
        qkv_kernel,
        name="qkv_rows",
        grid=(count // block,),
        in_specs=[
            pl.BlockSpec((block, width), lambda i: (i, 0)),
            kept_block((1, width)),
            kept_block((width, cols)),
        ],
        out_specs=[
            pl.BlockSpec((block, width), lambda i: (i, 0)),
            pl.BlockSpec((block, cols), lambda i: (i, 0)),
        ],
        out_shape=[
            jax.ShapeDtypeStruct((count, width), low),
            jax.ShapeDtypeStruct((count, cols), low),
        ],
        compiler_params=params(VMEM_ALONE),
        cost_estimate=SMALL,
    )(x_all, gain.reshape(1, width), w_qkv)


def seg_of(array, segment):
    return array[segment * SEG : (segment + 1) * SEG]


def local_probs(query_seg, key_seg, doc_rows, doc_cols):
    row_ids = lax.broadcasted_iota(jnp.int32, (SEG, SEG), 0)
    col_ids = lax.broadcasted_iota(jnp.int32, (SEG, SEG), 1)
    allowed = ((doc_rows == doc_cols) & (col_ids <= row_ids)) | (col_ids == row_ids)
    scores = jnp.where(allowed, dot_rows(query_seg, key_seg) * DH ** (-0.5), big_negative)
    shifted = jnp.exp(scores - jnp.max(scores, axis=1, keepdims=True))
    return shifted * (1.0 / jnp.sum(shifted, axis=1, keepdims=True))


def head_kernel(share_ref, qkv_ref, doc_rows_ref, doc_cols_ref, mixed_ref):
    share = share_ref[0]
    qkv = qkv_ref[...].reshape(LEN, 3 * DH)
    query, key, value = [qkv[:, i * DH : (i + 1) * DH] for i in range(3)]
    parts = []
    for segment in range(SEGS):
        begin = segment * SEG
        query_seg = seg_of(query, segment)
        doc_rows = doc_rows_ref[begin : begin + SEG]
        probs = local_probs(
            query_seg, seg_of(key, segment), doc_rows, doc_cols_ref[:, begin : begin + SEG]
        )
        result = (1.0 - share) * mm(probs.astype(low), seg_of(value, segment))
        if segment > 0:
            allowed = doc_rows == doc_cols_ref[:, :begin]
            pos_query = positive(query_seg.astype(wide)).astype(low)
            pos_key = positive(key[:begin].astype(wide)).astype(low)
            weights = jnp.where(allowed, dot_rows(pos_query, pos_key), 0.0)
            den = jnp.maximum(jnp.sum(weights, axis=1, keepdims=True), 1.0)
            result = result + share * (mm(weights.astype(low), value[:begin]) / den)
        parts.append(result.astype(low))
    mixed_ref[...] = jnp.concatenate(parts, axis=0).reshape(mixed_ref.shape)


def micro_spec(n_heads, rows, cols):
    return pl.BlockSpec((n_heads, None, rows, cols), lambda m: (0, m, 0, 0))


def doc_specs():
    return [
        pl.BlockSpec((None, LEN, 1), lambda m: (m, 0, 0)),
        pl.BlockSpec((None, 1, LEN), lambda m: (m, 0, 0)),
    ]


def head_forward(share, qkv, doc_rows, doc_cols):
    n_heads, micro, rows, cols = qkv.shape
    pairs = micro * LEN * SEG * 2
    return pl.pallas_call(
        head_kernel,
        name="head_forward",
        grid=(micro,),
        in_specs=[pl.BlockSpec(memory_space=pltpu.SMEM), micro_spec(n_heads, rows, cols), *doc_specs()],
        out_specs=micro_spec(n_heads, rows, DH),
        out_shape=jax.ShapeDtypeStruct((n_heads, micro, rows, DH), low),
        compiler_params=params(VMEM_ALONE),
        cost_estimate=SMALL,
    )(share, qkv, doc_rows, doc_cols)


def head_back_kernel(
    share_ref, qkv_ref, d_mixed_ref, doc_rows_ref, doc_cols_ref, _, d_qkv_ref, d_share_ref
):
    share = share_ref[0]
    scale = DH ** (-0.5)
    qkv = qkv_ref[...].reshape(LEN, 3 * DH)
    query, key, value = [qkv[:, i * DH : (i + 1) * DH] for i in range(3)]
    d_mixed = d_mixed_ref[...].reshape(LEN, DH).astype(wide)
    d_query, d_key, d_value = [[None] * SEGS for _ in range(3)]
    d_share = jnp.zeros((1, 1), wide)
    for segment in range(SEGS):
        begin = segment * SEG
        query_seg, key_seg, value_seg = [seg_of(a, segment) for a in (query, key, value)]
        doc_rows = doc_rows_ref[begin : begin + SEG]
        probs = local_probs(query_seg, key_seg, doc_rows, doc_cols_ref[:, begin : begin + SEG])
        probs_low = probs.astype(low)
        d_mixed_seg = seg_of(d_mixed, segment)
        d_dotted = ((1.0 - share) * d_mixed_seg).astype(low)
        gap = -mm(probs_low, value_seg)
        d_probs = dot_rows(d_dotted, value_seg)
        d_scores = (
            probs * (d_probs - jnp.sum(probs * d_probs, axis=1, keepdims=True))
        ).astype(low)
        d_value[segment] = dot_cols(probs_low, d_dotted)
        d_query[segment] = mm(d_scores, key_seg) * scale
        d_key[segment] = dot_cols(d_scores, query_seg) * scale
        if segment > 0:
            allowed = doc_rows == doc_cols_ref[:, :begin]
            query_float = query_seg.astype(wide)
            key_float = key[:begin].astype(wide)
            pos_query = positive(query_float).astype(low)
            pos_key = positive(key_float).astype(low)
            weights = jnp.where(allowed, dot_rows(pos_query, pos_key), 0.0)
            row_total = jnp.sum(weights, axis=1, keepdims=True)
            inverse = 1.0 / jnp.maximum(row_total, 1.0)
            weights_low = weights.astype(low)
            numerator = mm(weights_low, value[:begin])
            gap = gap + numerator * inverse
            d_recalled = share * d_mixed_seg
            d_numer = (d_recalled * inverse).astype(low)
            d_denom = jnp.where(
                row_total > 1.0,
                -jnp.sum(d_recalled * numerator, axis=1, keepdims=True) * inverse * inverse,
                0.0,
            )
            d_weights = jnp.where(
                allowed, dot_rows(d_numer, value[:begin]) + d_denom, 0.0
            ).astype(low)
            d_query[segment] += mm(d_weights, pos_key) * positive_slope(query_float)
            d_pos_key = dot_cols(d_weights, pos_query) * positive_slope(key_float)
            d_value_before = dot_cols(weights_low, d_numer)
            for earlier in range(segment):
                d_key[earlier] += seg_of(d_pos_key, earlier)
                d_value[earlier] += seg_of(d_value_before, earlier)
        d_share = d_share + jnp.sum(
            jnp.sum(d_mixed_seg * gap, axis=1, keepdims=True), axis=0, keepdims=True
        )
    whole = jnp.concatenate(
        [jnp.concatenate(parts, axis=0).astype(low) for parts in (d_query, d_key, d_value)], axis=1
    )
    d_qkv_ref[...] = whole.reshape(d_qkv_ref.shape)
    d_share_ref[...] = jnp.broadcast_to(d_share * (share * (1.0 - share)), d_share_ref.shape)


def head_backward(share, qkv, d_mixed, doc_rows, doc_cols, token):
    n_heads, micro, rows, cols = qkv.shape
    pairs = micro * LEN * SEG * 2
    return pl.pallas_call(
        head_back_kernel,
        name="head_backward",
        grid=(micro,),
        in_specs=[
            pl.BlockSpec(memory_space=pltpu.SMEM),
            micro_spec(n_heads, rows, cols),
            micro_spec(n_heads, rows, DH),
            *doc_specs(),
            ANYWHERE,
        ],
        out_specs=[
            micro_spec(n_heads, rows, cols),
            pl.BlockSpec((None, 8, 128), lambda m: (m, 0, 0)),
        ],
        out_shape=[
            jax.ShapeDtypeStruct((n_heads, micro, rows, cols), low),
            jax.ShapeDtypeStruct((micro, 8, 128), wide),
        ],
        compiler_params=params(VMEM_ALONE),
        cost_estimate=SMALL,
    )(share, qkv, d_mixed, doc_rows, doc_cols, token)


def mid_kernel(heads, place_ref, x_ref, *refs):
    mixed_refs = refs[:heads]
    w_ref, gain_ref, h2_ref, y1_ref, mixed_own_ref, w_near = refs[heads:]
    step = pl.program_id(0)
    def owner(number):
        return pl.multiple_of((place_ref[1] ^ number) * DH, DH)

    @pl.when(step == 0)
    def _():
        for number in range(heads):
            w_near[number * DH : (number + 1) * DH] = w_ref[pl.ds(owner(number), DH)]

    mixed = jnp.concatenate([ref[...] for ref in mixed_refs], axis=1)
    y1 = x_ref[...].astype(wide) + mm(mixed, w_near[...])
    h2_ref[...] = (y1 * norm_scale(y1) * gain_ref[...]).astype(low)

    @pl.when(step == place_ref[0])
    def _():
        y1_ref[...] = y1
        for number in range(heads):
            mixed_own_ref[:, pl.ds(owner(number), DH)] = mixed_refs[number][...]


def mid_rows(place, x_all, mixed_pieces, w_out_all, gain):
    count, width = x_all.shape
    heads = len(mixed_pieces)
    inner = w_out_all.shape[0]
    block = count // heads
    return pl.pallas_call(
        functools.partial(mid_kernel, heads),
        name="mid_rows",
        grid_spec=pltpu.PrefetchScalarGridSpec(
            num_scalar_prefetch=1,
            grid=(heads,),
            in_specs=[
                pl.BlockSpec((block, width), lambda i, _: (i, 0)),
                *[pl.BlockSpec((block, DH), lambda i, _: (i, 0))] * heads,
                kept_block((inner, width)),
                kept_block((1, width)),
            ],
            out_specs=[
                pl.BlockSpec((block, width), lambda i, _: (i, 0)),
                pl.BlockSpec((block, width), lambda i, _: (0, 0)),
                pl.BlockSpec((block, inner), lambda i, _: (0, 0)),
            ],
            scratch_shapes=[pltpu.VMEM((inner, width), low)],
        ),
        out_shape=[
            jax.ShapeDtypeStruct((count, width), low),
            jax.ShapeDtypeStruct((block, width), wide),
            jax.ShapeDtypeStruct((block, inner), low),
        ],
        compiler_params=params(VMEM_ALONE),
        cost_estimate=SMALL,
    )(place, x_all, *mixed_pieces, w_out_all, gain.reshape(1, width))


def ffn_rows(h2_ref, cot_ref, w_gate, w_up, w_down):
    h2 = h2_ref[...]
    gate = mm(h2, w_gate)
    up = mm(h2, w_up)
    d_hidden = dot_rows(cot_ref[...], w_down)
    sig = jax.nn.sigmoid(gate)
    act = gate * sig
    hidden = (act * up).astype(low)
    d_up = (d_hidden * act).astype(low)
    d_gate = (d_hidden * up * sig * (1.0 + gate * (1.0 - sig))).astype(low)
    return hidden, d_gate, d_up


def ffn_grads(step, hidden, d_both, h2_ref, cot_ref, top_ref, bottom_ref):
    cols = hidden.shape[1]
    side = 2 * cols
    half = cols // 2
    span = pl.ds(pl.multiple_of(step * side, side), side)
    top_ref[:cols, span] = dot_cols(hidden[...], cot_ref[...]).astype(low)
    square = dot_cols(h2_ref[...], d_both[...]).astype(low)
    top_ref[cols:, span] = square[3 * half :]
    bottom_ref[:, span] = square[: 3 * half]


def first_kernel(
    blocks, h2_ref, cot_ref, h2_col_ref, cot_col_ref, wg_ref, wu_ref, wd_ref, _, *refs
):
    hid_ref, dg_ref, du_ref, top_ref, bottom_ref, hid_all, both_all = refs
    step = pl.program_id(0)
    block, cols = hid_ref.shape

    @pl.when(step < blocks)
    def _():
        rows = pl.ds(pl.multiple_of(step * block, block), block)
        hidden, d_gate, d_up = ffn_rows(h2_ref, cot_ref, wg_ref[...], wu_ref[...], wd_ref[...])
        hid_ref[...] = hid_all[rows] = hidden
        dg_ref[...] = both_all[rows, :cols] = d_gate
        du_ref[...] = both_all[rows, cols:] = d_up

    @pl.when(step >= blocks)
    def _():
        ffn_grads(step - blocks, hid_all, both_all, h2_col_ref, cot_col_ref, top_ref, bottom_ref)


def ffn_first(number, cols, h2_all, cot_all, w_gate, w_up, w_down, token):
    count, width = h2_all.shape
    block = min(ROW_BLOCK, count // 2)
    blocks = count // block
    side = 2 * cols
    row_spec = pl.BlockSpec((block, width), lambda i: (jnp.minimum(i, blocks - 1), 0))
    side_spec = pl.BlockSpec((count, side), lambda i: (0, jnp.maximum(i - blocks, 0)))
    col_spec = pl.BlockSpec((width, cols), lambda i: (0, number), pipeline_mode=pl.Buffered(1))
    down_spec = pl.BlockSpec((cols, width), lambda i: (number, 0), pipeline_mode=pl.Buffered(1))
    out_spec = pl.BlockSpec((block, cols), lambda i: (jnp.minimum(i, blocks - 1), 0))
    piece = (3 * cols // 2, width)
    return pl.pallas_call(
        functools.partial(first_kernel, blocks),
        name="ffn_first",
        grid=(blocks + width // side,),
        in_specs=[row_spec, row_spec, side_spec, side_spec, col_spec, col_spec, down_spec, ANYWHERE],
        out_specs=[out_spec] * 3 + [kept_out(piece)] * 2,
        out_shape=[jax.ShapeDtypeStruct((count, cols), low)] * 3
        + [jax.ShapeDtypeStruct(piece, low)] * 2,
        scratch_shapes=[pltpu.VMEM((count, cols), low), pltpu.VMEM((count, side), low)],
        compiler_params=params(VMEM_ALONE),
        cost_estimate=SMALL,
    )(h2_all, cot_all, h2_all, cot_all, w_gate, w_up, w_down, token)


def rest_kernel(h2_ref, cot_ref, wg_ref, wu_ref, wd_ref, _, *refs):
    results = ffn_rows(h2_ref, cot_ref, wg_ref[...], wu_ref[...], wd_ref[...])
    for ref, result in zip(refs, results):
        ref[...] = result


def ffn_rest(h2_all, cot_all, w_gate, w_up, w_down, token):
    count, width = h2_all.shape
    block = min(ROW_BLOCK, count // 2)
    cols = w_gate.shape[1] // 2
    row_spec = pl.BlockSpec((block, width), lambda i: (i, 0))
    col_spec = pl.BlockSpec((width, cols), lambda i: (0, 1), pipeline_mode=pl.Buffered(1))
    down_spec = pl.BlockSpec((cols, width), lambda i: (1, 0), pipeline_mode=pl.Buffered(1))
    return pl.pallas_call(
        rest_kernel,
        name="ffn_rest",
        grid=(count // block,),
        in_specs=[row_spec, row_spec, col_spec, col_spec, down_spec, ANYWHERE],
        out_specs=[pl.BlockSpec((block, cols), lambda i: (i, 0))] * 3,
        out_shape=[jax.ShapeDtypeStruct((count, cols), low)] * 3,
        compiler_params=params(VMEM_ALONE),
        cost_estimate=SMALL,
    )(h2_all, cot_all, w_gate, w_up, w_down, token)


def grads_kernel(h2_ref, cot_ref, hid_ref, dg_ref, du_ref, _, top_ref, bottom_ref, both_all):
    step = pl.program_id(0)
    cols = hid_ref.shape[1]

    @pl.when(step == 0)
    def _():
        both_all[:, :cols] = dg_ref[...]
        both_all[:, cols:] = du_ref[...]

    ffn_grads(step, hid_ref, both_all, h2_ref, cot_ref, top_ref, bottom_ref)


def ffn_weights(number, cols, h2_all, cot_all, hidden, d_gate, d_up, token):
    count, width = h2_all.shape
    side = 2 * cols
    side_spec = pl.BlockSpec((count, side), lambda i: (0, i))
    col_spec = pl.BlockSpec((count, cols), lambda i: (0, number), pipeline_mode=pl.Buffered(1))
    piece = (3 * cols // 2, width)
    return pl.pallas_call(
        grads_kernel,
        name="ffn_weights",
        grid=(width // side,),
        in_specs=[side_spec, side_spec, col_spec, col_spec, col_spec, ANYWHERE],
        out_specs=[kept_out(piece)] * 2,
        out_shape=[jax.ShapeDtypeStruct(piece, low)] * 2,
        scratch_shapes=[pltpu.VMEM((count, side), low)],
        compiler_params=params(VMEM_ALONE),
        cost_estimate=SMALL,
    )(h2_all, cot_all, hidden, d_gate, d_up, token)


def is_one_of(place_ref, takers):
    found = place_ref[2] == takers[0]
    for taker in takers[1:]:
        found = found | (place_ref[2] == taker)
    return found


def chosen(takers, place_ref, array_ref, arrived_ref):
    if not takers:
        return array_ref[...].astype(wide)
    return jnp.where(is_one_of(place_ref, takers), arrived_ref[...], array_ref[...]).astype(wide)


def finish_kernel(cols, has_down, takers, place_ref, array_ref, arrived_ref, *refs):
    *_, gate_ref, up_ref, token_ref = refs
    value = chosen(takers, place_ref, array_ref, arrived_ref)
    if has_down:
        refs[-4][...] = value[:cols]
        value = value[cols:]
    for number in range(gate_ref.shape[0]):
        begin = number * 2 * cols
        gate_ref[number] = value[:, begin : begin + cols]
        up_ref[number] = value[:, begin + cols : begin + 2 * cols]
    token_ref[...] = jnp.zeros_like(token_ref)


def finish_ffn(is_top, number, cols, hidden_cols, token, place, takers, array, arrived, grads):
    count, width = array.shape
    squares = width // (2 * cols)
    in_spec = kept_block((count, width))
    square_shape = jax.ShapeDtypeStruct((squares, 2 * cols, hidden_cols), wide)
    if is_top:
        square_spec = pl.BlockSpec((squares, cols // 2, cols), lambda i: (0, 3, number))
    else:
        square_spec = pl.BlockSpec((squares, count, cols), lambda i: (0, 0, number))
    out_specs = [square_spec, square_spec, kept_out((8, 128))]
    out_shape = [square_shape, square_shape, jax.ShapeDtypeStruct((8, 128), wide)]
    names = ["gate", "up"]
    if is_top:
        out_specs.insert(0, pl.BlockSpec((cols, width), lambda i: (number, 0)))
        out_shape.insert(0, jax.ShapeDtypeStruct((hidden_cols, width), wide))
        names.insert(0, "down")
    carried = [(i, grads[name]) for i, name in enumerate(names) if name in grads]
    *buffers, token = pl.pallas_call(
        functools.partial(finish_kernel, cols, is_top, takers),
        name="finish_ffn",
        grid=(1,),
        in_specs=[pl.BlockSpec(memory_space=pltpu.SMEM), in_spec, in_spec, ANYWHERE]
        + [ANYWHERE] * len(carried),
        out_specs=out_specs,
        out_shape=out_shape,
        input_output_aliases={4 + i: target for i, (target, _) in enumerate(carried)},
        compiler_params=params(VMEM_ALONE),
        cost_estimate=SMALL,
    )(place, array, arrived, token, *[buffer for _, buffer in carried])
    grads.update(zip(names, buffers))
    return token


def cut_kernel(takers, place_ref, array_ref, arrived_ref, _, *outs):
    value = chosen(takers, place_ref, array_ref, arrived_ref)
    cols = outs[0].shape[1]
    for number, out in enumerate(outs[:-1]):
        out[...] = value[:, number * cols : (number + 1) * cols]
    outs[-1][...] = jnp.zeros_like(outs[-1])


def finish_cut(pieces, token, place, takers, array, arrived):
    count, width = array.shape
    block = count // 2
    cols = width // pieces
    in_spec = pl.BlockSpec((block, width), lambda i: (i, 0))
    out_spec = pl.BlockSpec((block, cols), lambda i: (i, 0))
    return pl.pallas_call(
        functools.partial(cut_kernel, takers),
        name="finish_cut",
        grid=(2,),
        in_specs=[pl.BlockSpec(memory_space=pltpu.SMEM), in_spec, in_spec, ANYWHERE],
        out_specs=[out_spec] * pieces + [kept_out((8, 128))],
        out_shape=[jax.ShapeDtypeStruct((count, cols), wide)] * pieces
        + [jax.ShapeDtypeStruct((8, 128), wide)],
        compiler_params=params(VMEM_ALONE),
        cost_estimate=SMALL,
    )(place, array, arrived, token)


def tie_kernel(*refs):
    refs[-1][...] = jnp.zeros_like(refs[-1])


def tie(*arrays, estimate=SMALL):
    return pl.pallas_call(
        tie_kernel,
        name="tie",
        in_specs=[ANYWHERE] * len(arrays),
        out_specs=IN_VMEM,
        out_shape=jax.ShapeDtypeStruct((8, 128), wide),
        compiler_params=params(VMEM_ALONE),
        cost_estimate=estimate,
    )(*arrays)


def hold_kernel(*_):
    pass


def hold(array, token, estimate=SMALL):
    return pl.pallas_call(
        hold_kernel,
        name="hold",
        in_specs=[ANYWHERE] * 2,
        out_specs=ANYWHERE,
        out_shape=jax.ShapeDtypeStruct(array.shape, array.dtype),
        input_output_aliases={0: 0},
        compiler_params=params(VMEM_ALONE),
        cost_estimate=estimate,
    )(array, token)


def last_kernel(d_h1_ref, x_ref, d_y1_ref, gain_ref, y1_ref, mlp_ref, _, out_ref, d_gain_ref, layer_ref):
    rows = x_ref[...].astype(wide)
    d_rows, d_gain = norm_back(rows, norm_scale(rows), gain_ref[...], d_h1_ref[...].astype(wide))
    out_ref[...] = d_rows + d_y1_ref[...]
    d_gain_ref[...] = d_gain[None]
    layer_ref[...] = (y1_ref[...] + mlp_ref[...].astype(wide)).astype(low)


def last_rows(token, d_h1, x_own, d_y1, gain, y1_own, mlp_own):
    count, width = d_y1.shape
    return pl.pallas_call(
        last_kernel,
        name="last_rows",
        grid=(1,),
        in_specs=[kept_block((count, width))] * 3
        + [kept_block((1, width))]
        + [kept_block((count, width))] * 2
        + [ANYWHERE],
        out_specs=[kept_block((count, width)), kept_block((1, width)), kept_block((count, width))],
        out_shape=[
            jax.ShapeDtypeStruct((count, width), wide),
            jax.ShapeDtypeStruct((1, width), wide),
            jax.ShapeDtypeStruct((count, width), low),
        ],
        compiler_params=params(VMEM_ALONE),
        cost_estimate=SMALL,
    )(d_h1, x_own, d_y1, gain.reshape(1, width), y1_own, mlp_own, token)


def kept_out(shape):
    return pl.BlockSpec(shape, lambda *_: (0,) * len(shape))


def together(refs):
    return jnp.concatenate([ref[...] for ref in refs], axis=1)


def back_kernel(count, wg_ref, wu_ref, *refs):
    total = dot_rows(together(refs[:count]), wg_ref[...])
    total = total + dot_rows(together(refs[count : 2 * count]), wu_ref[...])
    refs[-1][...] = total.astype(low)


def ffn_back(w_gate, w_up, d_gate, d_up, token):
    count = d_gate[0].shape[0]
    width = w_gate.shape[0]
    block = min(ROW_BLOCK, count)
    parts = [*d_gate, *d_up]
    return pl.pallas_call(
        functools.partial(back_kernel, len(d_gate)),
        name="ffn_back",
        grid=(count // block,),
        in_specs=[kept_block(w_gate.shape), kept_block(w_up.shape)]
        + [pl.BlockSpec((block, part.shape[1]), lambda i: (i, 0)) for part in parts]
        + [ANYWHERE],
        out_specs=pl.BlockSpec((block, width), lambda i: (i, 0)),
        out_shape=jax.ShapeDtypeStruct((count, width), low),
        compiler_params=params(VMEM_ALONE),
        cost_estimate=SMALL,
    )(w_gate, w_up, *parts, token)


def mlp_kernel(w_ref, *refs):
    result = mm(together(refs[:-2]), w_ref[...])
    refs[-1][...] = result.astype(low).reshape(refs[-1].shape)


def ffn_out(own_rows, w_down, hidden, token):
    count = hidden[0].shape[0]
    width = w_down.shape[1]
    devices = max(1, ROW_BLOCK // own_rows)
    block = devices * own_rows
    return pl.pallas_call(
        mlp_kernel,
        name="ffn_out",
        grid=(count // block,),
        in_specs=[kept_block(w_down.shape)]
        + [pl.BlockSpec((block, part.shape[1]), lambda i: (i, 0)) for part in hidden]
        + [ANYWHERE],
        out_specs=pl.BlockSpec((devices, own_rows, width), lambda i: (i, 0, 0)),
        out_shape=jax.ShapeDtypeStruct((count // own_rows, own_rows + DH, width), low),
        compiler_params=params(VMEM_ALONE),
        cost_estimate=SMALL,
    )(w_down, *hidden, token)


def own_kernel(d_h2_ref, y1_ref, cot_ref, gain_ref, w_ref, mixed_ref, *refs):
    d_y1_ref, d_mixed_ref, d_w_ref, d_gain_ref = refs[-4:]
    y1 = y1_ref[...]
    d_rows, d_gain = norm_back(y1, norm_scale(y1), gain_ref[...], d_h2_ref[...].astype(wide))
    d_y1 = d_rows + cot_ref[...].astype(wide)
    d_attn = d_y1.astype(low)
    d_y1_ref[...] = d_y1
    d_gain_ref[...] = d_gain[None]
    d_mixed_ref[...] = dot_rows(d_attn, w_ref[...]).astype(low)
    d_w_ref[...] = dot_cols(mixed_ref[...], d_attn).astype(low).reshape(d_w_ref.shape)


def own_rows_back(token, d_h2, y1_own, cot_own, gain, w_out_all, mixed_own, buffer):
    count, width = y1_own.shape
    inner = w_out_all.shape[0]
    heads = buffer.shape[0]
    once = [d_h2.shape, y1_own.shape, cot_own.shape, (1, width), w_out_all.shape, mixed_own.shape]
    return pl.pallas_call(
        own_kernel,
        name="own_rows_back",
        grid=(1,),
        in_specs=[kept_block(shape) for shape in once] + [ANYWHERE] * 2,
        out_specs=[
            kept_block((count, width)),
            kept_block((count, inner)),
            pl.BlockSpec(
                (heads, DH, width), lambda i: (0, count // DH, 0), pipeline_mode=pl.Buffered(1)
            ),
            kept_block((1, width)),
        ],
        out_shape=[
            jax.ShapeDtypeStruct((count, width), wide),
            jax.ShapeDtypeStruct((count, inner), low),
            jax.ShapeDtypeStruct(buffer.shape, low),
            jax.ShapeDtypeStruct((1, width), wide),
        ],
        input_output_aliases={7: 2},
        compiler_params=params(VMEM_ALONE),
        cost_estimate=SMALL,
    )(d_h2, y1_own, cot_own, gain.reshape(1, width), w_out_all, mixed_own, token, buffer)


def qkv_back_kernel(d_qkv_ref, h1_ref, w_ref, _, d_h1_ref, d_w_ref, total):
    step = pl.program_id(0)
    d_qkv = d_qkv_ref[...]
    d_h1_ref[...] = dot_rows(d_qkv, w_ref[...]).astype(low)
    part = dot_cols(h1_ref[...], d_qkv)

    @pl.when(step == 0)
    def _():
        total[...] = part

    @pl.when(step > 0)
    def _():
        total[...] += part

    @pl.when(step == pl.num_programs(0) - 1)
    def _():
        d_w_ref[...] = total[...].astype(low)


def qkv_back(d_qkv, h1_all, w_qkv, token):
    count, width = h1_all.shape
    cols = w_qkv.shape[1]
    block = min(ROW_BLOCK, count)
    return pl.pallas_call(
        qkv_back_kernel,
        name="qkv_back",
        grid=(count // block,),
        in_specs=[
            pl.BlockSpec((block, cols), lambda i: (i, 0)),
            pl.BlockSpec((block, width), lambda i: (i, 0)),
            kept_block((width, cols)),
            ANYWHERE,
        ],
        out_specs=[pl.BlockSpec((block, width), lambda i: (i, 0)), kept_out((width, cols))],
        out_shape=[
            jax.ShapeDtypeStruct((count, width), low),
            jax.ShapeDtypeStruct((width, cols), low),
        ],
        scratch_shapes=[pltpu.VMEM((width, cols), wide)],
        compiler_params=params(VMEM_ALONE),
        cost_estimate=SMALL,
    )(d_qkv, h1_all, w_qkv, token)


def join_kernel(takers, place_ref, array_ref, arrived_ref, _, out_ref):
    array, arrived = array_ref[...], arrived_ref[...]
    if takers:
        out_ref[...] = jnp.where(is_one_of(place_ref, takers), arrived, array)
    else:
        out_ref[...] = array + arrived


def join(token, place, takers, array, arrived):
    count, width = array.shape
    block = count // 2
    spec = pl.BlockSpec((block, width), lambda i: (i, 0))
    return pl.pallas_call(
        functools.partial(join_kernel, takers),
        name="join",
        grid=(count // block,),
        in_specs=[pl.BlockSpec(memory_space=pltpu.SMEM), spec, spec, ANYWHERE],
        out_specs=spec,
        out_shape=jax.ShapeDtypeStruct((count, width), low),
        compiler_params=params(VMEM_ALONE),
        cost_estimate=SMALL,
    )(place, array, arrived, token)


def butterfly(array, axis, size):
    if size & (size - 1):
        return lax.psum(array, axis)
    step = 1
    while step < size:
        array = array + lax.ppermute(array, axis, [(i, i ^ step) for i in range(size)])
        step *= 2
    return array


class Chain:
    def __init__(self, axis, size, place, token):
        self.axis, self.size, self.place, self.token = axis, size, place, token
        half = size // 2
        self.stages = [("in", [(s - 1, s), (size - s, size - 1 - s)]) for s in range(1, half)]
        self.stages.append(("in", [(half - 1, half), (half, half - 1)]))
        self.stages += [("out", [(s, s - 1), (size - 1 - s, size - s)]) for s in range(half - 1, 0, -1)]
        self.waiting = []
        self.moving = [[] for _ in self.stages]

    def push(self, array, land):
        self.waiting.append((land, array))

    def send(self, stage, land, array):
        arrived = lax.ppermute(array, self.axis, self.stages[stage][1])
        self.moving[stage].append((land, array, arrived))

    def move(self, stage):
        land, array, arrived = self.moving[stage].pop(0)
        kind, pairs = self.stages[stage]
        takers = tuple(target for _, target in pairs) if kind == "out" else ()
        last = stage + 1 == len(self.stages)
        if kind == "in" or not last:
            array = join(self.token, self.place, takers, array, arrived)
            arrived, takers = array, ()
            self.token = array
        if last:
            self.token = land(self.token, self.place, takers, array, arrived)
        else:
            self.send(stage + 1, land, array)

    def tick(self, between=None):
        if self.size == 1 or self.size % 2:
            for land, array in self.waiting:
                array = lax.psum(array, self.axis)
                self.token = land(self.token, self.place, (), array, array)
            self.waiting = []
            return between() if between else None
        result = None
        ready = [bool(moving) for moving in self.moving]
        if self.waiting:
            land, array = self.waiting.pop(0)
            array = self.token = hold(array, self.token)
            self.send(0, land, array)
        for stage, can_move in enumerate(ready):
            if can_move:
                self.move(stage)
            if stage == 0 and between:
                result = between()
        return result

    def drain(self):
        while self.waiting or any(self.moving):
            self.tick()


def assemble_kernel(place_ref, *refs):
    *pieces, out_ref = refs
    rows = pieces[0].shape[0]
    for number, piece in enumerate(pieces):
        begin = pl.multiple_of((place_ref[1] ^ number) * rows, rows)
        out_ref[pl.ds(begin, rows)] = piece[...]


def assemble(place, pieces):
    count = len(pieces)
    rows, cols = pieces[0].shape
    return pl.pallas_call(
        assemble_kernel,
        name="assemble",
        in_specs=[pl.BlockSpec(memory_space=pltpu.SMEM)]
        + [pl.BlockSpec(memory_space=pltpu.VMEM)] * count,
        out_specs=pl.BlockSpec(memory_space=pltpu.VMEM),
        out_shape=jax.ShapeDtypeStruct((count * rows, cols), pieces[0].dtype),
        compiler_params=params(24),
        cost_estimate=SMALL,
    )(place, *pieces)


def gather_pieces(array, axis, size):
    if size != 8:
        gathered = lax.all_gather(array, axis, axis=0)
        return [gathered[i] for i in range(size)]

    def flip(value, bits):
        return lax.ppermute(value, axis, [(i, i ^ bits) for i in range(size)])

    half = array.shape[0] // 2
    side_a, side_b = flip(array, 2), flip(array, 4)
    far_a, far_b = flip(side_a[:half], 4), flip(side_b[half:], 2)
    mine = [array, side_a, side_b, jnp.concatenate([far_a, far_b], axis=0)]
    pieces = []
    for piece in mine:
        pieces += [piece, flip(piece, 1)]
    return pieces


def per_device(
    tokens,
    cotangent,
    doc_lengths,
    pad_mask,
    w_query,
    w_key,
    w_value,
    w_out,
    w_gate,
    w_up,
    w_down,
    norm_attn,
    norm_mlp,
    mix_gate,
    *,
    n_heads,
    n_batch,
):
    width = tokens.shape[-1]
    rows = tokens.shape[2]
    own_rows = MICRO * rows
    here = lax.axis_index("heads")

    def gather(array):
        return lax.all_gather(array, "heads", axis=0, tiled=True)

    def scatter(array):
        return lax.psum_scatter(array, "heads", scatter_dimension=0, tiled=True)

    def grouped(array):
        return array.reshape(n_heads, MICRO, rows, array.shape[-1])

    def flat(array):
        return array.reshape(n_heads * own_rows, array.shape[-1])

    w_qkv = jnp.concatenate([w_query, w_key, w_value], axis=1)
    share = jax.nn.sigmoid(mix_gate)
    positions = jnp.arange(LEN, dtype=jnp.int32)
    doc_ends = jnp.cumsum(doc_lengths[:, 0], axis=1)
    doc_ids = jnp.sum((positions[None, :, None] >= doc_ends[:, None, :]).astype(jnp.int32), axis=2)
    doc_rows = doc_ids[:, :, None]
    doc_cols = jnp.where(pad_mask[:, 0] == 1, doc_ids, -1)[:, None, :]

    tok_own = tokens.reshape(own_rows, width)
    cot_own = cotangent.reshape(own_rows, width)
    place = jnp.stack(
        [here, here if n_heads == 8 else jnp.zeros_like(here), lax.axis_index("batch")]
    )
    tok_all = gather(tok_own)
    w_out_all = assemble(place, gather_pieces(w_out, "heads", n_heads))
    tok_all, w_out_all = lax.optimization_barrier((tok_all, w_out_all))
    cot_all = gather(lax.optimization_barrier((cot_own, tok_all))[0])
    h1_all, qkv = qkv_rows(tok_all, norm_attn, w_qkv)
    qkv = grouped(qkv)
    mixed = flat(head_forward(share, qkv, doc_rows, doc_cols))
    mixed_pieces = gather_pieces(mixed, "heads", n_heads)
    h2_all, y1_own, mixed_own = mid_rows(place, tok_all, mixed_pieces, w_out_all, norm_mlp)

    chain = Chain("batch", n_batch, place, norm_mlp)
    hidden_cols = w_gate.shape[1]
    cols = hidden_cols // FFN_CHUNKS
    grads = {}

    def push_ffn(number, top, bottom):
        for is_top, part in ((True, top), (False, bottom)):
            chain.push(
                part,
                lambda *moved, is_top=is_top: finish_ffn(
                    is_top, number, cols, hidden_cols, *moved, grads
                ),
            )

    def land_qkv(*moved):
        *grads["qkv"], token = finish_cut(3, *moved)
        return token

    def land_out(*moved):
        grads["out"], token = finish_cut(1, *moved)
        return token

    def first(number):
        *parts, top, bottom = ffn_first(
            number, cols, h2_all, cot_all, w_gate, w_up, w_down, chain.token
        )
        chain.token = parts[0]
        push_ffn(number, top, bottom)
        return parts

    def weights(number, parts):
        top, bottom = ffn_weights(number - 2, cols, h2_all, cot_all, *parts, chain.token)
        chain.token = bottom
        push_ffn(number, top, bottom)

    def wait_for(microseconds):
        chain.token = tie(chain.token, estimate=busy(microseconds))

    part_a = first(0)
    chain.tick()
    part_b = first(1)
    chain.tick()
    part_c = ffn_rest(h2_all, cot_all, w_gate, w_up, w_down, chain.token)
    chain.token = part_c[0]
    chain.tick()
    hidden, d_gate, d_up = zip(part_a, part_b, part_c)
    d_h2 = chain.token = ffn_back(w_gate, w_up, d_gate, d_up, chain.token)
    d_h2 = scatter(d_h2)
    chain.tick()
    weights(2, part_c)
    chain.tick()
    parts = chain.token = ffn_out(own_rows, w_down, hidden, chain.token)

    chain.tick()
    wait_for(WAITS[0])
    d_y1, d_mixed_own, parts, gain_mlp_part = own_rows_back(
        chain.token, d_h2, y1_own, cot_own, norm_mlp, w_out_all, mixed_own, parts
    )
    chain.token = d_y1
    d_mixed = lax.all_to_all(d_mixed_own, "heads", split_axis=1, concat_axis=0, tiled=True)
    parts = scatter(parts.reshape(-1, width))
    weights(3, part_c)
    chain.tick()
    wait_for(WAITS[2])
    d_qkv, d_share = head_backward(
        share, qkv, grouped(d_mixed), doc_rows, doc_cols, chain.token
    )
    chain.token = d_share
    chain.tick()
    d_h1, grad_qkv = qkv_back(flat(d_qkv), h1_all, w_qkv, chain.token)
    chain.token = d_h1
    chain.push(grad_qkv, land_qkv)

    def scatter_last():
        wait_for(WAITS[3])
        chain.token = tie(chain.token, parts)
        chain.token = hold(d_h1, chain.token)
        return scatter(chain.token)

    d_h1 = chain.tick(scatter_last)
    chain.push(parts[own_rows:], land_out)
    chain.tick()
    chain.tick()

    wait_for(WAITS[1])
    grad_tokens, gain_attn_part, layer_out = last_rows(
        chain.token, d_h1, tok_own, d_y1, norm_attn, y1_own, parts
    )
    grad_tokens = grad_tokens.reshape(tokens.shape)
    chain.token = gain_attn_part
    slots = jnp.where(jnp.arange(n_heads) == here, jnp.sum(d_share[:, 0, 0]), 0.0)
    sums = jnp.concatenate([gain_attn_part[0], gain_mlp_part[0], slots])
    sums = butterfly(butterfly(sums, "heads", n_heads), "batch", n_batch)
    grad_mix = lax.dynamic_slice_in_dim(sums, 2 * width + here, 1, 0)
    chain.drain()

    return (
        layer_out.reshape(tokens.shape),
        grad_tokens,
        *grads["qkv"],
        grads["out"],
        grads["gate"].reshape(w_gate.shape),
        grads["up"].reshape(w_up.shape),
        grads["down"],
        sums[:width],
        sums[width : 2 * width],
        grad_mix,
    )


def solution(mesh):
    in_specs = (
        P(None, "batch", "heads", None),
        P(None, "batch", "heads", None),
        P(None, "batch", None),
        P(None, "batch", None),
        P(None, "heads"),
        P(None, "heads"),
        P(None, "heads"),
        P("heads", None),
        P(None, "heads"),
        P(None, "heads"),
        P("heads", None),
        P(),
        P(),
        P("heads"),
    )
    out_specs = (
        P(None, "batch", "heads", None),
        P(None, "batch", "heads", None),
        P(None, "heads"),
        P(None, "heads"),
        P(None, "heads"),
        P("heads", None),
        P(None, "heads"),
        P(None, "heads"),
        P("heads", None),
        P(),
        P(),
        P("heads"),
    )

    def program(*arrays):
        return per_device(*arrays, n_heads=mesh.shape["heads"], n_batch=mesh.shape["batch"])

    return jax.shard_map(
        program, mesh=mesh, in_specs=in_specs, out_specs=out_specs, check_vma=False
    )
```

```python
import functools

import jax
import jax.numpy as jnp
from jax import lax
from jax.experimental import pallas as pl
from jax.experimental.pallas import tpu as pltpu
from jax.sharding import PartitionSpec as P

DH = 128
SEG = 512
SEGS = 2
LEN = 1024
MICRO = 2
FFN_CHUNKS = 4
WAITS = (102, 108, 5, 172)
ROW_BLOCK = 512
MIB = 1 << 20
VMEM_ALONE = 60
IN_VMEM = pl.BlockSpec(memory_space=pltpu.VMEM)
ANYWHERE = pl.BlockSpec(memory_space=pl.ANY)
SMALL = pl.CostEstimate(flops=1, bytes_accessed=1, transcendentals=0)
def busy(microseconds):
    return pl.CostEstimate(flops=int(microseconds * 10**9), bytes_accessed=1, transcendentals=0)


epsilon = 1e-05
big_negative = -1e30
low = jnp.bfloat16
wide = jnp.float32


def mm(left_mat, right_mat):
    return jnp.dot(left_mat, right_mat, preferred_element_type=wide)


def dot_rows(left_mat, right_mat):
    return lax.dot_general(
        left_mat, right_mat, (((1,), (1,)), ((), ())), preferred_element_type=wide
    )


def dot_cols(left_mat, right_mat):
    return lax.dot_general(
        left_mat, right_mat, (((0,), (0,)), ((), ())), preferred_element_type=wide
    )


def norm_scale(row_block):
    return lax.rsqrt(jnp.mean(row_block * row_block, axis=-1, keepdims=True) + epsilon)


def norm_back(row_block, row_scale, gain_vec, upstream):
    shaped = upstream * gain_vec
    inner = jnp.mean(shaped * row_block, axis=-1, keepdims=True)
    d_rows = row_scale * shaped - row_block * row_scale * row_scale * row_scale * inner
    d_gain = jnp.sum(upstream * row_block * row_scale, axis=0)
    return (d_rows, d_gain)


def positive(values_in):
    return jnp.where(values_in > 0, values_in + 1.0, jnp.exp(values_in))


def positive_slope(values_in):
    return jnp.where(values_in > 0, 1.0, jnp.exp(values_in))


def params(mebibytes):
    return pltpu.CompilerParams(vmem_limit_bytes=mebibytes * MIB)


def kept_block(shape):
    return pl.BlockSpec(shape, lambda *_: (0,) * len(shape), pipeline_mode=pl.Buffered(1))


def qkv_kernel(x_ref, gain_ref, w_ref, h1_ref, qkv_ref):
    rows = x_ref[...].astype(wide)
    h1 = (rows * norm_scale(rows) * gain_ref[...]).astype(low)
    h1_ref[...] = h1
    qkv_ref[...] = mm(h1, w_ref[...]).astype(low)


def qkv_rows(x_all, gain, w_qkv):
    count, width = x_all.shape
    cols = w_qkv.shape[1]
    block = min(ROW_BLOCK, count)
    return pl.pallas_call(
        qkv_kernel,
        name="qkv_rows",
        grid=(count // block,),
        in_specs=[
            pl.BlockSpec((block, width), lambda i: (i, 0)),
            kept_block((1, width)),
            kept_block((width, cols)),
        ],
        out_specs=[
            pl.BlockSpec((block, width), lambda i: (i, 0)),
            pl.BlockSpec((block, cols), lambda i: (i, 0)),
        ],
        out_shape=[
            jax.ShapeDtypeStruct((count, width), low),
            jax.ShapeDtypeStruct((count, cols), low),
        ],
        compiler_params=params(VMEM_ALONE),
        cost_estimate=SMALL,
    )(x_all, gain.reshape(1, width), w_qkv)


def seg_of(array, segment):
    return array[segment * SEG : (segment + 1) * SEG]


def local_probs(query_seg, key_seg, doc_rows, doc_cols):
    row_ids = lax.broadcasted_iota(jnp.int32, (SEG, SEG), 0)
    col_ids = lax.broadcasted_iota(jnp.int32, (SEG, SEG), 1)
    allowed = ((doc_rows == doc_cols) & (col_ids <= row_ids)) | (col_ids == row_ids)
    scores = jnp.where(allowed, dot_rows(query_seg, key_seg) * DH ** (-0.5), big_negative)
    shifted = jnp.exp(scores - jnp.max(scores, axis=1, keepdims=True))
    return shifted * (1.0 / jnp.sum(shifted, axis=1, keepdims=True))


def head_kernel(share_ref, qkv_ref, doc_rows_ref, doc_cols_ref, mixed_ref):
    share = share_ref[0]
    qkv = qkv_ref[...].reshape(LEN, 3 * DH)
    query, key, value = [qkv[:, i * DH : (i + 1) * DH] for i in range(3)]
    parts = []
    for segment in range(SEGS):
        begin = segment * SEG
        query_seg = seg_of(query, segment)
        doc_rows = doc_rows_ref[begin : begin + SEG]
        probs = local_probs(
            query_seg, seg_of(key, segment), doc_rows, doc_cols_ref[:, begin : begin + SEG]
        )
        result = (1.0 - share) * mm(probs.astype(low), seg_of(value, segment))
        if segment > 0:
            allowed = doc_rows == doc_cols_ref[:, :begin]
            pos_query = positive(query_seg.astype(wide)).astype(low)
            pos_key = positive(key[:begin].astype(wide)).astype(low)
            weights = jnp.where(allowed, dot_rows(pos_query, pos_key), 0.0)
            den = jnp.maximum(jnp.sum(weights, axis=1, keepdims=True), 1.0)
            result = result + share * (mm(weights.astype(low), value[:begin]) / den)
        parts.append(result.astype(low))
    mixed_ref[...] = jnp.concatenate(parts, axis=0).reshape(mixed_ref.shape)


def micro_spec(n_heads, rows, cols):
    return pl.BlockSpec((n_heads, None, rows, cols), lambda m: (0, m, 0, 0))


def doc_specs():
    return [
        pl.BlockSpec((None, LEN, 1), lambda m: (m, 0, 0)),
        pl.BlockSpec((None, 1, LEN), lambda m: (m, 0, 0)),
    ]


def head_forward(share, qkv, doc_rows, doc_cols):
    n_heads, micro, rows, cols = qkv.shape
    pairs = micro * LEN * SEG * 2
    return pl.pallas_call(
        head_kernel,
        name="head_forward",
        grid=(micro,),
        in_specs=[pl.BlockSpec(memory_space=pltpu.SMEM), micro_spec(n_heads, rows, cols), *doc_specs()],
        out_specs=micro_spec(n_heads, rows, DH),
        out_shape=jax.ShapeDtypeStruct((n_heads, micro, rows, DH), low),
        compiler_params=params(VMEM_ALONE),
        cost_estimate=SMALL,
    )(share, qkv, doc_rows, doc_cols)


def head_back_kernel(
    share_ref, qkv_ref, d_mixed_ref, doc_rows_ref, doc_cols_ref, _, d_qkv_ref, d_share_ref
):
    share = share_ref[0]
    scale = DH ** (-0.5)
    qkv = qkv_ref[...].reshape(LEN, 3 * DH)
    query, key, value = [qkv[:, i * DH : (i + 1) * DH] for i in range(3)]
    d_mixed = d_mixed_ref[...].reshape(LEN, DH).astype(wide)
    d_query, d_key, d_value = [[None] * SEGS for _ in range(3)]
    d_share = jnp.zeros((1, 1), wide)
    for segment in range(SEGS):
        begin = segment * SEG
        query_seg, key_seg, value_seg = [seg_of(a, segment) for a in (query, key, value)]
        doc_rows = doc_rows_ref[begin : begin + SEG]
        probs = local_probs(query_seg, key_seg, doc_rows, doc_cols_ref[:, begin : begin + SEG])
        probs_low = probs.astype(low)
        d_mixed_seg = seg_of(d_mixed, segment)
        d_dotted = ((1.0 - share) * d_mixed_seg).astype(low)
        gap = -mm(probs_low, value_seg)
        d_probs = dot_rows(d_dotted, value_seg)
        d_scores = (
            probs * (d_probs - jnp.sum(probs * d_probs, axis=1, keepdims=True))
        ).astype(low)
        d_value[segment] = dot_cols(probs_low, d_dotted)
        d_query[segment] = mm(d_scores, key_seg) * scale
        d_key[segment] = dot_cols(d_scores, query_seg) * scale
        if segment > 0:
            allowed = doc_rows == doc_cols_ref[:, :begin]
            query_float = query_seg.astype(wide)
            key_float = key[:begin].astype(wide)
            pos_query = positive(query_float).astype(low)
            pos_key = positive(key_float).astype(low)
            weights = jnp.where(allowed, dot_rows(pos_query, pos_key), 0.0)
            row_total = jnp.sum(weights, axis=1, keepdims=True)
            inverse = 1.0 / jnp.maximum(row_total, 1.0)
            weights_low = weights.astype(low)
            numerator = mm(weights_low, value[:begin])
            gap = gap + numerator * inverse
            d_recalled = share * d_mixed_seg
            d_numer = (d_recalled * inverse).astype(low)
            d_denom = jnp.where(
                row_total > 1.0,
                -jnp.sum(d_recalled * numerator, axis=1, keepdims=True) * inverse * inverse,
                0.0,
            )
            d_weights = jnp.where(
                allowed, dot_rows(d_numer, value[:begin]) + d_denom, 0.0
            ).astype(low)
            d_query[segment] += mm(d_weights, pos_key) * positive_slope(query_float)
            d_pos_key = dot_cols(d_weights, pos_query) * positive_slope(key_float)
            d_value_before = dot_cols(weights_low, d_numer)
            for earlier in range(segment):
                d_key[earlier] += seg_of(d_pos_key, earlier)
                d_value[earlier] += seg_of(d_value_before, earlier)
        d_share = d_share + jnp.sum(
            jnp.sum(d_mixed_seg * gap, axis=1, keepdims=True), axis=0, keepdims=True
        )
    whole = jnp.concatenate(
        [jnp.concatenate(parts, axis=0).astype(low) for parts in (d_query, d_key, d_value)], axis=1
    )
    d_qkv_ref[...] = whole.reshape(d_qkv_ref.shape)
    d_share_ref[...] = jnp.broadcast_to(d_share * (share * (1.0 - share)), d_share_ref.shape)


def head_backward(share, qkv, d_mixed, doc_rows, doc_cols, token):
    n_heads, micro, rows, cols = qkv.shape
    pairs = micro * LEN * SEG * 2
    return pl.pallas_call(
        head_back_kernel,
        name="head_backward",
        grid=(micro,),
        in_specs=[
            pl.BlockSpec(memory_space=pltpu.SMEM),
            micro_spec(n_heads, rows, cols),
            micro_spec(n_heads, rows, DH),
            *doc_specs(),
            ANYWHERE,
        ],
        out_specs=[
            micro_spec(n_heads, rows, cols),
            pl.BlockSpec((None, 8, 128), lambda m: (m, 0, 0)),
        ],
        out_shape=[
            jax.ShapeDtypeStruct((n_heads, micro, rows, cols), low),
            jax.ShapeDtypeStruct((micro, 8, 128), wide),
        ],
        compiler_params=params(VMEM_ALONE),
        cost_estimate=SMALL,
    )(share, qkv, d_mixed, doc_rows, doc_cols, token)


def mid_kernel(heads, place_ref, x_ref, *refs):
    mixed_refs = refs[:heads]
    w_ref, gain_ref, h2_ref, y1_ref, mixed_own_ref, w_near = refs[heads:]
    step = pl.program_id(0)
    own_rows = y1_ref.shape[0]
    devices = x_ref.shape[0] // own_rows

    def owner(number):
        return pl.multiple_of((place_ref[1] ^ number) * DH, DH)

    @pl.when(step == 0)
    def _():
        for number in range(heads):
            w_near[number * DH : (number + 1) * DH] = w_ref[pl.ds(owner(number), DH)]

    mixed = jnp.concatenate([ref[...] for ref in mixed_refs], axis=1)
    y1 = x_ref[...].astype(wide) + mm(mixed, w_near[...])
    h2_ref[...] = (y1 * norm_scale(y1) * gain_ref[...]).astype(low)
    for device in range(devices):
        begin = device * own_rows

        @pl.when(step * devices + device == place_ref[0])
        def _():
            y1_ref[...] = y1[begin : begin + own_rows]
            for number in range(heads):
                mixed_own_ref[:, pl.ds(owner(number), DH)] = mixed_refs[number][
                    begin : begin + own_rows
                ]


def mid_rows(place, x_all, mixed_pieces, w_out_all, gain):
    count, width = x_all.shape
    heads = len(mixed_pieces)
    inner = w_out_all.shape[0]
    own_rows = count // heads
    block = max(1, ROW_BLOCK // own_rows) * own_rows
    return pl.pallas_call(
        functools.partial(mid_kernel, heads),
        name="mid_rows",
        grid_spec=pltpu.PrefetchScalarGridSpec(
            num_scalar_prefetch=1,
            grid=(count // block,),
            in_specs=[
                pl.BlockSpec((block, width), lambda i, _: (i, 0)),
                *[pl.BlockSpec((block, DH), lambda i, _: (i, 0))] * heads,
                kept_block((inner, width)),
                kept_block((1, width)),
            ],
            out_specs=[
                pl.BlockSpec((block, width), lambda i, _: (i, 0)),
                pl.BlockSpec((own_rows, width), lambda i, _: (0, 0)),
                pl.BlockSpec((own_rows, inner), lambda i, _: (0, 0)),
            ],
            scratch_shapes=[pltpu.VMEM((inner, width), low)],
        ),
        out_shape=[
            jax.ShapeDtypeStruct((count, width), low),
            jax.ShapeDtypeStruct((own_rows, width), wide),
            jax.ShapeDtypeStruct((own_rows, inner), low),
        ],
        compiler_params=params(VMEM_ALONE),
        cost_estimate=SMALL,
    )(place, x_all, *mixed_pieces, w_out_all, gain.reshape(1, width))


def ffn_rows(h2_ref, cot_ref, w_gate, w_up, w_down):
    h2 = h2_ref[...]
    gate = mm(h2, w_gate)
    up = mm(h2, w_up)
    d_hidden = dot_rows(cot_ref[...], w_down)
    sig = jax.nn.sigmoid(gate)
    act = gate * sig
    hidden = (act * up).astype(low)
    d_up = (d_hidden * act).astype(low)
    d_gate = (d_hidden * up * sig * (1.0 + gate * (1.0 - sig))).astype(low)
    return hidden, d_gate, d_up


def ffn_grads(step, hidden, d_both, h2_ref, cot_ref, top_ref, bottom_ref):
    cols = hidden.shape[1]
    side = 2 * cols
    half = cols // 2
    span = pl.ds(pl.multiple_of(step * side, side), side)
    top_ref[:cols, span] = dot_cols(hidden[...], cot_ref[...]).astype(low)
    square = dot_cols(h2_ref[...], d_both[...]).astype(low)
    top_ref[cols:, span] = square[3 * half :]
    bottom_ref[:, span] = square[: 3 * half]


def first_kernel(
    blocks, h2_ref, cot_ref, h2_col_ref, cot_col_ref, wg_ref, wu_ref, wd_ref, _, *refs
):
    hid_ref, dg_ref, du_ref, top_ref, bottom_ref, hid_all, both_all = refs
    step = pl.program_id(0)
    block, cols = hid_ref.shape

    @pl.when(step < blocks)
    def _():
        rows = pl.ds(pl.multiple_of(step * block, block), block)
        hidden, d_gate, d_up = ffn_rows(h2_ref, cot_ref, wg_ref[...], wu_ref[...], wd_ref[...])
        hid_ref[...] = hid_all[rows] = hidden
        dg_ref[...] = both_all[rows, :cols] = d_gate
        du_ref[...] = both_all[rows, cols:] = d_up

    @pl.when(step >= blocks)
    def _():
        ffn_grads(step - blocks, hid_all, both_all, h2_col_ref, cot_col_ref, top_ref, bottom_ref)


def ffn_first(number, cols, h2_all, cot_all, w_gate, w_up, w_down, token):
    count, width = h2_all.shape
    block = min(ROW_BLOCK, count // 2)
    blocks = count // block
    side = 2 * cols
    row_spec = pl.BlockSpec((block, width), lambda i: (jnp.minimum(i, blocks - 1), 0))
    side_spec = pl.BlockSpec((count, side), lambda i: (0, jnp.maximum(i - blocks, 0)))
    col_spec = pl.BlockSpec((width, cols), lambda i: (0, number), pipeline_mode=pl.Buffered(1))
    down_spec = pl.BlockSpec((cols, width), lambda i: (number, 0), pipeline_mode=pl.Buffered(1))
    out_spec = pl.BlockSpec((block, cols), lambda i: (jnp.minimum(i, blocks - 1), 0))
    piece = (3 * cols // 2, width)
    return pl.pallas_call(
        functools.partial(first_kernel, blocks),
        name="ffn_first",
        grid=(blocks + width // side,),
        in_specs=[row_spec, row_spec, side_spec, side_spec, col_spec, col_spec, down_spec, ANYWHERE],
        out_specs=[out_spec] * 3 + [kept_out(piece)] * 2,
        out_shape=[jax.ShapeDtypeStruct((count, cols), low)] * 3
        + [jax.ShapeDtypeStruct(piece, low)] * 2,
        scratch_shapes=[pltpu.VMEM((count, cols), low), pltpu.VMEM((count, side), low)],
        compiler_params=params(VMEM_ALONE),
        cost_estimate=SMALL,
    )(h2_all, cot_all, h2_all, cot_all, w_gate, w_up, w_down, token)


def rest_kernel(h2_ref, cot_ref, wg_ref, wu_ref, wd_ref, _, *refs):
    results = ffn_rows(h2_ref, cot_ref, wg_ref[...], wu_ref[...], wd_ref[...])
    for ref, result in zip(refs, results):
        ref[...] = result


def ffn_rest(number, cols, h2_all, cot_all, w_gate, w_up, w_down, token):
    count, width = h2_all.shape
    block = min(ROW_BLOCK, count // 2)
    row_spec = pl.BlockSpec((block, width), lambda i: (i, 0))
    col_spec = pl.BlockSpec((width, cols), lambda i: (0, number), pipeline_mode=pl.Buffered(1))
    down_spec = pl.BlockSpec((cols, width), lambda i: (number, 0), pipeline_mode=pl.Buffered(1))
    return pl.pallas_call(
        rest_kernel,
        name="ffn_rest",
        grid=(count // block,),
        in_specs=[row_spec, row_spec, col_spec, col_spec, down_spec, ANYWHERE],
        out_specs=[pl.BlockSpec((block, cols), lambda i: (i, 0))] * 3,
        out_shape=[jax.ShapeDtypeStruct((count, cols), low)] * 3,
        compiler_params=params(VMEM_ALONE),
        cost_estimate=SMALL,
    )(h2_all, cot_all, w_gate, w_up, w_down, token)


def grads_kernel(h2_ref, cot_ref, hid_ref, dg_ref, du_ref, _, top_ref, bottom_ref, both_all):
    step = pl.program_id(0)
    cols = hid_ref.shape[1]

    @pl.when(step == 0)
    def _():
        both_all[:, :cols] = dg_ref[...]
        both_all[:, cols:] = du_ref[...]

    ffn_grads(step, hid_ref, both_all, h2_ref, cot_ref, top_ref, bottom_ref)


def ffn_weights(number, cols, h2_all, cot_all, hidden, d_gate, d_up, token):
    count, width = h2_all.shape
    side = 2 * cols
    side_spec = pl.BlockSpec((count, side), lambda i: (0, i))
    col_spec = pl.BlockSpec((count, cols), lambda i: (0, number), pipeline_mode=pl.Buffered(1))
    piece = (3 * cols // 2, width)
    return pl.pallas_call(
        grads_kernel,
        name="ffn_weights",
        grid=(width // side,),
        in_specs=[side_spec, side_spec, col_spec, col_spec, col_spec, ANYWHERE],
        out_specs=[kept_out(piece)] * 2,
        out_shape=[jax.ShapeDtypeStruct(piece, low)] * 2,
        scratch_shapes=[pltpu.VMEM((count, side), low)],
        compiler_params=params(VMEM_ALONE),
        cost_estimate=SMALL,
    )(h2_all, cot_all, hidden, d_gate, d_up, token)


def is_one_of(place_ref, takers):
    found = place_ref[2] == takers[0]
    for taker in takers[1:]:
        found = found | (place_ref[2] == taker)
    return found


def chosen(takers, place_ref, array_ref, arrived_ref):
    if not takers:
        return array_ref[...].astype(wide)
    return jnp.where(is_one_of(place_ref, takers), arrived_ref[...], array_ref[...]).astype(wide)


def finish_kernel(cols, has_down, takers, place_ref, array_ref, arrived_ref, *refs):
    *_, gate_ref, up_ref, token_ref = refs
    value = chosen(takers, place_ref, array_ref, arrived_ref)
    if has_down:
        refs[-4][...] = value[:cols]
        value = value[cols:]
    for number in range(gate_ref.shape[0]):
        begin = number * 2 * cols
        gate_ref[number] = value[:, begin : begin + cols]
        up_ref[number] = value[:, begin + cols : begin + 2 * cols]
    token_ref[...] = jnp.zeros_like(token_ref)


def finish_ffn(is_top, number, cols, hidden_cols, token, place, takers, array, arrived, grads):
    count, width = array.shape
    squares = width // (2 * cols)
    in_spec = kept_block((count, width))
    square_shape = jax.ShapeDtypeStruct((squares, 2 * cols, hidden_cols), wide)
    if is_top:
        square_spec = pl.BlockSpec((squares, cols // 2, cols), lambda i: (0, 3, number))
    else:
        square_spec = pl.BlockSpec((squares, count, cols), lambda i: (0, 0, number))
    out_specs = [square_spec, square_spec, kept_out((8, 128))]
    out_shape = [square_shape, square_shape, jax.ShapeDtypeStruct((8, 128), wide)]
    names = ["gate", "up"]
    if is_top:
        out_specs.insert(0, pl.BlockSpec((cols, width), lambda i: (number, 0)))
        out_shape.insert(0, jax.ShapeDtypeStruct((hidden_cols, width), wide))
        names.insert(0, "down")
    carried = [(i, grads[name]) for i, name in enumerate(names) if name in grads]
    *buffers, token = pl.pallas_call(
        functools.partial(finish_kernel, cols, is_top, takers),
        name="finish_ffn",
        grid=(1,),
        in_specs=[pl.BlockSpec(memory_space=pltpu.SMEM), in_spec, in_spec, ANYWHERE]
        + [ANYWHERE] * len(carried),
        out_specs=out_specs,
        out_shape=out_shape,
        input_output_aliases={4 + i: target for i, (target, _) in enumerate(carried)},
        compiler_params=params(VMEM_ALONE),
        cost_estimate=SMALL,
    )(place, array, arrived, token, *[buffer for _, buffer in carried])
    grads.update(zip(names, buffers))
    return token


def cut_kernel(takers, place_ref, array_ref, arrived_ref, _, *outs):
    value = chosen(takers, place_ref, array_ref, arrived_ref)
    cols = outs[0].shape[1]
    for number, out in enumerate(outs[:-1]):
        out[...] = value[:, number * cols : (number + 1) * cols]
    outs[-1][...] = jnp.zeros_like(outs[-1])


def finish_cut(pieces, token, place, takers, array, arrived):
    count, width = array.shape
    block = count // 2
    cols = width // pieces
    in_spec = pl.BlockSpec((block, width), lambda i: (i, 0))
    out_spec = pl.BlockSpec((block, cols), lambda i: (i, 0))
    return pl.pallas_call(
        functools.partial(cut_kernel, takers),
        name="finish_cut",
        grid=(2,),
        in_specs=[pl.BlockSpec(memory_space=pltpu.SMEM), in_spec, in_spec, ANYWHERE],
        out_specs=[out_spec] * pieces + [kept_out((8, 128))],
        out_shape=[jax.ShapeDtypeStruct((count, cols), wide)] * pieces
        + [jax.ShapeDtypeStruct((8, 128), wide)],
        compiler_params=params(VMEM_ALONE),
        cost_estimate=SMALL,
    )(place, array, arrived, token)


def tie_kernel(*refs):
    refs[-1][...] = jnp.zeros_like(refs[-1])


def tie(*arrays, estimate=SMALL):
    return pl.pallas_call(
        tie_kernel,
        name="tie",
        in_specs=[ANYWHERE] * len(arrays),
        out_specs=IN_VMEM,
        out_shape=jax.ShapeDtypeStruct((8, 128), wide),
        compiler_params=params(VMEM_ALONE),
        cost_estimate=estimate,
    )(*arrays)


def hold_kernel(*_):
    pass


def hold(array, token, estimate=SMALL):
    return pl.pallas_call(
        hold_kernel,
        name="hold",
        in_specs=[ANYWHERE] * 2,
        out_specs=ANYWHERE,
        out_shape=jax.ShapeDtypeStruct(array.shape, array.dtype),
        input_output_aliases={0: 0},
        compiler_params=params(VMEM_ALONE),
        cost_estimate=estimate,
    )(array, token)


def last_kernel(d_h1_ref, x_ref, d_y1_ref, gain_ref, y1_ref, mlp_ref, _, out_ref, d_gain_ref, layer_ref):
    rows = x_ref[...].astype(wide)
    d_rows, d_gain = norm_back(rows, norm_scale(rows), gain_ref[...], d_h1_ref[...].astype(wide))
    out_ref[...] = d_rows + d_y1_ref[...]
    d_gain_ref[...] = d_gain[None]
    layer_ref[...] = (y1_ref[...] + mlp_ref[...].astype(wide)).astype(low)


def last_rows(token, d_h1, x_own, d_y1, gain, y1_own, mlp_own):
    count, width = d_y1.shape
    return pl.pallas_call(
        last_kernel,
        name="last_rows",
        grid=(1,),
        in_specs=[kept_block((count, width))] * 3
        + [kept_block((1, width))]
        + [kept_block((count, width))] * 2
        + [ANYWHERE],
        out_specs=[kept_block((count, width)), kept_block((1, width)), kept_block((count, width))],
        out_shape=[
            jax.ShapeDtypeStruct((count, width), wide),
            jax.ShapeDtypeStruct((1, width), wide),
            jax.ShapeDtypeStruct((count, width), low),
        ],
        compiler_params=params(VMEM_ALONE),
        cost_estimate=SMALL,
    )(d_h1, x_own, d_y1, gain.reshape(1, width), y1_own, mlp_own, token)


def kept_out(shape):
    return pl.BlockSpec(shape, lambda *_: (0,) * len(shape))


def together(refs):
    return jnp.concatenate([ref[...] for ref in refs], axis=1)


def back_kernel(count, wg_ref, wu_ref, *refs):
    total = dot_rows(together(refs[:count]), wg_ref[...])
    total = total + dot_rows(together(refs[count : 2 * count]), wu_ref[...])
    refs[-1][...] = total.astype(low)


def ffn_back(w_gate, w_up, d_gate, d_up, token):
    count = d_gate[0].shape[0]
    width = w_gate.shape[0]
    block = min(ROW_BLOCK, count)
    parts = [*d_gate, *d_up]
    return pl.pallas_call(
        functools.partial(back_kernel, len(d_gate)),
        name="ffn_back",
        grid=(count // block,),
        in_specs=[kept_block(w_gate.shape), kept_block(w_up.shape)]
        + [pl.BlockSpec((block, part.shape[1]), lambda i: (i, 0)) for part in parts]
        + [ANYWHERE],
        out_specs=pl.BlockSpec((block, width), lambda i: (i, 0)),
        out_shape=jax.ShapeDtypeStruct((count, width), low),
        compiler_params=params(VMEM_ALONE),
        cost_estimate=SMALL,
    )(w_gate, w_up, *parts, token)


def mlp_kernel(w_ref, *refs):
    result = mm(together(refs[:-2]), w_ref[...])
    refs[-1][...] = result.astype(low).reshape(refs[-1].shape)


def ffn_out(own_rows, w_down, hidden, token):
    count = hidden[0].shape[0]
    width = w_down.shape[1]
    devices = max(1, ROW_BLOCK // own_rows)
    block = devices * own_rows
    return pl.pallas_call(
        mlp_kernel,
        name="ffn_out",
        grid=(count // block,),
        in_specs=[kept_block(w_down.shape)]
        + [pl.BlockSpec((block, part.shape[1]), lambda i: (i, 0)) for part in hidden]
        + [ANYWHERE],
        out_specs=pl.BlockSpec((devices, own_rows, width), lambda i: (i, 0, 0)),
        out_shape=jax.ShapeDtypeStruct((count // own_rows, own_rows + DH, width), low),
        compiler_params=params(VMEM_ALONE),
        cost_estimate=SMALL,
    )(w_down, *hidden, token)


def own_kernel(d_h2_ref, y1_ref, cot_ref, gain_ref, w_ref, mixed_ref, *refs):
    d_y1_ref, d_mixed_ref, d_w_ref, d_gain_ref = refs[-4:]
    y1 = y1_ref[...]
    d_rows, d_gain = norm_back(y1, norm_scale(y1), gain_ref[...], d_h2_ref[...].astype(wide))
    d_y1 = d_rows + cot_ref[...].astype(wide)
    d_attn = d_y1.astype(low)
    d_y1_ref[...] = d_y1
    d_gain_ref[...] = d_gain[None]
    d_mixed_ref[...] = dot_rows(d_attn, w_ref[...]).astype(low)
    d_w_ref[...] = dot_cols(mixed_ref[...], d_attn).astype(low).reshape(d_w_ref.shape)


def own_rows_back(token, d_h2, y1_own, cot_own, gain, w_out_all, mixed_own, buffer):
    count, width = y1_own.shape
    inner = w_out_all.shape[0]
    heads = buffer.shape[0]
    once = [d_h2.shape, y1_own.shape, cot_own.shape, (1, width), w_out_all.shape, mixed_own.shape]
    return pl.pallas_call(
        own_kernel,
        name="own_rows_back",
        grid=(1,),
        in_specs=[kept_block(shape) for shape in once] + [ANYWHERE] * 2,
        out_specs=[
            kept_block((count, width)),
            kept_block((count, inner)),
            pl.BlockSpec(
                (heads, DH, width), lambda i: (0, count // DH, 0), pipeline_mode=pl.Buffered(1)
            ),
            kept_block((1, width)),
        ],
        out_shape=[
            jax.ShapeDtypeStruct((count, width), wide),
            jax.ShapeDtypeStruct((count, inner), low),
            jax.ShapeDtypeStruct(buffer.shape, low),
            jax.ShapeDtypeStruct((1, width), wide),
        ],
        input_output_aliases={7: 2},
        compiler_params=params(VMEM_ALONE),
        cost_estimate=SMALL,
    )(d_h2, y1_own, cot_own, gain.reshape(1, width), w_out_all, mixed_own, token, buffer)


def qkv_back_kernel(d_qkv_ref, h1_ref, w_ref, _, d_h1_ref, d_w_ref, total):
    step = pl.program_id(0)
    d_qkv = d_qkv_ref[...]
    d_h1_ref[...] = dot_rows(d_qkv, w_ref[...]).astype(low)
    part = dot_cols(h1_ref[...], d_qkv)

    @pl.when(step == 0)
    def _():
        total[...] = part

    @pl.when(step > 0)
    def _():
        total[...] += part

    @pl.when(step == pl.num_programs(0) - 1)
    def _():
        d_w_ref[...] = total[...].astype(low)


def qkv_back(d_qkv, h1_all, w_qkv, token):
    count, width = h1_all.shape
    cols = w_qkv.shape[1]
    block = min(ROW_BLOCK, count)
    return pl.pallas_call(
        qkv_back_kernel,
        name="qkv_back",
        grid=(count // block,),
        in_specs=[
            pl.BlockSpec((block, cols), lambda i: (i, 0)),
            pl.BlockSpec((block, width), lambda i: (i, 0)),
            kept_block((width, cols)),
            ANYWHERE,
        ],
        out_specs=[pl.BlockSpec((block, width), lambda i: (i, 0)), kept_out((width, cols))],
        out_shape=[
            jax.ShapeDtypeStruct((count, width), low),
            jax.ShapeDtypeStruct((width, cols), low),
        ],
        scratch_shapes=[pltpu.VMEM((width, cols), wide)],
        compiler_params=params(VMEM_ALONE),
        cost_estimate=SMALL,
    )(d_qkv, h1_all, w_qkv, token)


def join_kernel(takers, place_ref, array_ref, arrived_ref, _, out_ref):
    array, arrived = array_ref[...], arrived_ref[...]
    if takers:
        out_ref[...] = jnp.where(is_one_of(place_ref, takers), arrived, array)
    else:
        out_ref[...] = array + arrived


def join(token, place, takers, array, arrived):
    count, width = array.shape
    block = count // 2
    spec = pl.BlockSpec((block, width), lambda i: (i, 0))
    return pl.pallas_call(
        functools.partial(join_kernel, takers),
        name="join",
        grid=(count // block,),
        in_specs=[pl.BlockSpec(memory_space=pltpu.SMEM), spec, spec, ANYWHERE],
        out_specs=spec,
        out_shape=jax.ShapeDtypeStruct((count, width), low),
        compiler_params=params(VMEM_ALONE),
        cost_estimate=SMALL,
    )(place, array, arrived, token)


def butterfly(array, axis, size):
    if size & (size - 1):
        return lax.psum(array, axis)
    step = 1
    while step < size:
        array = array + lax.ppermute(array, axis, [(i, i ^ step) for i in range(size)])
        step *= 2
    return array


class Chain:
    def __init__(self, axis, size, place, token):
        self.axis, self.size, self.place, self.token = axis, size, place, token
        half = size // 2
        self.stages = [("in", [(s - 1, s), (size - s, size - 1 - s)]) for s in range(1, half)]
        self.stages.append(("in", [(half - 1, half), (half, half - 1)]))
        self.stages += [("out", [(s, s - 1), (size - 1 - s, size - s)]) for s in range(half - 1, 0, -1)]
        self.waiting = []
        self.moving = [[] for _ in self.stages]

    def push(self, array, land):
        self.waiting.append((land, array))

    def send(self, stage, land, array):
        arrived = lax.ppermute(array, self.axis, self.stages[stage][1])
        self.moving[stage].append((land, array, arrived))

    def move(self, stage):
        land, array, arrived = self.moving[stage].pop(0)
        kind, pairs = self.stages[stage]
        takers = tuple(target for _, target in pairs) if kind == "out" else ()
        last = stage + 1 == len(self.stages)
        if kind == "in" or not last:
            array = join(self.token, self.place, takers, array, arrived)
            arrived, takers = array, ()
            self.token = array
        if last:
            self.token = land(self.token, self.place, takers, array, arrived)
        else:
            self.send(stage + 1, land, array)

    def tick(self, between=None):
        if self.size == 1 or self.size % 2:
            for land, array in self.waiting:
                array = lax.psum(array, self.axis)
                self.token = land(self.token, self.place, (), array, array)
            self.waiting = []
            return between() if between else None
        result = None
        ready = [bool(moving) for moving in self.moving]
        if self.waiting:
            land, array = self.waiting.pop(0)
            array = self.token = hold(array, self.token)
            self.send(0, land, array)
        for stage, can_move in enumerate(ready):
            if can_move:
                self.move(stage)
            if stage == max(len(ready) - 2, 0) and between:
                result = between()
        return result

    def drain(self):
        while self.waiting or any(self.moving):
            self.tick()


def assemble_kernel(place_ref, *refs):
    *pieces, out_ref = refs
    rows = pieces[0].shape[0]
    for number, piece in enumerate(pieces):
        begin = pl.multiple_of((place_ref[1] ^ number) * rows, rows)
        out_ref[pl.ds(begin, rows)] = piece[...]


def assemble(place, pieces):
    count = len(pieces)
    rows, cols = pieces[0].shape
    return pl.pallas_call(
        assemble_kernel,
        name="assemble",
        in_specs=[pl.BlockSpec(memory_space=pltpu.SMEM)]
        + [pl.BlockSpec(memory_space=pltpu.VMEM)] * count,
        out_specs=pl.BlockSpec(memory_space=pltpu.VMEM),
        out_shape=jax.ShapeDtypeStruct((count * rows, cols), pieces[0].dtype),
        compiler_params=params(24),
        cost_estimate=SMALL,
    )(place, *pieces)


def gather_pieces(array, axis, size):
    if size != 8:
        gathered = lax.all_gather(array, axis, axis=0)
        return [gathered[i] for i in range(size)]

    def flip(value, bits):
        return lax.ppermute(value, axis, [(i, i ^ bits) for i in range(size)])

    half = array.shape[0] // 2
    side_a, side_b = flip(array, 2), flip(array, 4)
    far_a, far_b = flip(side_a[:half], 4), flip(side_b[half:], 2)
    mine = [array, side_a, side_b, jnp.concatenate([far_a, far_b], axis=0)]
    pieces = []
    for piece in mine:
        pieces += [piece, flip(piece, 1)]
    return pieces


def per_device(
    tokens,
    cotangent,
    doc_lengths,
    pad_mask,
    w_query,
    w_key,
    w_value,
    w_out,
    w_gate,
    w_up,
    w_down,
    norm_attn,
    norm_mlp,
    mix_gate,
    *,
    n_heads,
    n_batch,
):
    width = tokens.shape[-1]
    rows = tokens.shape[2]
    own_rows = MICRO * rows
    here = lax.axis_index("heads")

    def gather(array):
        return lax.all_gather(array, "heads", axis=0, tiled=True)

    def scatter(array):
        return lax.psum_scatter(array, "heads", scatter_dimension=0, tiled=True)

    def grouped(array):
        return array.reshape(n_heads, MICRO, rows, array.shape[-1])

    def flat(array):
        return array.reshape(n_heads * own_rows, array.shape[-1])

    w_qkv = jnp.concatenate([w_query, w_key, w_value], axis=1)
    share = jax.nn.sigmoid(mix_gate)
    positions = jnp.arange(LEN, dtype=jnp.int32)
    doc_ends = jnp.cumsum(doc_lengths[:, 0], axis=1)
    doc_ids = jnp.sum((positions[None, :, None] >= doc_ends[:, None, :]).astype(jnp.int32), axis=2)
    doc_rows = doc_ids[:, :, None]
    doc_cols = jnp.where(pad_mask[:, 0] == 1, doc_ids, -1)[:, None, :]

    tok_own = tokens.reshape(own_rows, width)
    cot_own = cotangent.reshape(own_rows, width)
    place = jnp.stack(
        [here, here if n_heads == 8 else jnp.zeros_like(here), lax.axis_index("batch")]
    )
    tok_all = gather(tok_own)
    w_out_all = assemble(place, gather_pieces(w_out, "heads", n_heads))
    tok_all, w_out_all = lax.optimization_barrier((tok_all, w_out_all))
    cot_all = gather(lax.optimization_barrier((cot_own, tok_all))[0])
    h1_all, qkv = qkv_rows(tok_all, norm_attn, w_qkv)
    qkv = grouped(qkv)
    mixed = flat(head_forward(share, qkv, doc_rows, doc_cols))
    mixed_pieces = gather_pieces(mixed, "heads", n_heads)
    h2_all, y1_own, mixed_own = mid_rows(place, tok_all, mixed_pieces, w_out_all, norm_mlp)

    chain = Chain("batch", n_batch, place, norm_mlp)
    hidden_cols = w_gate.shape[1]
    cols = hidden_cols // FFN_CHUNKS
    grads = {}

    def push_ffn(number, top, bottom):
        for is_top, part in ((True, top), (False, bottom)):
            chain.push(
                part,
                lambda *moved, is_top=is_top: finish_ffn(
                    is_top, number, cols, hidden_cols, *moved, grads
                ),
            )

    def land_qkv(*moved):
        *grads["qkv"], token = finish_cut(3, *moved)
        return token

    def land_out(*moved):
        grads["out"], token = finish_cut(1, *moved)
        return token

    def first(number):
        *parts, top, bottom = ffn_first(
            number, cols, h2_all, cot_all, w_gate, w_up, w_down, chain.token
        )
        chain.token = parts[0]
        push_ffn(number, top, bottom)
        return parts

    def rest(number):
        results = ffn_rest(number, cols, h2_all, cot_all, w_gate, w_up, w_down, chain.token)
        chain.token = results[0]
        return results

    def weights(number, parts):
        top, bottom = ffn_weights(0, cols, h2_all, cot_all, *parts, chain.token)
        chain.token = bottom
        push_ffn(number, top, bottom)

    def wait_for(microseconds):
        chain.token = tie(chain.token, estimate=busy(microseconds))

    part_a = first(0)
    chain.tick()
    part_b = first(1)
    part_c = rest(2)
    chain.tick()
    part_d = rest(3)
    weights(2, part_c)
    chain.tick()
    hidden, d_gate, d_up = zip(part_a, part_b, part_c, part_d)
    d_h2 = chain.token = ffn_back(w_gate, w_up, d_gate, d_up, chain.token)
    d_h2 = scatter(d_h2)
    chain.tick()
    parts = chain.token = ffn_out(own_rows, w_down, hidden, chain.token)
    chain.tick()
    weights(3, part_d)
    chain.tick()
    wait_for(WAITS[0])
    d_y1, d_mixed_own, parts, gain_mlp_part = own_rows_back(
        chain.token, d_h2, y1_own, cot_own, norm_mlp, w_out_all, mixed_own, parts
    )
    chain.token = d_y1
    d_mixed = lax.all_to_all(d_mixed_own, "heads", split_axis=1, concat_axis=0, tiled=True)
    parts = scatter(parts.reshape(-1, width))
    chain.tick()
    wait_for(WAITS[2])
    d_qkv, d_share = head_backward(
        share, qkv, grouped(d_mixed), doc_rows, doc_cols, chain.token
    )
    chain.token = d_share
    chain.tick()
    d_h1, grad_qkv = qkv_back(flat(d_qkv), h1_all, w_qkv, chain.token)
    chain.token = d_h1
    chain.push(grad_qkv, land_qkv)

    def scatter_last():
        wait_for(WAITS[3])
        chain.token = tie(chain.token, parts)
        chain.token = hold(d_h1, chain.token)
        return scatter(chain.token)

    d_h1 = chain.tick(scatter_last)
    chain.push(parts[own_rows:], land_out)
    chain.tick()
    chain.tick()

    wait_for(WAITS[1])
    grad_tokens, gain_attn_part, layer_out = last_rows(
        chain.token, d_h1, tok_own, d_y1, norm_attn, y1_own, parts
    )
    grad_tokens = grad_tokens.reshape(tokens.shape)
    chain.token = gain_attn_part
    slots = jnp.where(jnp.arange(n_heads) == here, jnp.sum(d_share[:, 0, 0]), 0.0)
    sums = jnp.concatenate([gain_attn_part[0], gain_mlp_part[0], slots])
    sums = butterfly(butterfly(sums, "heads", n_heads), "batch", n_batch)
    grad_mix = lax.dynamic_slice_in_dim(sums, 2 * width + here, 1, 0)
    chain.drain()

    return (
        layer_out.reshape(tokens.shape),
        grad_tokens,
        *grads["qkv"],
        grads["out"],
        grads["gate"].reshape(w_gate.shape),
        grads["up"].reshape(w_up.shape),
        grads["down"],
        sums[:width],
        sums[width : 2 * width],
        grad_mix,
    )


def solution(mesh):
    in_specs = (
        P(None, "batch", "heads", None),
        P(None, "batch", "heads", None),
        P(None, "batch", None),
        P(None, "batch", None),
        P(None, "heads"),
        P(None, "heads"),
        P(None, "heads"),
        P("heads", None),
        P(None, "heads"),
        P(None, "heads"),
        P("heads", None),
        P(),
        P(),
        P("heads"),
    )
    out_specs = (
        P(None, "batch", "heads", None),
        P(None, "batch", "heads", None),
        P(None, "heads"),
        P(None, "heads"),
        P(None, "heads"),
        P("heads", None),
        P(None, "heads"),
        P(None, "heads"),
        P("heads", None),
        P(),
        P(),
        P("heads"),
    )

    def program(*arrays):
        return per_device(*arrays, n_heads=mesh.shape["heads"], n_batch=mesh.shape["batch"])

    return jax.shard_map(
        program, mesh=mesh, in_specs=in_specs, out_specs=out_specs, check_vma=False
    )
```

```python
import functools

import jax
import jax.numpy as jnp
from jax import lax
from jax.experimental import pallas as pl
from jax.experimental.pallas import tpu as pltpu
from jax.sharding import PartitionSpec as P

DH = 128
SEG = 512
SEGS = 2
LEN = 1024
MICRO = 2
FFN_CHUNKS = 4
WAITS = (102, 108, 5, 172)
ROW_BLOCK = 512
MIB = 1 << 20
VMEM_ALONE = 60
IN_VMEM = pl.BlockSpec(memory_space=pltpu.VMEM)
ANYWHERE = pl.BlockSpec(memory_space=pl.ANY)
SMALL = pl.CostEstimate(flops=1, bytes_accessed=1, transcendentals=0)
def busy(microseconds):
    return pl.CostEstimate(flops=int(microseconds * 10**9), bytes_accessed=1, transcendentals=0)


epsilon = 1e-05
big_negative = -1e30
low = jnp.bfloat16
wide = jnp.float32


def mm(left_mat, right_mat):
    return jnp.dot(left_mat, right_mat, preferred_element_type=wide)


def dot_rows(left_mat, right_mat):
    return lax.dot_general(
        left_mat, right_mat, (((1,), (1,)), ((), ())), preferred_element_type=wide
    )


def dot_cols(left_mat, right_mat):
    return lax.dot_general(
        left_mat, right_mat, (((0,), (0,)), ((), ())), preferred_element_type=wide
    )


def norm_scale(row_block):
    return lax.rsqrt(jnp.mean(row_block * row_block, axis=-1, keepdims=True) + epsilon)


def norm_back(row_block, row_scale, gain_vec, upstream):
    shaped = upstream * gain_vec
    inner = jnp.mean(shaped * row_block, axis=-1, keepdims=True)
    d_rows = row_scale * shaped - row_block * row_scale * row_scale * row_scale * inner
    d_gain = jnp.sum(upstream * row_block * row_scale, axis=0)
    return (d_rows, d_gain)


def positive(values_in):
    return jnp.where(values_in > 0, values_in + 1.0, jnp.exp(values_in))


def positive_slope(values_in):
    return jnp.where(values_in > 0, 1.0, jnp.exp(values_in))


def params(mebibytes):
    return pltpu.CompilerParams(vmem_limit_bytes=mebibytes * MIB)


def kept_block(shape):
    return pl.BlockSpec(shape, lambda *_: (0,) * len(shape), pipeline_mode=pl.Buffered(1))


def qkv_kernel(x_ref, gain_ref, w_ref, h1_ref, qkv_ref):
    rows = x_ref[...].astype(wide)
    h1 = (rows * norm_scale(rows) * gain_ref[...]).astype(low)
    h1_ref[...] = h1
    qkv_ref[...] = mm(h1, w_ref[...]).astype(low)


def qkv_rows(x_all, gain, w_qkv):
    count, width = x_all.shape
    cols = w_qkv.shape[1]
    block = min(ROW_BLOCK, count)
    return pl.pallas_call(
        qkv_kernel,
        name="qkv_rows",
        grid=(count // block,),
        in_specs=[
            pl.BlockSpec((block, width), lambda i: (i, 0)),
            kept_block((1, width)),
            kept_block((width, cols)),
        ],
        out_specs=[
            pl.BlockSpec((block, width), lambda i: (i, 0)),
            pl.BlockSpec((block, cols), lambda i: (i, 0)),
        ],
        out_shape=[
            jax.ShapeDtypeStruct((count, width), low),
            jax.ShapeDtypeStruct((count, cols), low),
        ],
        compiler_params=params(VMEM_ALONE),
        cost_estimate=SMALL,
    )(x_all, gain.reshape(1, width), w_qkv)


def seg_of(array, segment):
    return array[segment * SEG : (segment + 1) * SEG]


def local_probs(query_seg, key_seg, doc_rows, doc_cols):
    row_ids = lax.broadcasted_iota(jnp.int32, (SEG, SEG), 0)
    col_ids = lax.broadcasted_iota(jnp.int32, (SEG, SEG), 1)
    allowed = ((doc_rows == doc_cols) & (col_ids <= row_ids)) | (col_ids == row_ids)
    scores = jnp.where(allowed, dot_rows(query_seg, key_seg) * DH ** (-0.5), big_negative)
    shifted = jnp.exp(scores - jnp.max(scores, axis=1, keepdims=True))
    return shifted * (1.0 / jnp.sum(shifted, axis=1, keepdims=True))


def head_kernel(share_ref, qkv_ref, doc_rows_ref, doc_cols_ref, mixed_ref):
    share = share_ref[0]
    qkv = qkv_ref[...].reshape(LEN, 3 * DH)
    query, key, value = [qkv[:, i * DH : (i + 1) * DH] for i in range(3)]
    parts = []
    for segment in range(SEGS):
        begin = segment * SEG
        query_seg = seg_of(query, segment)
        doc_rows = doc_rows_ref[begin : begin + SEG]
        probs = local_probs(
            query_seg, seg_of(key, segment), doc_rows, doc_cols_ref[:, begin : begin + SEG]
        )
        result = (1.0 - share) * mm(probs.astype(low), seg_of(value, segment))
        if segment > 0:
            allowed = doc_rows == doc_cols_ref[:, :begin]
            pos_query = positive(query_seg.astype(wide)).astype(low)
            pos_key = positive(key[:begin].astype(wide)).astype(low)
            weights = jnp.where(allowed, dot_rows(pos_query, pos_key), 0.0)
            den = jnp.maximum(jnp.sum(weights, axis=1, keepdims=True), 1.0)
            result = result + share * (mm(weights.astype(low), value[:begin]) / den)
        parts.append(result.astype(low))
    mixed_ref[...] = jnp.concatenate(parts, axis=0).reshape(mixed_ref.shape)


def micro_spec(n_heads, rows, cols):
    return pl.BlockSpec((n_heads, None, rows, cols), lambda m: (0, m, 0, 0))


def doc_specs():
    return [
        pl.BlockSpec((None, LEN, 1), lambda m: (m, 0, 0)),
        pl.BlockSpec((None, 1, LEN), lambda m: (m, 0, 0)),
    ]


def head_forward(share, qkv, doc_rows, doc_cols):
    n_heads, micro, rows, cols = qkv.shape
    pairs = micro * LEN * SEG * 2
    return pl.pallas_call(
        head_kernel,
        name="head_forward",
        grid=(micro,),
        in_specs=[pl.BlockSpec(memory_space=pltpu.SMEM), micro_spec(n_heads, rows, cols), *doc_specs()],
        out_specs=micro_spec(n_heads, rows, DH),
        out_shape=jax.ShapeDtypeStruct((n_heads, micro, rows, DH), low),
        compiler_params=params(VMEM_ALONE),
        cost_estimate=SMALL,
    )(share, qkv, doc_rows, doc_cols)


def head_back_kernel(
    share_ref, qkv_ref, d_mixed_ref, doc_rows_ref, doc_cols_ref, _, d_qkv_ref, d_share_ref
):
    share = share_ref[0]
    scale = DH ** (-0.5)
    qkv = qkv_ref[...].reshape(LEN, 3 * DH)
    query, key, value = [qkv[:, i * DH : (i + 1) * DH] for i in range(3)]
    d_mixed = d_mixed_ref[...].reshape(LEN, DH).astype(wide)
    d_query, d_key, d_value = [[None] * SEGS for _ in range(3)]
    d_share = jnp.zeros((1, 1), wide)
    for segment in range(SEGS):
        begin = segment * SEG
        query_seg, key_seg, value_seg = [seg_of(a, segment) for a in (query, key, value)]
        doc_rows = doc_rows_ref[begin : begin + SEG]
        probs = local_probs(query_seg, key_seg, doc_rows, doc_cols_ref[:, begin : begin + SEG])
        probs_low = probs.astype(low)
        d_mixed_seg = seg_of(d_mixed, segment)
        d_dotted = ((1.0 - share) * d_mixed_seg).astype(low)
        gap = -mm(probs_low, value_seg)
        d_probs = dot_rows(d_dotted, value_seg)
        d_scores = (
            probs * (d_probs - jnp.sum(probs * d_probs, axis=1, keepdims=True))
        ).astype(low)
        d_value[segment] = dot_cols(probs_low, d_dotted)
        d_query[segment] = mm(d_scores, key_seg) * scale
        d_key[segment] = dot_cols(d_scores, query_seg) * scale
        if segment > 0:
            allowed = doc_rows == doc_cols_ref[:, :begin]
            query_float = query_seg.astype(wide)
            key_float = key[:begin].astype(wide)
            pos_query = positive(query_float).astype(low)
            pos_key = positive(key_float).astype(low)
            weights = jnp.where(allowed, dot_rows(pos_query, pos_key), 0.0)
            row_total = jnp.sum(weights, axis=1, keepdims=True)
            inverse = 1.0 / jnp.maximum(row_total, 1.0)
            weights_low = weights.astype(low)
            numerator = mm(weights_low, value[:begin])
            gap = gap + numerator * inverse
            d_recalled = share * d_mixed_seg
            d_numer = (d_recalled * inverse).astype(low)
            d_denom = jnp.where(
                row_total > 1.0,
                -jnp.sum(d_recalled * numerator, axis=1, keepdims=True) * inverse * inverse,
                0.0,
            )
            d_weights = jnp.where(
                allowed, dot_rows(d_numer, value[:begin]) + d_denom, 0.0
            ).astype(low)
            d_query[segment] += mm(d_weights, pos_key) * positive_slope(query_float)
            d_pos_key = dot_cols(d_weights, pos_query) * positive_slope(key_float)
            d_value_before = dot_cols(weights_low, d_numer)
            for earlier in range(segment):
                d_key[earlier] += seg_of(d_pos_key, earlier)
                d_value[earlier] += seg_of(d_value_before, earlier)
        d_share = d_share + jnp.sum(
            jnp.sum(d_mixed_seg * gap, axis=1, keepdims=True), axis=0, keepdims=True
        )
    whole = jnp.concatenate(
        [jnp.concatenate(parts, axis=0).astype(low) for parts in (d_query, d_key, d_value)], axis=1
    )
    d_qkv_ref[...] = whole.reshape(d_qkv_ref.shape)
    d_share_ref[...] = jnp.broadcast_to(d_share * (share * (1.0 - share)), d_share_ref.shape)


def head_backward(share, qkv, d_mixed, doc_rows, doc_cols, token):
    n_heads, micro, rows, cols = qkv.shape
    pairs = micro * LEN * SEG * 2
    return pl.pallas_call(
        head_back_kernel,
        name="head_backward",
        grid=(micro,),
        in_specs=[
            pl.BlockSpec(memory_space=pltpu.SMEM),
            micro_spec(n_heads, rows, cols),
            micro_spec(n_heads, rows, DH),
            *doc_specs(),
            ANYWHERE,
        ],
        out_specs=[
            micro_spec(n_heads, rows, cols),
            pl.BlockSpec((None, 8, 128), lambda m: (m, 0, 0)),
        ],
        out_shape=[
            jax.ShapeDtypeStruct((n_heads, micro, rows, cols), low),
            jax.ShapeDtypeStruct((micro, 8, 128), wide),
        ],
        compiler_params=params(VMEM_ALONE),
        cost_estimate=SMALL,
    )(share, qkv, d_mixed, doc_rows, doc_cols, token)


def mid_kernel(heads, place_ref, x_ref, *refs):
    mixed_refs = refs[:heads]
    w_ref, gain_ref, h2_ref, y1_ref, mixed_own_ref, w_near = refs[heads:]
    step = pl.program_id(0)
    own_rows = y1_ref.shape[0]
    devices = x_ref.shape[0] // own_rows

    def owner(number):
        return pl.multiple_of((place_ref[1] ^ number) * DH, DH)

    @pl.when(step == 0)
    def _():
        for number in range(heads):
            w_near[number * DH : (number + 1) * DH] = w_ref[pl.ds(owner(number), DH)]

    mixed = jnp.concatenate([ref[...] for ref in mixed_refs], axis=1)
    y1 = x_ref[...].astype(wide) + mm(mixed, w_near[...])
    h2_ref[...] = (y1 * norm_scale(y1) * gain_ref[...]).astype(low)
    for device in range(devices):
        begin = device * own_rows

        @pl.when(step * devices + device == place_ref[0])
        def _():
            y1_ref[...] = y1[begin : begin + own_rows]
            for number in range(heads):
                mixed_own_ref[:, pl.ds(owner(number), DH)] = mixed_refs[number][
                    begin : begin + own_rows
                ]


def mid_rows(place, x_all, mixed_pieces, w_out_all, gain):
    count, width = x_all.shape
    heads = len(mixed_pieces)
    inner = w_out_all.shape[0]
    own_rows = count // heads
    block = max(1, ROW_BLOCK // own_rows) * own_rows
    return pl.pallas_call(
        functools.partial(mid_kernel, heads),
        name="mid_rows",
        grid_spec=pltpu.PrefetchScalarGridSpec(
            num_scalar_prefetch=1,
            grid=(count // block,),
            in_specs=[
                pl.BlockSpec((block, width), lambda i, _: (i, 0)),
                *[pl.BlockSpec((block, DH), lambda i, _: (i, 0))] * heads,
                kept_block((inner, width)),
                kept_block((1, width)),
            ],
            out_specs=[
                pl.BlockSpec((block, width), lambda i, _: (i, 0)),
                pl.BlockSpec((own_rows, width), lambda i, _: (0, 0)),
                pl.BlockSpec((own_rows, inner), lambda i, _: (0, 0)),
            ],
            scratch_shapes=[pltpu.VMEM((inner, width), low)],
        ),
        out_shape=[
            jax.ShapeDtypeStruct((count, width), low),
            jax.ShapeDtypeStruct((own_rows, width), wide),
            jax.ShapeDtypeStruct((own_rows, inner), low),
        ],
        compiler_params=params(VMEM_ALONE),
        cost_estimate=SMALL,
    )(place, x_all, *mixed_pieces, w_out_all, gain.reshape(1, width))


def ffn_rows(h2_ref, cot_ref, w_gate, w_up, w_down):
    h2 = h2_ref[...]
    gate = mm(h2, w_gate)
    up = mm(h2, w_up)
    d_hidden = dot_rows(cot_ref[...], w_down)
    sig = jax.nn.sigmoid(gate)
    act = gate * sig
    hidden = (act * up).astype(low)
    d_up = (d_hidden * act).astype(low)
    d_gate = (d_hidden * up * sig * (1.0 + gate * (1.0 - sig))).astype(low)
    return hidden, d_gate, d_up


def ffn_grads(step, hidden, d_both, h2_ref, cot_ref, top_ref, bottom_ref):
    cols = hidden.shape[1]
    side = 2 * cols
    half = cols // 2
    span = pl.ds(pl.multiple_of(step * side, side), side)
    top_ref[:cols, span] = dot_cols(hidden[...], cot_ref[...]).astype(low)
    square = dot_cols(h2_ref[...], d_both[...]).astype(low)
    top_ref[cols:, span] = square[3 * half :]
    bottom_ref[:, span] = square[: 3 * half]


def first_kernel(
    blocks, h2_ref, cot_ref, h2_col_ref, cot_col_ref, wg_ref, wu_ref, wd_ref, _, *refs
):
    hid_ref, dg_ref, du_ref, top_ref, bottom_ref, hid_all, both_all = refs
    step = pl.program_id(0)
    block, cols = hid_ref.shape

    @pl.when(step < blocks)
    def _():
        rows = pl.ds(pl.multiple_of(step * block, block), block)
        hidden, d_gate, d_up = ffn_rows(h2_ref, cot_ref, wg_ref[...], wu_ref[...], wd_ref[...])
        hid_ref[...] = hid_all[rows] = hidden
        dg_ref[...] = both_all[rows, :cols] = d_gate
        du_ref[...] = both_all[rows, cols:] = d_up

    @pl.when(step >= blocks)
    def _():
        ffn_grads(step - blocks, hid_all, both_all, h2_col_ref, cot_col_ref, top_ref, bottom_ref)


def ffn_first(number, cols, h2_all, cot_all, w_gate, w_up, w_down, token):
    count, width = h2_all.shape
    block = min(ROW_BLOCK, count // 2)
    blocks = count // block
    side = 2 * cols
    row_spec = pl.BlockSpec((block, width), lambda i: (jnp.minimum(i, blocks - 1), 0))
    side_spec = pl.BlockSpec((count, side), lambda i: (0, jnp.maximum(i - blocks, 0)))
    col_spec = pl.BlockSpec((width, cols), lambda i: (0, number), pipeline_mode=pl.Buffered(1))
    down_spec = pl.BlockSpec((cols, width), lambda i: (number, 0), pipeline_mode=pl.Buffered(1))
    out_spec = pl.BlockSpec((block, cols), lambda i: (jnp.minimum(i, blocks - 1), 0))
    piece = (3 * cols // 2, width)
    return pl.pallas_call(
        functools.partial(first_kernel, blocks),
        name="ffn_first",
        grid=(blocks + width // side,),
        in_specs=[row_spec, row_spec, side_spec, side_spec, col_spec, col_spec, down_spec, ANYWHERE],
        out_specs=[out_spec] * 3 + [kept_out(piece)] * 2,
        out_shape=[jax.ShapeDtypeStruct((count, cols), low)] * 3
        + [jax.ShapeDtypeStruct(piece, low)] * 2,
        scratch_shapes=[pltpu.VMEM((count, cols), low), pltpu.VMEM((count, side), low)],
        compiler_params=params(VMEM_ALONE),
        cost_estimate=SMALL,
    )(h2_all, cot_all, h2_all, cot_all, w_gate, w_up, w_down, token)


def rest_kernel(h2_ref, cot_ref, wg_ref, wu_ref, wd_ref, _, *refs):
    results = ffn_rows(h2_ref, cot_ref, wg_ref[...], wu_ref[...], wd_ref[...])
    for ref, result in zip(refs, results):
        ref[...] = result


def ffn_rest(number, cols, h2_all, cot_all, w_gate, w_up, w_down, token):
    count, width = h2_all.shape
    block = min(ROW_BLOCK, count // 2)
    row_spec = pl.BlockSpec((block, width), lambda i: (i, 0))
    col_spec = pl.BlockSpec((width, cols), lambda i: (0, number), pipeline_mode=pl.Buffered(1))
    down_spec = pl.BlockSpec((cols, width), lambda i: (number, 0), pipeline_mode=pl.Buffered(1))
    return pl.pallas_call(
        rest_kernel,
        name="ffn_rest",
        grid=(count // block,),
        in_specs=[row_spec, row_spec, col_spec, col_spec, down_spec, ANYWHERE],
        out_specs=[pl.BlockSpec((block, cols), lambda i: (i, 0))] * 3,
        out_shape=[jax.ShapeDtypeStruct((count, cols), low)] * 3,
        compiler_params=params(VMEM_ALONE),
        cost_estimate=SMALL,
    )(h2_all, cot_all, w_gate, w_up, w_down, token)


def grads_kernel(h2_ref, cot_ref, hid_ref, dg_ref, du_ref, _, top_ref, bottom_ref, both_all):
    step = pl.program_id(0)
    cols = hid_ref.shape[1]

    @pl.when(step == 0)
    def _():
        both_all[:, :cols] = dg_ref[...]
        both_all[:, cols:] = du_ref[...]

    ffn_grads(step, hid_ref, both_all, h2_ref, cot_ref, top_ref, bottom_ref)


def ffn_weights(number, cols, h2_all, cot_all, hidden, d_gate, d_up, token):
    count, width = h2_all.shape
    side = 2 * cols
    side_spec = pl.BlockSpec((count, side), lambda i: (0, i))
    col_spec = pl.BlockSpec((count, cols), lambda i: (0, number), pipeline_mode=pl.Buffered(1))
    piece = (3 * cols // 2, width)
    return pl.pallas_call(
        grads_kernel,
        name="ffn_weights",
        grid=(width // side,),
        in_specs=[side_spec, side_spec, col_spec, col_spec, col_spec, ANYWHERE],
        out_specs=[kept_out(piece)] * 2,
        out_shape=[jax.ShapeDtypeStruct(piece, low)] * 2,
        scratch_shapes=[pltpu.VMEM((count, side), low)],
        compiler_params=params(VMEM_ALONE),
        cost_estimate=SMALL,
    )(h2_all, cot_all, hidden, d_gate, d_up, token)


def is_one_of(place_ref, takers):
    found = place_ref[2] == takers[0]
    for taker in takers[1:]:
        found = found | (place_ref[2] == taker)
    return found


def chosen(takers, place_ref, array_ref, arrived_ref):
    if not takers:
        return array_ref[...].astype(wide)
    return jnp.where(is_one_of(place_ref, takers), arrived_ref[...], array_ref[...]).astype(wide)


def finish_kernel(cols, has_down, takers, place_ref, array_ref, arrived_ref, *refs):
    *_, gate_ref, up_ref, token_ref = refs
    value = chosen(takers, place_ref, array_ref, arrived_ref)
    if has_down:
        refs[-4][...] = value[:cols]
        value = value[cols:]
    for number in range(gate_ref.shape[0]):
        begin = number * 2 * cols
        gate_ref[number] = value[:, begin : begin + cols]
        up_ref[number] = value[:, begin + cols : begin + 2 * cols]
    token_ref[...] = jnp.zeros_like(token_ref)


def finish_ffn(is_top, number, cols, hidden_cols, token, place, takers, array, arrived, grads):
    count, width = array.shape
    squares = width // (2 * cols)
    in_spec = kept_block((count, width))
    square_shape = jax.ShapeDtypeStruct((squares, 2 * cols, hidden_cols), wide)
    if is_top:
        square_spec = pl.BlockSpec((squares, cols // 2, cols), lambda i: (0, 3, number))
    else:
        square_spec = pl.BlockSpec((squares, count, cols), lambda i: (0, 0, number))
    out_specs = [square_spec, square_spec, kept_out((8, 128))]
    out_shape = [square_shape, square_shape, jax.ShapeDtypeStruct((8, 128), wide)]
    names = ["gate", "up"]
    if is_top:
        out_specs.insert(0, pl.BlockSpec((cols, width), lambda i: (number, 0)))
        out_shape.insert(0, jax.ShapeDtypeStruct((hidden_cols, width), wide))
        names.insert(0, "down")
    carried = [(i, grads[name]) for i, name in enumerate(names) if name in grads]
    *buffers, token = pl.pallas_call(
        functools.partial(finish_kernel, cols, is_top, takers),
        name="finish_ffn",
        grid=(1,),
        in_specs=[pl.BlockSpec(memory_space=pltpu.SMEM), in_spec, in_spec, ANYWHERE]
        + [ANYWHERE] * len(carried),
        out_specs=out_specs,
        out_shape=out_shape,
        input_output_aliases={4 + i: target for i, (target, _) in enumerate(carried)},
        compiler_params=params(VMEM_ALONE),
        cost_estimate=SMALL,
    )(place, array, arrived, token, *[buffer for _, buffer in carried])
    grads.update(zip(names, buffers))
    return token


def cut_kernel(takers, place_ref, array_ref, arrived_ref, _, *outs):
    value = chosen(takers, place_ref, array_ref, arrived_ref)
    cols = outs[0].shape[1]
    for number, out in enumerate(outs[:-1]):
        out[...] = value[:, number * cols : (number + 1) * cols]
    outs[-1][...] = jnp.zeros_like(outs[-1])


def finish_cut(pieces, token, place, takers, array, arrived):
    count, width = array.shape
    block = count // 2
    cols = width // pieces
    in_spec = pl.BlockSpec((block, width), lambda i: (i, 0))
    out_spec = pl.BlockSpec((block, cols), lambda i: (i, 0))
    return pl.pallas_call(
        functools.partial(cut_kernel, takers),
        name="finish_cut",
        grid=(2,),
        in_specs=[pl.BlockSpec(memory_space=pltpu.SMEM), in_spec, in_spec, ANYWHERE],
        out_specs=[out_spec] * pieces + [kept_out((8, 128))],
        out_shape=[jax.ShapeDtypeStruct((count, cols), wide)] * pieces
        + [jax.ShapeDtypeStruct((8, 128), wide)],
        compiler_params=params(VMEM_ALONE),
        cost_estimate=SMALL,
    )(place, array, arrived, token)


def tie_kernel(*refs):
    refs[-1][...] = jnp.zeros_like(refs[-1])


def tie(*arrays, estimate=SMALL):
    return pl.pallas_call(
        tie_kernel,
        name="tie",
        in_specs=[ANYWHERE] * len(arrays),
        out_specs=IN_VMEM,
        out_shape=jax.ShapeDtypeStruct((8, 128), wide),
        compiler_params=params(VMEM_ALONE),
        cost_estimate=estimate,
    )(*arrays)


def hold_kernel(*_):
    pass


def hold(array, token, estimate=SMALL):
    return pl.pallas_call(
        hold_kernel,
        name="hold",
        in_specs=[ANYWHERE] * 2,
        out_specs=ANYWHERE,
        out_shape=jax.ShapeDtypeStruct(array.shape, array.dtype),
        input_output_aliases={0: 0},
        compiler_params=params(VMEM_ALONE),
        cost_estimate=estimate,
    )(array, token)


def last_kernel(d_h1_ref, x_ref, d_y1_ref, gain_ref, y1_ref, mlp_ref, _, out_ref, d_gain_ref, layer_ref):
    rows = x_ref[...].astype(wide)
    d_rows, d_gain = norm_back(rows, norm_scale(rows), gain_ref[...], d_h1_ref[...].astype(wide))
    out_ref[...] = d_rows + d_y1_ref[...]
    d_gain_ref[...] = d_gain[None]
    layer_ref[...] = (y1_ref[...] + mlp_ref[...].astype(wide)).astype(low)


def last_rows(token, d_h1, x_own, d_y1, gain, y1_own, mlp_own):
    count, width = d_y1.shape
    return pl.pallas_call(
        last_kernel,
        name="last_rows",
        grid=(1,),
        in_specs=[kept_block((count, width))] * 3
        + [kept_block((1, width))]
        + [kept_block((count, width))] * 2
        + [ANYWHERE],
        out_specs=[kept_block((count, width)), kept_block((1, width)), kept_block((count, width))],
        out_shape=[
            jax.ShapeDtypeStruct((count, width), wide),
            jax.ShapeDtypeStruct((1, width), wide),
            jax.ShapeDtypeStruct((count, width), low),
        ],
        compiler_params=params(VMEM_ALONE),
        cost_estimate=SMALL,
    )(d_h1, x_own, d_y1, gain.reshape(1, width), y1_own, mlp_own, token)


def kept_out(shape):
    return pl.BlockSpec(shape, lambda *_: (0,) * len(shape))


def together(refs):
    return jnp.concatenate([ref[...] for ref in refs], axis=1)


def back_kernel(count, wg_ref, wu_ref, *refs):
    total = dot_rows(together(refs[:count]), wg_ref[...])
    total = total + dot_rows(together(refs[count : 2 * count]), wu_ref[...])
    refs[-1][...] = total.astype(low)


def ffn_back(w_gate, w_up, d_gate, d_up, token):
    count = d_gate[0].shape[0]
    width = w_gate.shape[0]
    block = min(ROW_BLOCK, count)
    parts = [*d_gate, *d_up]
    return pl.pallas_call(
        functools.partial(back_kernel, len(d_gate)),
        name="ffn_back",
        grid=(count // block,),
        in_specs=[kept_block(w_gate.shape), kept_block(w_up.shape)]
        + [pl.BlockSpec((block, part.shape[1]), lambda i: (i, 0)) for part in parts]
        + [ANYWHERE],
        out_specs=pl.BlockSpec((block, width), lambda i: (i, 0)),
        out_shape=jax.ShapeDtypeStruct((count, width), low),
        compiler_params=params(VMEM_ALONE),
        cost_estimate=SMALL,
    )(w_gate, w_up, *parts, token)


def mlp_kernel(w_ref, *refs):
    result = mm(together(refs[:-2]), w_ref[...])
    refs[-1][...] = result.astype(low).reshape(refs[-1].shape)


def ffn_out(own_rows, w_down, hidden, token):
    count = hidden[0].shape[0]
    width = w_down.shape[1]
    devices = max(1, ROW_BLOCK // own_rows)
    block = devices * own_rows
    return pl.pallas_call(
        mlp_kernel,
        name="ffn_out",
        grid=(count // block,),
        in_specs=[kept_block(w_down.shape)]
        + [pl.BlockSpec((block, part.shape[1]), lambda i: (i, 0)) for part in hidden]
        + [ANYWHERE],
        out_specs=pl.BlockSpec((devices, own_rows, width), lambda i: (i, 0, 0)),
        out_shape=jax.ShapeDtypeStruct((count // own_rows, own_rows + DH, width), low),
        compiler_params=params(VMEM_ALONE),
        cost_estimate=SMALL,
    )(w_down, *hidden, token)


def own_kernel(d_h2_ref, y1_ref, cot_ref, gain_ref, w_ref, mixed_ref, *refs):
    d_y1_ref, d_mixed_ref, d_w_ref, d_gain_ref = refs[-4:]
    y1 = y1_ref[...]
    d_rows, d_gain = norm_back(y1, norm_scale(y1), gain_ref[...], d_h2_ref[...].astype(wide))
    d_y1 = d_rows + cot_ref[...].astype(wide)
    d_attn = d_y1.astype(low)
    d_y1_ref[...] = d_y1
    d_gain_ref[...] = d_gain[None]
    d_mixed_ref[...] = dot_rows(d_attn, w_ref[...]).astype(low)
    d_w_ref[...] = dot_cols(mixed_ref[...], d_attn).astype(low).reshape(d_w_ref.shape)


def own_rows_back(token, d_h2, y1_own, cot_own, gain, w_out_all, mixed_own, buffer):
    count, width = y1_own.shape
    inner = w_out_all.shape[0]
    heads = buffer.shape[0]
    once = [d_h2.shape, y1_own.shape, cot_own.shape, (1, width), w_out_all.shape, mixed_own.shape]
    return pl.pallas_call(
        own_kernel,
        name="own_rows_back",
        grid=(1,),
        in_specs=[kept_block(shape) for shape in once] + [ANYWHERE] * 2,
        out_specs=[
            kept_block((count, width)),
            kept_block((count, inner)),
            pl.BlockSpec(
                (heads, DH, width), lambda i: (0, count // DH, 0), pipeline_mode=pl.Buffered(1)
            ),
            kept_block((1, width)),
        ],
        out_shape=[
            jax.ShapeDtypeStruct((count, width), wide),
            jax.ShapeDtypeStruct((count, inner), low),
            jax.ShapeDtypeStruct(buffer.shape, low),
            jax.ShapeDtypeStruct((1, width), wide),
        ],
        input_output_aliases={7: 2},
        compiler_params=params(VMEM_ALONE),
        cost_estimate=SMALL,
    )(d_h2, y1_own, cot_own, gain.reshape(1, width), w_out_all, mixed_own, token, buffer)


def qkv_back_kernel(d_qkv_ref, h1_ref, w_ref, _, d_h1_ref, d_w_ref, total):
    step = pl.program_id(0)
    d_qkv = d_qkv_ref[...]
    d_h1_ref[...] = dot_rows(d_qkv, w_ref[...]).astype(low)
    part = dot_cols(h1_ref[...], d_qkv)

    @pl.when(step == 0)
    def _():
        total[...] = part

    @pl.when(step > 0)
    def _():
        total[...] += part

    @pl.when(step == pl.num_programs(0) - 1)
    def _():
        d_w_ref[...] = total[...].astype(low)


def qkv_back(d_qkv, h1_all, w_qkv, token):
    count, width = h1_all.shape
    cols = w_qkv.shape[1]
    block = min(ROW_BLOCK, count)
    return pl.pallas_call(
        qkv_back_kernel,
        name="qkv_back",
        grid=(count // block,),
        in_specs=[
            pl.BlockSpec((block, cols), lambda i: (i, 0)),
            pl.BlockSpec((block, width), lambda i: (i, 0)),
            kept_block((width, cols)),
            ANYWHERE,
        ],
        out_specs=[pl.BlockSpec((block, width), lambda i: (i, 0)), kept_out((width, cols))],
        out_shape=[
            jax.ShapeDtypeStruct((count, width), low),
            jax.ShapeDtypeStruct((width, cols), low),
        ],
        scratch_shapes=[pltpu.VMEM((width, cols), wide)],
        compiler_params=params(VMEM_ALONE),
        cost_estimate=SMALL,
    )(d_qkv, h1_all, w_qkv, token)


def join_kernel(takers, place_ref, array_ref, arrived_ref, _, out_ref):
    array, arrived = array_ref[...], arrived_ref[...]
    if takers:
        out_ref[...] = jnp.where(is_one_of(place_ref, takers), arrived, array)
    else:
        out_ref[...] = array + arrived


def join(token, place, takers, array, arrived):
    count, width = array.shape
    block = count // 2
    spec = pl.BlockSpec((block, width), lambda i: (i, 0))
    return pl.pallas_call(
        functools.partial(join_kernel, takers),
        name="join",
        grid=(count // block,),
        in_specs=[pl.BlockSpec(memory_space=pltpu.SMEM), spec, spec, ANYWHERE],
        out_specs=spec,
        out_shape=jax.ShapeDtypeStruct((count, width), low),
        compiler_params=params(VMEM_ALONE),
        cost_estimate=SMALL,
    )(place, array, arrived, token)


def butterfly(array, axis, size):
    if size & (size - 1):
        return lax.psum(array, axis)
    step = 1
    while step < size:
        array = array + lax.ppermute(array, axis, [(i, i ^ step) for i in range(size)])
        step *= 2
    return array


class Chain:
    def __init__(self, axis, size, place, token):
        self.axis, self.size, self.place, self.token = axis, size, place, token
        half = size // 2
        self.stages = [("in", [(s - 1, s), (size - s, size - 1 - s)]) for s in range(1, half)]
        self.stages.append(("in", [(half - 1, half), (half, half - 1)]))
        self.stages += [("out", [(s, s - 1), (size - 1 - s, size - s)]) for s in range(half - 1, 0, -1)]
        self.waiting = []
        self.moving = [[] for _ in self.stages]

    def push(self, array, land):
        self.waiting.append((land, array))

    def send(self, stage, land, array):
        arrived = lax.ppermute(array, self.axis, self.stages[stage][1])
        self.moving[stage].append((land, array, arrived))

    def move(self, stage):
        land, array, arrived = self.moving[stage].pop(0)
        kind, pairs = self.stages[stage]
        takers = tuple(target for _, target in pairs) if kind == "out" else ()
        last = stage + 1 == len(self.stages)
        if kind == "in" or not last:
            array = join(self.token, self.place, takers, array, arrived)
            arrived, takers = array, ()
            self.token = array
        if last:
            self.token = land(self.token, self.place, takers, array, arrived)
        else:
            self.send(stage + 1, land, array)

    def tick(self, between=None):
        if self.size == 1 or self.size % 2:
            for land, array in self.waiting:
                array = lax.psum(array, self.axis)
                self.token = land(self.token, self.place, (), array, array)
            self.waiting = []
            return between() if between else None
        result = None
        ready = [bool(moving) for moving in self.moving]
        if self.waiting:
            land, array = self.waiting.pop(0)
            array = self.token = hold(array, self.token)
            self.send(0, land, array)
        for stage, can_move in enumerate(ready):
            if can_move:
                self.move(stage)
            if stage == max(len(ready) - 2, 0) and between:
                result = between()
        return result

    def drain(self):
        while self.waiting or any(self.moving):
            self.tick()


def assemble_kernel(place_ref, *refs):
    *pieces, out_ref = refs
    rows = pieces[0].shape[0]
    for number, piece in enumerate(pieces):
        begin = pl.multiple_of((place_ref[1] ^ number) * rows, rows)
        out_ref[pl.ds(begin, rows)] = piece[...]


def assemble(place, pieces):
    count = len(pieces)
    rows, cols = pieces[0].shape
    return pl.pallas_call(
        assemble_kernel,
        name="assemble",
        in_specs=[pl.BlockSpec(memory_space=pltpu.SMEM)]
        + [pl.BlockSpec(memory_space=pltpu.VMEM)] * count,
        out_specs=pl.BlockSpec(memory_space=pltpu.VMEM),
        out_shape=jax.ShapeDtypeStruct((count * rows, cols), pieces[0].dtype),
        compiler_params=params(24),
        cost_estimate=SMALL,
    )(place, *pieces)


def gather_pieces(array, axis, size):
    if size != 8:
        gathered = lax.all_gather(array, axis, axis=0)
        return [gathered[i] for i in range(size)]

    def flip(value, bits):
        return lax.ppermute(value, axis, [(i, i ^ bits) for i in range(size)])

    half = array.shape[0] // 2
    side_a, side_b = flip(array, 2), flip(array, 4)
    far_a, far_b = flip(side_a[:half], 4), flip(side_b[half:], 2)
    mine = [array, side_a, side_b, jnp.concatenate([far_a, far_b], axis=0)]
    pieces = []
    for piece in mine:
        pieces += [piece, flip(piece, 1)]
    return pieces


def per_device(
    tokens,
    cotangent,
    doc_lengths,
    pad_mask,
    w_query,
    w_key,
    w_value,
    w_out,
    w_gate,
    w_up,
    w_down,
    norm_attn,
    norm_mlp,
    mix_gate,
    *,
    n_heads,
    n_batch,
):
    width = tokens.shape[-1]
    rows = tokens.shape[2]
    own_rows = MICRO * rows
    here = lax.axis_index("heads")

    def gather(array):
        return lax.all_gather(array, "heads", axis=0, tiled=True)

    def scatter(array):
        return lax.psum_scatter(array, "heads", scatter_dimension=0, tiled=True)

    def grouped(array):
        return array.reshape(n_heads, MICRO, rows, array.shape[-1])

    def flat(array):
        return array.reshape(n_heads * own_rows, array.shape[-1])

    w_qkv = jnp.concatenate([w_query, w_key, w_value], axis=1)
    share = jax.nn.sigmoid(mix_gate)
    positions = jnp.arange(LEN, dtype=jnp.int32)
    doc_ends = jnp.cumsum(doc_lengths[:, 0], axis=1)
    doc_ids = jnp.sum((positions[None, :, None] >= doc_ends[:, None, :]).astype(jnp.int32), axis=2)
    doc_rows = doc_ids[:, :, None]
    doc_cols = jnp.where(pad_mask[:, 0] == 1, doc_ids, -1)[:, None, :]

    tok_own = tokens.reshape(own_rows, width)
    cot_own = cotangent.reshape(own_rows, width)
    place = jnp.stack(
        [here, here if n_heads == 8 else jnp.zeros_like(here), lax.axis_index("batch")]
    )
    tok_all = gather(tok_own)
    w_out_all = assemble(place, gather_pieces(w_out, "heads", n_heads))
    tok_all, w_out_all = lax.optimization_barrier((tok_all, w_out_all))
    cot_all = gather(lax.optimization_barrier((cot_own, tok_all))[0])
    h1_all, qkv = qkv_rows(tok_all, norm_attn, w_qkv)
    qkv = grouped(qkv)
    mixed = flat(head_forward(share, qkv, doc_rows, doc_cols))
    mixed_pieces = gather_pieces(mixed, "heads", n_heads)
    h2_all, y1_own, mixed_own = mid_rows(place, tok_all, mixed_pieces, w_out_all, norm_mlp)

    chain = Chain("batch", n_batch, place, norm_mlp)
    hidden_cols = w_gate.shape[1]
    cols = hidden_cols // FFN_CHUNKS
    grads = {}

    def push_ffn(number, top, bottom):
        for is_top, part in ((True, top), (False, bottom)):
            chain.push(
                part,
                lambda *moved, is_top=is_top: finish_ffn(
                    is_top, number, cols, hidden_cols, *moved, grads
                ),
            )

    def land_qkv(*moved):
        *grads["qkv"], token = finish_cut(3, *moved)
        return token

    def land_out(*moved):
        grads["out"], token = finish_cut(1, *moved)
        return token

    def first(number):
        *parts, top, bottom = ffn_first(
            number, cols, h2_all, cot_all, w_gate, w_up, w_down, chain.token
        )
        chain.token = parts[0]
        push_ffn(number, top, bottom)
        return parts

    def rest(number):
        results = ffn_rest(number, cols, h2_all, cot_all, w_gate, w_up, w_down, chain.token)
        chain.token = results[0]
        return results

    def weights(number, parts):
        top, bottom = ffn_weights(0, cols, h2_all, cot_all, *parts, chain.token)
        chain.token = bottom
        push_ffn(number, top, bottom)

    def wait_for(microseconds):
        chain.token = tie(chain.token, estimate=busy(microseconds))

    part_a = first(0)
    chain.tick()
    part_b = first(1)
    part_c = rest(2)
    chain.tick()
    part_d = rest(3)
    weights(2, part_c)
    chain.tick()
    hidden, d_gate, d_up = zip(part_a, part_b, part_c, part_d)
    d_h2 = chain.token = ffn_back(w_gate, w_up, d_gate, d_up, chain.token)
    d_h2 = scatter(d_h2)
    chain.tick()
    out_parts = chain.token = ffn_out(own_rows, w_down, hidden, chain.token)
    chain.tick()
    weights(3, part_d)

    def own_part():
        wait_for(WAITS[0])
        results = own_rows_back(
            chain.token, d_h2, y1_own, cot_own, norm_mlp, w_out_all, mixed_own, out_parts
        )
        chain.token = results[0]
        return results

    d_y1, d_mixed_own, parts, gain_mlp_part = chain.tick(own_part)
    d_mixed = lax.all_to_all(d_mixed_own, "heads", split_axis=1, concat_axis=0, tiled=True)
    parts = scatter(parts.reshape(-1, width))
    chain.tick()
    wait_for(WAITS[2])
    d_qkv, d_share = head_backward(
        share, qkv, grouped(d_mixed), doc_rows, doc_cols, chain.token
    )
    chain.token = d_share
    chain.tick()
    d_h1, grad_qkv = qkv_back(flat(d_qkv), h1_all, w_qkv, chain.token)
    chain.token = d_h1
    chain.push(grad_qkv, land_qkv)

    def scatter_last():
        wait_for(WAITS[3])
        chain.token = tie(chain.token, parts)
        chain.token = hold(d_h1, chain.token)
        return scatter(chain.token)

    d_h1 = chain.tick(scatter_last)
    chain.push(parts[own_rows:], land_out)
    chain.tick()
    chain.tick()

    wait_for(WAITS[1])
    grad_tokens, gain_attn_part, layer_out = last_rows(
        chain.token, d_h1, tok_own, d_y1, norm_attn, y1_own, parts
    )
    grad_tokens = grad_tokens.reshape(tokens.shape)
    chain.token = gain_attn_part
    slots = jnp.where(jnp.arange(n_heads) == here, jnp.sum(d_share[:, 0, 0]), 0.0)
    sums = jnp.concatenate([gain_attn_part[0], gain_mlp_part[0], slots])
    sums = butterfly(sums, "heads", n_heads)
    if n_batch == 4:
        sums = sums + lax.ppermute(sums, "batch", [(i, i ^ 1) for i in range(4)])
        chain.tick()
        sums = chain.token = hold(sums, chain.token)
        sums = sums + lax.ppermute(sums, "batch", [(i, i ^ 2) for i in range(4)])
    else:
        sums = butterfly(sums, "batch", n_batch)
    grad_mix = lax.dynamic_slice_in_dim(sums, 2 * width + here, 1, 0)
    chain.drain()

    return (
        layer_out.reshape(tokens.shape),
        grad_tokens,
        *grads["qkv"],
        grads["out"],
        grads["gate"].reshape(w_gate.shape),
        grads["up"].reshape(w_up.shape),
        grads["down"],
        sums[:width],
        sums[width : 2 * width],
        grad_mix,
    )


def solution(mesh):
    in_specs = (
        P(None, "batch", "heads", None),
        P(None, "batch", "heads", None),
        P(None, "batch", None),
        P(None, "batch", None),
        P(None, "heads"),
        P(None, "heads"),
        P(None, "heads"),
        P("heads", None),
        P(None, "heads"),
        P(None, "heads"),
        P("heads", None),
        P(),
        P(),
        P("heads"),
    )
    out_specs = (
        P(None, "batch", "heads", None),
        P(None, "batch", "heads", None),
        P(None, "heads"),
        P(None, "heads"),
        P(None, "heads"),
        P("heads", None),
        P(None, "heads"),
        P(None, "heads"),
        P("heads", None),
        P(),
        P(),
        P("heads"),
    )

    def program(*arrays):
        return per_device(*arrays, n_heads=mesh.shape["heads"], n_batch=mesh.shape["batch"])

    return jax.shard_map(
        program, mesh=mesh, in_specs=in_specs, out_specs=out_specs, check_vma=False
    )
```

```python
import functools

import jax
import jax.numpy as jnp
from jax import lax
from jax.experimental import pallas as pl
from jax.experimental.pallas import tpu as pltpu
from jax.sharding import PartitionSpec as P

DH = 128
SEG = 512
SEGS = 2
LEN = 1024
MICRO = 2
FFN_CHUNKS = 4
WAITS = (102, 108, 5, 172)
ROW_BLOCK = 512
MIB = 1 << 20
VMEM_ALONE = 60
IN_VMEM = pl.BlockSpec(memory_space=pltpu.VMEM)
ANYWHERE = pl.BlockSpec(memory_space=pl.ANY)
SMALL = pl.CostEstimate(flops=1, bytes_accessed=1, transcendentals=0)
def busy(microseconds):
    return pl.CostEstimate(flops=int(microseconds * 10**9), bytes_accessed=1, transcendentals=0)


epsilon = 1e-05
big_negative = -1e30
low = jnp.bfloat16
wide = jnp.float32


def mm(left_mat, right_mat):
    return jnp.dot(left_mat, right_mat, preferred_element_type=wide)


def dot_rows(left_mat, right_mat):
    return lax.dot_general(
        left_mat, right_mat, (((1,), (1,)), ((), ())), preferred_element_type=wide
    )


def dot_cols(left_mat, right_mat):
    return lax.dot_general(
        left_mat, right_mat, (((0,), (0,)), ((), ())), preferred_element_type=wide
    )


def norm_scale(row_block):
    return lax.rsqrt(jnp.mean(row_block * row_block, axis=-1, keepdims=True) + epsilon)


def norm_back(row_block, row_scale, gain_vec, upstream):
    shaped = upstream * gain_vec
    inner = jnp.mean(shaped * row_block, axis=-1, keepdims=True)
    d_rows = row_scale * shaped - row_block * row_scale * row_scale * row_scale * inner
    d_gain = jnp.sum(upstream * row_block * row_scale, axis=0)
    return (d_rows, d_gain)


def positive(values_in):
    return jnp.where(values_in > 0, values_in + 1.0, jnp.exp(values_in))


def positive_slope(values_in):
    return jnp.where(values_in > 0, 1.0, jnp.exp(values_in))


def params(mebibytes):
    return pltpu.CompilerParams(vmem_limit_bytes=mebibytes * MIB)


def kept_block(shape):
    return pl.BlockSpec(shape, lambda *_: (0,) * len(shape), pipeline_mode=pl.Buffered(1))


def qkv_kernel(x_ref, gain_ref, w_ref, h1_ref, qkv_ref):
    rows = x_ref[...].astype(wide)
    h1 = (rows * norm_scale(rows) * gain_ref[...]).astype(low)
    h1_ref[...] = h1
    qkv_ref[...] = mm(h1, w_ref[...]).astype(low)


def qkv_rows(x_all, gain, w_qkv):
    count, width = x_all.shape
    cols = w_qkv.shape[1]
    block = min(ROW_BLOCK, count)
    return pl.pallas_call(
        qkv_kernel,
        name="qkv_rows",
        grid=(count // block,),
        in_specs=[
            pl.BlockSpec((block, width), lambda i: (i, 0)),
            kept_block((1, width)),
            kept_block((width, cols)),
        ],
        out_specs=[
            pl.BlockSpec((block, width), lambda i: (i, 0)),
            pl.BlockSpec((block, cols), lambda i: (i, 0)),
        ],
        out_shape=[
            jax.ShapeDtypeStruct((count, width), low),
            jax.ShapeDtypeStruct((count, cols), low),
        ],
        compiler_params=params(VMEM_ALONE),
        cost_estimate=SMALL,
    )(x_all, gain.reshape(1, width), w_qkv)


def seg_of(array, segment):
    return array[segment * SEG : (segment + 1) * SEG]


def local_probs(query_seg, key_seg, doc_rows, doc_cols):
    row_ids = lax.broadcasted_iota(jnp.int32, (SEG, SEG), 0)
    col_ids = lax.broadcasted_iota(jnp.int32, (SEG, SEG), 1)
    allowed = ((doc_rows == doc_cols) & (col_ids <= row_ids)) | (col_ids == row_ids)
    scores = jnp.where(allowed, dot_rows(query_seg, key_seg) * DH ** (-0.5), big_negative)
    shifted = jnp.exp(scores - jnp.max(scores, axis=1, keepdims=True))
    return shifted * (1.0 / jnp.sum(shifted, axis=1, keepdims=True))


def head_kernel(share_ref, qkv_ref, doc_rows_ref, doc_cols_ref, mixed_ref):
    share = share_ref[0]
    qkv = qkv_ref[...].reshape(LEN, 3 * DH)
    query, key, value = [qkv[:, i * DH : (i + 1) * DH] for i in range(3)]
    parts = []
    for segment in range(SEGS):
        begin = segment * SEG
        query_seg = seg_of(query, segment)
        doc_rows = doc_rows_ref[begin : begin + SEG]
        probs = local_probs(
            query_seg, seg_of(key, segment), doc_rows, doc_cols_ref[:, begin : begin + SEG]
        )
        result = (1.0 - share) * mm(probs.astype(low), seg_of(value, segment))
        if segment > 0:
            allowed = doc_rows == doc_cols_ref[:, :begin]
            pos_query = positive(query_seg.astype(wide)).astype(low)
            pos_key = positive(key[:begin].astype(wide)).astype(low)
            weights = jnp.where(allowed, dot_rows(pos_query, pos_key), 0.0)
            den = jnp.maximum(jnp.sum(weights, axis=1, keepdims=True), 1.0)
            result = result + share * (mm(weights.astype(low), value[:begin]) / den)
        parts.append(result.astype(low))
    mixed_ref[...] = jnp.concatenate(parts, axis=0).reshape(mixed_ref.shape)


def micro_spec(n_heads, rows, cols):
    return pl.BlockSpec((n_heads, None, rows, cols), lambda m: (0, m, 0, 0))


def doc_specs():
    return [
        pl.BlockSpec((None, LEN, 1), lambda m: (m, 0, 0)),
        pl.BlockSpec((None, 1, LEN), lambda m: (m, 0, 0)),
    ]


def head_forward(share, qkv, doc_rows, doc_cols):
    n_heads, micro, rows, cols = qkv.shape
    pairs = micro * LEN * SEG * 2
    return pl.pallas_call(
        head_kernel,
        name="head_forward",
        grid=(micro,),
        in_specs=[pl.BlockSpec(memory_space=pltpu.SMEM), micro_spec(n_heads, rows, cols), *doc_specs()],
        out_specs=micro_spec(n_heads, rows, DH),
        out_shape=jax.ShapeDtypeStruct((n_heads, micro, rows, DH), low),
        compiler_params=params(VMEM_ALONE),
        cost_estimate=SMALL,
    )(share, qkv, doc_rows, doc_cols)


def head_back_kernel(
    share_ref, qkv_ref, d_mixed_ref, doc_rows_ref, doc_cols_ref, _, d_qkv_ref, d_share_ref
):
    share = share_ref[0]
    scale = DH ** (-0.5)
    qkv = qkv_ref[...].reshape(LEN, 3 * DH)
    query, key, value = [qkv[:, i * DH : (i + 1) * DH] for i in range(3)]
    d_mixed = d_mixed_ref[...].reshape(LEN, DH).astype(wide)
    d_query, d_key, d_value = [[None] * SEGS for _ in range(3)]
    d_share = jnp.zeros((1, 1), wide)
    for segment in range(SEGS):
        begin = segment * SEG
        query_seg, key_seg, value_seg = [seg_of(a, segment) for a in (query, key, value)]
        doc_rows = doc_rows_ref[begin : begin + SEG]
        probs = local_probs(query_seg, key_seg, doc_rows, doc_cols_ref[:, begin : begin + SEG])
        probs_low = probs.astype(low)
        d_mixed_seg = seg_of(d_mixed, segment)
        d_dotted = ((1.0 - share) * d_mixed_seg).astype(low)
        gap = -mm(probs_low, value_seg)
        d_probs = dot_rows(d_dotted, value_seg)
        d_scores = (
            probs * (d_probs - jnp.sum(probs * d_probs, axis=1, keepdims=True))
        ).astype(low)
        d_value[segment] = dot_cols(probs_low, d_dotted)
        d_query[segment] = mm(d_scores, key_seg) * scale
        d_key[segment] = dot_cols(d_scores, query_seg) * scale
        if segment > 0:
            allowed = doc_rows == doc_cols_ref[:, :begin]
            query_float = query_seg.astype(wide)
            key_float = key[:begin].astype(wide)
            pos_query = positive(query_float).astype(low)
            pos_key = positive(key_float).astype(low)
            weights = jnp.where(allowed, dot_rows(pos_query, pos_key), 0.0)
            row_total = jnp.sum(weights, axis=1, keepdims=True)
            inverse = 1.0 / jnp.maximum(row_total, 1.0)
            weights_low = weights.astype(low)
            numerator = mm(weights_low, value[:begin])
            gap = gap + numerator * inverse
            d_recalled = share * d_mixed_seg
            d_numer = (d_recalled * inverse).astype(low)
            d_denom = jnp.where(
                row_total > 1.0,
                -jnp.sum(d_recalled * numerator, axis=1, keepdims=True) * inverse * inverse,
                0.0,
            )
            d_weights = jnp.where(
                allowed, dot_rows(d_numer, value[:begin]) + d_denom, 0.0
            ).astype(low)
            d_query[segment] += mm(d_weights, pos_key) * positive_slope(query_float)
            d_pos_key = dot_cols(d_weights, pos_query) * positive_slope(key_float)
            d_value_before = dot_cols(weights_low, d_numer)
            for earlier in range(segment):
                d_key[earlier] += seg_of(d_pos_key, earlier)
                d_value[earlier] += seg_of(d_value_before, earlier)
        d_share = d_share + jnp.sum(
            jnp.sum(d_mixed_seg * gap, axis=1, keepdims=True), axis=0, keepdims=True
        )
    whole = jnp.concatenate(
        [jnp.concatenate(parts, axis=0).astype(low) for parts in (d_query, d_key, d_value)], axis=1
    )
    d_qkv_ref[...] = whole.reshape(d_qkv_ref.shape)
    d_share_ref[...] = jnp.broadcast_to(d_share * (share * (1.0 - share)), d_share_ref.shape)


def head_backward(share, qkv, d_mixed, doc_rows, doc_cols, token):
    n_heads, micro, rows, cols = qkv.shape
    pairs = micro * LEN * SEG * 2
    return pl.pallas_call(
        head_back_kernel,
        name="head_backward",
        grid=(micro,),
        in_specs=[
            pl.BlockSpec(memory_space=pltpu.SMEM),
            micro_spec(n_heads, rows, cols),
            micro_spec(n_heads, rows, DH),
            *doc_specs(),
            ANYWHERE,
        ],
        out_specs=[
            micro_spec(n_heads, rows, cols),
            pl.BlockSpec((None, 8, 128), lambda m: (m, 0, 0)),
        ],
        out_shape=[
            jax.ShapeDtypeStruct((n_heads, micro, rows, cols), low),
            jax.ShapeDtypeStruct((micro, 8, 128), wide),
        ],
        compiler_params=params(VMEM_ALONE),
        cost_estimate=SMALL,
    )(share, qkv, d_mixed, doc_rows, doc_cols, token)


def mid_kernel(heads, place_ref, x_ref, *refs):
    mixed_refs = refs[:heads]
    w_ref, gain_ref, h2_ref, y1_ref, mixed_own_ref, w_near = refs[heads:]
    step = pl.program_id(0)
    own_rows = y1_ref.shape[0]
    devices = x_ref.shape[0] // own_rows

    def owner(number):
        return pl.multiple_of((place_ref[1] ^ number) * DH, DH)

    @pl.when(step == 0)
    def _():
        for number in range(heads):
            w_near[number * DH : (number + 1) * DH] = w_ref[pl.ds(owner(number), DH)]

    mixed = jnp.concatenate([ref[...] for ref in mixed_refs], axis=1)
    y1 = x_ref[...].astype(wide) + mm(mixed, w_near[...])
    h2_ref[...] = (y1 * norm_scale(y1) * gain_ref[...]).astype(low)
    for device in range(devices):
        begin = device * own_rows

        @pl.when(step * devices + device == place_ref[0])
        def _():
            y1_ref[...] = y1[begin : begin + own_rows]
            for number in range(heads):
                mixed_own_ref[:, pl.ds(owner(number), DH)] = mixed_refs[number][
                    begin : begin + own_rows
                ]


def mid_rows(place, x_all, mixed_pieces, w_out_all, gain):
    count, width = x_all.shape
    heads = len(mixed_pieces)
    inner = w_out_all.shape[0]
    own_rows = count // heads
    block = max(1, ROW_BLOCK // own_rows) * own_rows
    return pl.pallas_call(
        functools.partial(mid_kernel, heads),
        name="mid_rows",
        grid_spec=pltpu.PrefetchScalarGridSpec(
            num_scalar_prefetch=1,
            grid=(count // block,),
            in_specs=[
                pl.BlockSpec((block, width), lambda i, _: (i, 0)),
                *[pl.BlockSpec((block, DH), lambda i, _: (i, 0))] * heads,
                kept_block((inner, width)),
                kept_block((1, width)),
            ],
            out_specs=[
                pl.BlockSpec((block, width), lambda i, _: (i, 0)),
                pl.BlockSpec((own_rows, width), lambda i, _: (0, 0)),
                pl.BlockSpec((own_rows, inner), lambda i, _: (0, 0)),
            ],
            scratch_shapes=[pltpu.VMEM((inner, width), low)],
        ),
        out_shape=[
            jax.ShapeDtypeStruct((count, width), low),
            jax.ShapeDtypeStruct((own_rows, width), wide),
            jax.ShapeDtypeStruct((own_rows, inner), low),
        ],
        compiler_params=params(VMEM_ALONE),
        cost_estimate=SMALL,
    )(place, x_all, *mixed_pieces, w_out_all, gain.reshape(1, width))


def ffn_rows(h2_ref, cot_ref, w_gate, w_up, w_down):
    h2 = h2_ref[...]
    gate = mm(h2, w_gate)
    up = mm(h2, w_up)
    d_hidden = dot_rows(cot_ref[...], w_down)
    sig = jax.nn.sigmoid(gate)
    act = gate * sig
    hidden = (act * up).astype(low)
    d_up = (d_hidden * act).astype(low)
    d_gate = (d_hidden * up * sig * (1.0 + gate * (1.0 - sig))).astype(low)
    return hidden, d_gate, d_up


def ffn_grads(step, hidden, d_both, h2_ref, cot_ref, top_ref, bottom_ref):
    cols = hidden.shape[1]
    side = 2 * cols
    half = cols // 2
    span = pl.ds(pl.multiple_of(step * side, side), side)
    top_ref[:cols, span] = dot_cols(hidden[...], cot_ref[...]).astype(low)
    square = dot_cols(h2_ref[...], d_both[...]).astype(low)
    top_ref[cols:, span] = square[3 * half :]
    bottom_ref[:, span] = square[: 3 * half]


def first_kernel(
    blocks, h2_ref, cot_ref, h2_col_ref, cot_col_ref, wg_ref, wu_ref, wd_ref, _, *refs
):
    hid_ref, dg_ref, du_ref, top_ref, bottom_ref, hid_all, both_all = refs
    step = pl.program_id(0)
    block, cols = hid_ref.shape

    @pl.when(step < blocks)
    def _():
        rows = pl.ds(pl.multiple_of(step * block, block), block)
        hidden, d_gate, d_up = ffn_rows(h2_ref, cot_ref, wg_ref[...], wu_ref[...], wd_ref[...])
        hid_ref[...] = hid_all[rows] = hidden
        dg_ref[...] = both_all[rows, :cols] = d_gate
        du_ref[...] = both_all[rows, cols:] = d_up

    @pl.when(step >= blocks)
    def _():
        ffn_grads(step - blocks, hid_all, both_all, h2_col_ref, cot_col_ref, top_ref, bottom_ref)


def ffn_first(number, cols, h2_all, cot_all, w_gate, w_up, w_down, token):
    count, width = h2_all.shape
    block = min(ROW_BLOCK, count // 2)
    blocks = count // block
    side = 2 * cols
    row_spec = pl.BlockSpec((block, width), lambda i: (jnp.minimum(i, blocks - 1), 0))
    side_spec = pl.BlockSpec((count, side), lambda i: (0, jnp.maximum(i - blocks, 0)))
    col_spec = pl.BlockSpec((width, cols), lambda i: (0, number), pipeline_mode=pl.Buffered(1))
    down_spec = pl.BlockSpec((cols, width), lambda i: (number, 0), pipeline_mode=pl.Buffered(1))
    out_spec = pl.BlockSpec((block, cols), lambda i: (jnp.minimum(i, blocks - 1), 0))
    piece = (3 * cols // 2, width)
    return pl.pallas_call(
        functools.partial(first_kernel, blocks),
        name="ffn_first",
        grid=(blocks + width // side,),
        in_specs=[row_spec, row_spec, side_spec, side_spec, col_spec, col_spec, down_spec, ANYWHERE],
        out_specs=[out_spec] * 3 + [kept_out(piece)] * 2,
        out_shape=[jax.ShapeDtypeStruct((count, cols), low)] * 3
        + [jax.ShapeDtypeStruct(piece, low)] * 2,
        scratch_shapes=[pltpu.VMEM((count, cols), low), pltpu.VMEM((count, side), low)],
        compiler_params=params(VMEM_ALONE),
        cost_estimate=SMALL,
    )(h2_all, cot_all, h2_all, cot_all, w_gate, w_up, w_down, token)


def rest_kernel(h2_ref, cot_ref, wg_ref, wu_ref, wd_ref, _, *refs):
    results = ffn_rows(h2_ref, cot_ref, wg_ref[...], wu_ref[...], wd_ref[...])
    for ref, result in zip(refs, results):
        ref[...] = result


def ffn_rest(number, cols, h2_all, cot_all, w_gate, w_up, w_down, token):
    count, width = h2_all.shape
    block = min(ROW_BLOCK, count // 2)
    row_spec = pl.BlockSpec((block, width), lambda i: (i, 0))
    col_spec = pl.BlockSpec((width, cols), lambda i: (0, number), pipeline_mode=pl.Buffered(1))
    down_spec = pl.BlockSpec((cols, width), lambda i: (number, 0), pipeline_mode=pl.Buffered(1))
    return pl.pallas_call(
        rest_kernel,
        name="ffn_rest",
        grid=(count // block,),
        in_specs=[row_spec, row_spec, col_spec, col_spec, down_spec, ANYWHERE],
        out_specs=[pl.BlockSpec((block, cols), lambda i: (i, 0))] * 3,
        out_shape=[jax.ShapeDtypeStruct((count, cols), low)] * 3,
        compiler_params=params(VMEM_ALONE),
        cost_estimate=SMALL,
    )(h2_all, cot_all, w_gate, w_up, w_down, token)


def grads_kernel(h2_ref, cot_ref, hid_ref, dg_ref, du_ref, _, top_ref, bottom_ref, both_all):
    step = pl.program_id(0)
    cols = hid_ref.shape[1]

    @pl.when(step == 0)
    def _():
        both_all[:, :cols] = dg_ref[...]
        both_all[:, cols:] = du_ref[...]

    ffn_grads(step, hid_ref, both_all, h2_ref, cot_ref, top_ref, bottom_ref)


def ffn_weights(number, cols, h2_all, cot_all, hidden, d_gate, d_up, token):
    count, width = h2_all.shape
    side = 2 * cols
    side_spec = pl.BlockSpec((count, side), lambda i: (0, i))
    col_spec = pl.BlockSpec((count, cols), lambda i: (0, number), pipeline_mode=pl.Buffered(1))
    piece = (3 * cols // 2, width)
    return pl.pallas_call(
        grads_kernel,
        name="ffn_weights",
        grid=(width // side,),
        in_specs=[side_spec, side_spec, col_spec, col_spec, col_spec, ANYWHERE],
        out_specs=[kept_out(piece)] * 2,
        out_shape=[jax.ShapeDtypeStruct(piece, low)] * 2,
        scratch_shapes=[pltpu.VMEM((count, side), low)],
        compiler_params=params(VMEM_ALONE),
        cost_estimate=SMALL,
    )(h2_all, cot_all, hidden, d_gate, d_up, token)


def is_one_of(place_ref, takers):
    found = place_ref[2] == takers[0]
    for taker in takers[1:]:
        found = found | (place_ref[2] == taker)
    return found


def chosen(takers, place_ref, array_ref, arrived_ref):
    if not takers:
        return array_ref[...].astype(wide)
    return jnp.where(is_one_of(place_ref, takers), arrived_ref[...], array_ref[...]).astype(wide)


def finish_kernel(cols, has_down, takers, place_ref, array_ref, arrived_ref, *refs):
    *_, gate_ref, up_ref, token_ref = refs
    value = chosen(takers, place_ref, array_ref, arrived_ref)
    if has_down:
        refs[-4][...] = value[:cols]
        value = value[cols:]
    for number in range(gate_ref.shape[0]):
        begin = number * 2 * cols
        gate_ref[number] = value[:, begin : begin + cols]
        up_ref[number] = value[:, begin + cols : begin + 2 * cols]
    token_ref[...] = jnp.zeros_like(token_ref)


def finish_ffn(is_top, number, cols, hidden_cols, token, place, takers, array, arrived, grads):
    count, width = array.shape
    squares = width // (2 * cols)
    in_spec = kept_block((count, width))
    square_shape = jax.ShapeDtypeStruct((squares, 2 * cols, hidden_cols), wide)
    if is_top:
        square_spec = pl.BlockSpec((squares, cols // 2, cols), lambda i: (0, 3, number))
    else:
        square_spec = pl.BlockSpec((squares, count, cols), lambda i: (0, 0, number))
    out_specs = [square_spec, square_spec, kept_out((8, 128))]
    out_shape = [square_shape, square_shape, jax.ShapeDtypeStruct((8, 128), wide)]
    names = ["gate", "up"]
    if is_top:
        out_specs.insert(0, pl.BlockSpec((cols, width), lambda i: (number, 0)))
        out_shape.insert(0, jax.ShapeDtypeStruct((hidden_cols, width), wide))
        names.insert(0, "down")
    carried = [(i, grads[name]) for i, name in enumerate(names) if name in grads]
    *buffers, token = pl.pallas_call(
        functools.partial(finish_kernel, cols, is_top, takers),
        name="finish_ffn",
        grid=(1,),
        in_specs=[pl.BlockSpec(memory_space=pltpu.SMEM), in_spec, in_spec, ANYWHERE]
        + [ANYWHERE] * len(carried),
        out_specs=out_specs,
        out_shape=out_shape,
        input_output_aliases={4 + i: target for i, (target, _) in enumerate(carried)},
        compiler_params=params(VMEM_ALONE),
        cost_estimate=SMALL,
    )(place, array, arrived, token, *[buffer for _, buffer in carried])
    grads.update(zip(names, buffers))
    return token


def cut_kernel(takers, place_ref, array_ref, arrived_ref, _, *outs):
    value = chosen(takers, place_ref, array_ref, arrived_ref)
    cols = outs[0].shape[1]
    for number, out in enumerate(outs[:-1]):
        out[...] = value[:, number * cols : (number + 1) * cols]
    outs[-1][...] = jnp.zeros_like(outs[-1])


def finish_cut(pieces, token, place, takers, array, arrived):
    count, width = array.shape
    block = count // 2
    cols = width // pieces
    in_spec = pl.BlockSpec((block, width), lambda i: (i, 0))
    out_spec = pl.BlockSpec((block, cols), lambda i: (i, 0))
    return pl.pallas_call(
        functools.partial(cut_kernel, takers),
        name="finish_cut",
        grid=(2,),
        in_specs=[pl.BlockSpec(memory_space=pltpu.SMEM), in_spec, in_spec, ANYWHERE],
        out_specs=[out_spec] * pieces + [kept_out((8, 128))],
        out_shape=[jax.ShapeDtypeStruct((count, cols), wide)] * pieces
        + [jax.ShapeDtypeStruct((8, 128), wide)],
        compiler_params=params(VMEM_ALONE),
        cost_estimate=SMALL,
    )(place, array, arrived, token)


def tie_kernel(*refs):
    refs[-1][...] = jnp.zeros_like(refs[-1])


def tie(*arrays, estimate=SMALL):
    return pl.pallas_call(
        tie_kernel,
        name="tie",
        in_specs=[ANYWHERE] * len(arrays),
        out_specs=IN_VMEM,
        out_shape=jax.ShapeDtypeStruct((8, 128), wide),
        compiler_params=params(VMEM_ALONE),
        cost_estimate=estimate,
    )(*arrays)


def hold_kernel(*_):
    pass


def hold(array, token, estimate=SMALL):
    return pl.pallas_call(
        hold_kernel,
        name="hold",
        in_specs=[ANYWHERE] * 2,
        out_specs=ANYWHERE,
        out_shape=jax.ShapeDtypeStruct(array.shape, array.dtype),
        input_output_aliases={0: 0},
        compiler_params=params(VMEM_ALONE),
        cost_estimate=estimate,
    )(array, token)


def last_kernel(d_h1_ref, x_ref, d_y1_ref, gain_ref, y1_ref, mlp_ref, _, out_ref, d_gain_ref, layer_ref):
    rows = x_ref[...].astype(wide)
    d_rows, d_gain = norm_back(rows, norm_scale(rows), gain_ref[...], d_h1_ref[...].astype(wide))
    out_ref[...] = d_rows + d_y1_ref[...]
    d_gain_ref[...] = d_gain[None]
    layer_ref[...] = (y1_ref[...] + mlp_ref[...].astype(wide)).astype(low)


def last_rows(token, d_h1, x_own, d_y1, gain, y1_own, mlp_own):
    count, width = d_y1.shape
    return pl.pallas_call(
        last_kernel,
        name="last_rows",
        grid=(1,),
        in_specs=[kept_block((count, width))] * 3
        + [kept_block((1, width))]
        + [kept_block((count, width))] * 2
        + [ANYWHERE],
        out_specs=[kept_block((count, width)), kept_block((1, width)), kept_block((count, width))],
        out_shape=[
            jax.ShapeDtypeStruct((count, width), wide),
            jax.ShapeDtypeStruct((1, width), wide),
            jax.ShapeDtypeStruct((count, width), low),
        ],
        compiler_params=params(VMEM_ALONE),
        cost_estimate=SMALL,
    )(d_h1, x_own, d_y1, gain.reshape(1, width), y1_own, mlp_own, token)


def kept_out(shape):
    return pl.BlockSpec(shape, lambda *_: (0,) * len(shape))


def together(refs):
    return jnp.concatenate([ref[...] for ref in refs], axis=1)


def back_kernel(count, wg_ref, wu_ref, *refs):
    total = dot_rows(together(refs[:count]), wg_ref[...])
    total = total + dot_rows(together(refs[count : 2 * count]), wu_ref[...])
    refs[-1][...] = total.astype(low)


def ffn_back(w_gate, w_up, d_gate, d_up, token):
    count = d_gate[0].shape[0]
    width = w_gate.shape[0]
    block = min(ROW_BLOCK, count)
    parts = [*d_gate, *d_up]
    return pl.pallas_call(
        functools.partial(back_kernel, len(d_gate)),
        name="ffn_back",
        grid=(count // block,),
        in_specs=[kept_block(w_gate.shape), kept_block(w_up.shape)]
        + [pl.BlockSpec((block, part.shape[1]), lambda i: (i, 0)) for part in parts]
        + [ANYWHERE],
        out_specs=pl.BlockSpec((block, width), lambda i: (i, 0)),
        out_shape=jax.ShapeDtypeStruct((count, width), low),
        compiler_params=params(VMEM_ALONE),
        cost_estimate=SMALL,
    )(w_gate, w_up, *parts, token)


def mlp_kernel(w_ref, *refs):
    result = mm(together(refs[:-2]), w_ref[...])
    refs[-1][...] = result.astype(low).reshape(refs[-1].shape)


def ffn_out(own_rows, w_down, hidden, token):
    count = hidden[0].shape[0]
    width = w_down.shape[1]
    devices = max(1, ROW_BLOCK // own_rows)
    block = devices * own_rows
    return pl.pallas_call(
        mlp_kernel,
        name="ffn_out",
        grid=(count // block,),
        in_specs=[kept_block(w_down.shape)]
        + [pl.BlockSpec((block, part.shape[1]), lambda i: (i, 0)) for part in hidden]
        + [ANYWHERE],
        out_specs=pl.BlockSpec((devices, own_rows, width), lambda i: (i, 0, 0)),
        out_shape=jax.ShapeDtypeStruct((count // own_rows, own_rows + DH, width), low),
        compiler_params=params(VMEM_ALONE),
        cost_estimate=SMALL,
    )(w_down, *hidden, token)


def own_kernel(d_h2_ref, y1_ref, cot_ref, gain_ref, w_ref, mixed_ref, *refs):
    d_y1_ref, d_mixed_ref, d_w_ref, d_gain_ref = refs[-4:]
    y1 = y1_ref[...]
    d_rows, d_gain = norm_back(y1, norm_scale(y1), gain_ref[...], d_h2_ref[...].astype(wide))
    d_y1 = d_rows + cot_ref[...].astype(wide)
    d_attn = d_y1.astype(low)
    d_y1_ref[...] = d_y1
    d_gain_ref[...] = d_gain[None]
    d_mixed_ref[...] = dot_rows(d_attn, w_ref[...]).astype(low)
    d_w_ref[...] = dot_cols(mixed_ref[...], d_attn).astype(low).reshape(d_w_ref.shape)


def own_rows_back(token, d_h2, y1_own, cot_own, gain, w_out_all, mixed_own, buffer):
    count, width = y1_own.shape
    inner = w_out_all.shape[0]
    heads = buffer.shape[0]
    once = [d_h2.shape, y1_own.shape, cot_own.shape, (1, width), w_out_all.shape, mixed_own.shape]
    return pl.pallas_call(
        own_kernel,
        name="own_rows_back",
        grid=(1,),
        in_specs=[kept_block(shape) for shape in once] + [ANYWHERE] * 2,
        out_specs=[
            kept_block((count, width)),
            kept_block((count, inner)),
            pl.BlockSpec(
                (heads, DH, width), lambda i: (0, count // DH, 0), pipeline_mode=pl.Buffered(1)
            ),
            kept_block((1, width)),
        ],
        out_shape=[
            jax.ShapeDtypeStruct((count, width), wide),
            jax.ShapeDtypeStruct((count, inner), low),
            jax.ShapeDtypeStruct(buffer.shape, low),
            jax.ShapeDtypeStruct((1, width), wide),
        ],
        input_output_aliases={7: 2},
        compiler_params=params(VMEM_ALONE),
        cost_estimate=SMALL,
    )(d_h2, y1_own, cot_own, gain.reshape(1, width), w_out_all, mixed_own, token, buffer)


def qkv_back_kernel(d_qkv_ref, h1_ref, w_ref, _, d_h1_ref, d_w_ref, total):
    step = pl.program_id(0)
    d_qkv = d_qkv_ref[...]
    d_h1_ref[...] = dot_rows(d_qkv, w_ref[...]).astype(low)
    part = dot_cols(h1_ref[...], d_qkv)

    @pl.when(step == 0)
    def _():
        total[...] = part

    @pl.when(step > 0)
    def _():
        total[...] += part

    @pl.when(step == pl.num_programs(0) - 1)
    def _():
        d_w_ref[...] = total[...].astype(low)


def qkv_back(d_qkv, h1_all, w_qkv, token):
    count, width = h1_all.shape
    cols = w_qkv.shape[1]
    block = min(ROW_BLOCK, count)
    return pl.pallas_call(
        qkv_back_kernel,
        name="qkv_back",
        grid=(count // block,),
        in_specs=[
            pl.BlockSpec((block, cols), lambda i: (i, 0)),
            pl.BlockSpec((block, width), lambda i: (i, 0)),
            kept_block((width, cols)),
            ANYWHERE,
        ],
        out_specs=[pl.BlockSpec((block, width), lambda i: (i, 0)), kept_out((width, cols))],
        out_shape=[
            jax.ShapeDtypeStruct((count, width), low),
            jax.ShapeDtypeStruct((width, cols), low),
        ],
        scratch_shapes=[pltpu.VMEM((width, cols), wide)],
        compiler_params=params(VMEM_ALONE),
        cost_estimate=SMALL,
    )(d_qkv, h1_all, w_qkv, token)


def join_kernel(takers, place_ref, array_ref, arrived_ref, _, out_ref):
    array, arrived = array_ref[...], arrived_ref[...]
    if takers:
        out_ref[...] = jnp.where(is_one_of(place_ref, takers), arrived, array)
    else:
        out_ref[...] = array + arrived


def join(token, place, takers, array, arrived):
    count, width = array.shape
    block = count // 2
    spec = pl.BlockSpec((block, width), lambda i: (i, 0))
    return pl.pallas_call(
        functools.partial(join_kernel, takers),
        name="join",
        grid=(count // block,),
        in_specs=[pl.BlockSpec(memory_space=pltpu.SMEM), spec, spec, ANYWHERE],
        out_specs=spec,
        out_shape=jax.ShapeDtypeStruct((count, width), low),
        compiler_params=params(VMEM_ALONE),
        cost_estimate=SMALL,
    )(place, array, arrived, token)


def butterfly(array, axis, size):
    if size & (size - 1):
        return lax.psum(array, axis)
    step = 1
    while step < size:
        array = array + lax.ppermute(array, axis, [(i, i ^ step) for i in range(size)])
        step *= 2
    return array


class Chain:
    def __init__(self, axis, size, place, token):
        self.axis, self.size, self.place, self.token = axis, size, place, token
        half = size // 2
        self.stages = [("in", [(s - 1, s), (size - s, size - 1 - s)]) for s in range(1, half)]
        self.stages.append(("in", [(half - 1, half), (half, half - 1)]))
        self.stages += [("out", [(s, s - 1), (size - 1 - s, size - s)]) for s in range(half - 1, 0, -1)]
        self.waiting = []
        self.moving = [[] for _ in self.stages]

    def push(self, array, land):
        self.waiting.append((land, array))

    def send(self, stage, land, array):
        arrived = lax.ppermute(array, self.axis, self.stages[stage][1])
        self.moving[stage].append((land, array, arrived))

    def move(self, stage):
        land, array, arrived = self.moving[stage].pop(0)
        kind, pairs = self.stages[stage]
        takers = tuple(target for _, target in pairs) if kind == "out" else ()
        last = stage + 1 == len(self.stages)
        if kind == "in" or not last:
            array = join(self.token, self.place, takers, array, arrived)
            arrived, takers = array, ()
            self.token = array
        if last:
            self.token = land(self.token, self.place, takers, array, arrived)
        else:
            self.send(stage + 1, land, array)

    def tick(self, between=None, turn=0):
        if self.size == 1 or self.size % 2:
            for land, array in self.waiting:
                array = lax.psum(array, self.axis)
                self.token = land(self.token, self.place, (), array, array)
            self.waiting = []
            return between() if between else None
        result = None
        ready = [bool(moving) for moving in self.moving]
        if self.waiting:
            land, array = self.waiting.pop(0)
            array = self.token = hold(array, self.token)
            self.send(0, land, array)
        for stage, can_move in enumerate(ready):
            if can_move:
                self.move(stage)
            if stage == turn and between:
                result = between()
        return result

    def drain(self):
        while self.waiting or any(self.moving):
            self.tick()


def assemble_kernel(place_ref, *refs):
    *pieces, out_ref = refs
    rows = pieces[0].shape[0]
    for number, piece in enumerate(pieces):
        begin = pl.multiple_of((place_ref[1] ^ number) * rows, rows)
        out_ref[pl.ds(begin, rows)] = piece[...]


def assemble(place, pieces):
    count = len(pieces)
    rows, cols = pieces[0].shape
    return pl.pallas_call(
        assemble_kernel,
        name="assemble",
        in_specs=[pl.BlockSpec(memory_space=pltpu.SMEM)]
        + [pl.BlockSpec(memory_space=pltpu.VMEM)] * count,
        out_specs=pl.BlockSpec(memory_space=pltpu.VMEM),
        out_shape=jax.ShapeDtypeStruct((count * rows, cols), pieces[0].dtype),
        compiler_params=params(24),
        cost_estimate=SMALL,
    )(place, *pieces)


def gather_pieces(array, axis, size):
    if size != 8:
        gathered = lax.all_gather(array, axis, axis=0)
        return [gathered[i] for i in range(size)]

    def flip(value, bits):
        return lax.ppermute(value, axis, [(i, i ^ bits) for i in range(size)])

    half = array.shape[0] // 2
    side_a, side_b = flip(array, 2), flip(array, 4)
    far_a, far_b = flip(side_a[:half], 4), flip(side_b[half:], 2)
    mine = [array, side_a, side_b, jnp.concatenate([far_a, far_b], axis=0)]
    pieces = []
    for piece in mine:
        pieces += [piece, flip(piece, 1)]
    return pieces


def per_device(
    tokens,
    cotangent,
    doc_lengths,
    pad_mask,
    w_query,
    w_key,
    w_value,
    w_out,
    w_gate,
    w_up,
    w_down,
    norm_attn,
    norm_mlp,
    mix_gate,
    *,
    n_heads,
    n_batch,
):
    width = tokens.shape[-1]
    rows = tokens.shape[2]
    own_rows = MICRO * rows
    here = lax.axis_index("heads")

    def gather(array):
        return lax.all_gather(array, "heads", axis=0, tiled=True)

    def scatter(array):
        return lax.psum_scatter(array, "heads", scatter_dimension=0, tiled=True)

    def grouped(array):
        return array.reshape(n_heads, MICRO, rows, array.shape[-1])

    def flat(array):
        return array.reshape(n_heads * own_rows, array.shape[-1])

    w_qkv = jnp.concatenate([w_query, w_key, w_value], axis=1)
    share = jax.nn.sigmoid(mix_gate)
    positions = jnp.arange(LEN, dtype=jnp.int32)
    doc_ends = jnp.cumsum(doc_lengths[:, 0], axis=1)
    doc_ids = jnp.sum((positions[None, :, None] >= doc_ends[:, None, :]).astype(jnp.int32), axis=2)
    doc_rows = doc_ids[:, :, None]
    doc_cols = jnp.where(pad_mask[:, 0] == 1, doc_ids, -1)[:, None, :]

    tok_own = tokens.reshape(own_rows, width)
    cot_own = cotangent.reshape(own_rows, width)
    place = jnp.stack(
        [here, here if n_heads == 8 else jnp.zeros_like(here), lax.axis_index("batch")]
    )
    tok_all = gather(tok_own)
    w_out_all = assemble(place, gather_pieces(w_out, "heads", n_heads))
    tok_all, w_out_all = lax.optimization_barrier((tok_all, w_out_all))
    cot_all = gather(lax.optimization_barrier((cot_own, tok_all))[0])
    h1_all, qkv = qkv_rows(tok_all, norm_attn, w_qkv)
    qkv = grouped(qkv)
    mixed = flat(head_forward(share, qkv, doc_rows, doc_cols))
    mixed_pieces = gather_pieces(mixed, "heads", n_heads)
    h2_all, y1_own, mixed_own = mid_rows(place, tok_all, mixed_pieces, w_out_all, norm_mlp)

    chain = Chain("batch", n_batch, place, norm_mlp)
    hidden_cols = w_gate.shape[1]
    cols = hidden_cols // FFN_CHUNKS
    grads = {}

    def push_ffn(number, top, bottom):
        for is_top, part in ((True, top), (False, bottom)):
            chain.push(
                part,
                lambda *moved, is_top=is_top: finish_ffn(
                    is_top, number, cols, hidden_cols, *moved, grads
                ),
            )

    def land_qkv(*moved):
        *grads["qkv"], token = finish_cut(3, *moved)
        return token

    def land_out(*moved):
        grads["out"], token = finish_cut(1, *moved)
        return token

    def first(number):
        *parts, top, bottom = ffn_first(
            number, cols, h2_all, cot_all, w_gate, w_up, w_down, chain.token
        )
        chain.token = parts[0]
        push_ffn(number, top, bottom)
        return parts

    def rest(number):
        results = ffn_rest(number, cols, h2_all, cot_all, w_gate, w_up, w_down, chain.token)
        chain.token = results[0]
        return results

    def weights(number, parts):
        top, bottom = ffn_weights(0, cols, h2_all, cot_all, *parts, chain.token)
        chain.token = bottom
        push_ffn(number, top, bottom)

    def wait_for(microseconds):
        chain.token = tie(chain.token, estimate=busy(microseconds))

    part_a = first(0)
    chain.tick()
    part_b = first(1)
    part_c = rest(2)
    chain.tick()
    part_d = rest(3)
    weights(2, part_c)
    chain.tick()
    hidden, d_gate, d_up = zip(part_a, part_b, part_c, part_d)
    d_h2 = chain.token = ffn_back(w_gate, w_up, d_gate, d_up, chain.token)
    d_h2 = scatter(d_h2)
    chain.tick()
    out_parts = chain.token = ffn_out(own_rows, w_down, hidden, chain.token)
    chain.tick()
    weights(3, part_d)

    def own_part():
        wait_for(WAITS[0])
        results = own_rows_back(
            chain.token, d_h2, y1_own, cot_own, norm_mlp, w_out_all, mixed_own, out_parts
        )
        chain.token = results[0]
        return results

    d_y1, d_mixed_own, parts, gain_mlp_part = chain.tick(own_part, max(len(chain.stages) - 2, 0))
    d_mixed = lax.all_to_all(d_mixed_own, "heads", split_axis=1, concat_axis=0, tiled=True)
    parts = scatter(parts.reshape(-1, width))
    chain.tick()
    wait_for(WAITS[2])
    d_qkv, d_share = head_backward(
        share, qkv, grouped(d_mixed), doc_rows, doc_cols, chain.token
    )
    chain.token = d_share
    chain.tick()
    d_h1, grad_qkv = qkv_back(flat(d_qkv), h1_all, w_qkv, chain.token)
    chain.token = d_h1
    chain.push(grad_qkv, land_qkv)

    def scatter_last():
        wait_for(WAITS[3])
        chain.token = tie(chain.token, parts)
        chain.token = hold(d_h1, chain.token)
        return scatter(chain.token)

    d_h1 = chain.tick(scatter_last)
    chain.push(parts[own_rows:], land_out)
    chain.tick()
    chain.tick()

    wait_for(WAITS[1])
    grad_tokens, gain_attn_part, layer_out = last_rows(
        chain.token, d_h1, tok_own, d_y1, norm_attn, y1_own, parts
    )
    grad_tokens = grad_tokens.reshape(tokens.shape)
    chain.token = gain_attn_part
    slots = jnp.where(jnp.arange(n_heads) == here, jnp.sum(d_share[:, 0, 0]), 0.0)
    sums = jnp.concatenate([gain_attn_part[0], gain_mlp_part[0], slots])
    sums = butterfly(sums, "heads", n_heads)
    if n_batch == 4:
        sums = sums + lax.ppermute(sums, "batch", [(i, i ^ 1) for i in range(4)])
        chain.tick()
        sums = chain.token = hold(sums, chain.token)
        sums = sums + lax.ppermute(sums, "batch", [(i, i ^ 2) for i in range(4)])
    else:
        sums = butterfly(sums, "batch", n_batch)
    grad_mix = lax.dynamic_slice_in_dim(sums, 2 * width + here, 1, 0)
    chain.drain()

    return (
        layer_out.reshape(tokens.shape),
        grad_tokens,
        *grads["qkv"],
        grads["out"],
        grads["gate"].reshape(w_gate.shape),
        grads["up"].reshape(w_up.shape),
        grads["down"],
        sums[:width],
        sums[width : 2 * width],
        grad_mix,
    )


def solution(mesh):
    in_specs = (
        P(None, "batch", "heads", None),
        P(None, "batch", "heads", None),
        P(None, "batch", None),
        P(None, "batch", None),
        P(None, "heads"),
        P(None, "heads"),
        P(None, "heads"),
        P("heads", None),
        P(None, "heads"),
        P(None, "heads"),
        P("heads", None),
        P(),
        P(),
        P("heads"),
    )
    out_specs = (
        P(None, "batch", "heads", None),
        P(None, "batch", "heads", None),
        P(None, "heads"),
        P(None, "heads"),
        P(None, "heads"),
        P("heads", None),
        P(None, "heads"),
        P(None, "heads"),
        P("heads", None),
        P(),
        P(),
        P("heads"),
    )

    def program(*arrays):
        return per_device(*arrays, n_heads=mesh.shape["heads"], n_batch=mesh.shape["batch"])

    return jax.shard_map(
        program, mesh=mesh, in_specs=in_specs, out_specs=out_specs, check_vma=False
    )
```
